32 devices in a mesh: group: 2 (over y), att: 4 (over z), ffn: 4 (over x, core).
Axes of the slice: x: 2, y: 2, z: 4, core: 2. Of those that a mesh axis runs over, the one named last changes fastest.
Arguments:
- hidden_state: bfloat16 [160, 8192], P(('group', 'att'), 'ffn'), parts along dimension 0, may hold values from -40 to 40
- queries: bfloat16 [160, 8192], P(('group', 'att'), 'ffn'), parts along dimension 0, may hold values from -800 to 800
- key_cache: bfloat16 [102400, 1024], P(('group', 'att'), 'ffn'), parts along dimension 0, may hold values from -6 to 6
- value_cache: bfloat16 [102400, 1024], P(('group', 'att'), 'ffn'), parts along dimension 0, may hold values from -6 to 6
- lengths: int32 [160], P(('group', 'att')), parts along dimension 0, may hold values from 1 to 1279, as said below
- assignment: int32 [160], P('group'), parts along dimension 0, may hold values from 0 to 79, each once
- out_weight: bfloat16 [8, 1024, 8192], P(None, 'att', 'ffn'), may hold values from -0.375 to 0.375
- norm_gain: bfloat16 [8192], P('ffn'), may hold values from 0.099609375 to 1.8984375
- gate_weight: bfloat16 [14336, 8192], P('att', 'ffn'), may hold values from -0.0625 to 0.0625
- up_weight: bfloat16 [14336, 8192], P('att', 'ffn'), may hold values from -0.0625 to 0.0625
- down_weight: bfloat16 [14336, 8192], P('att', 'ffn'), may hold values from -0.0625 to 0.0625
Outputs:
- next_hidden: bfloat16 [160, 8192], P(('group', 'att'), 'ffn'), parts along dimension 0
The draws below stay inside these ranges and needn't reach their ends.
There are 2 independent parts, one for each index of `group`. The reference program is written for one: setup_inputs(seed, part) draws one part's arguments, and reference() takes and returns one part's arrays. A program takes and returns all parts, laid end to end along the dimension named above; an argument that names none is the same for every part. Nothing has to cross between parts.
Inputs may be any that keep to these rules, and one draw needn't show every extreme that they name: Each attention index holds the contexts of its 20 slots end to end in its 12800 cache rows in slot order; their lengths sum to at most 12800, and to exactly 12800 on some attention index in every draw. `assignment`: A permutation of the requests.
All inputs are finite; a program needn't handle non-finite values.
Results may differ from the reference program's by a relative error of at most 0.02.
Values may be sent and summed in bfloat16 or wider, within the bound.
No kernel may reach another device: no remote copies, remote signals or barrier semaphores. Data moves between devices by JAX's collectives and lax.ppermute only.
A program may use at most 192 MiB of HBM per device.

```python
import math
import jax
import jax.numpy as jnp
from jax import lax

D = 8192
HQ = 64
KVH = 8
HD = 128
FF = 14336
R_DEV = 20
POOL = 12800
REQS = 80
ROWS = 51200
N_ATT = 4


def draw_lengths(key, part):
    key = jax.random.fold_in(key, 11)
    key_full, key_level, key_pair, key_split, key_order = jax.random.split(key, 5)
    device_count = REQS // R_DEV
    pair_cap = POOL // R_DEV
    pair_count = R_DEV // 2
    full_device = jax.random.randint(key_full, (), 0, device_count)
    device_level = jax.random.randint(key_level, (device_count, 1), max(2, pair_cap // 2), 2 * pair_cap + 1)
    lower_cap = jnp.maximum(2, device_level // 2)
    budget = jax.random.randint(key_pair, (device_count, pair_count), lower_cap, device_level + 1)
    device_rows = jnp.arange(device_count, dtype=jnp.int32)[:, None]
    budget = jnp.where(device_rows == full_device, 2 * pair_cap, budget)
    split_at = jax.random.randint(key_split, (device_count, pair_count), 1, budget)
    lead_pair = jnp.arange(pair_count, dtype=jnp.int32)[None, :] == 0
    split_at = jnp.where((device_rows == full_device) & lead_pair, 1, split_at)
    lengths_grid = jnp.stack([split_at, budget - split_at], axis=-1).reshape(device_count, R_DEV)
    order_keys = jax.random.split(key_order, device_count)
    slot_orders = jax.vmap(lambda order_key: jax.random.permutation(order_key, R_DEV))(order_keys)
    return jnp.take_along_axis(lengths_grid, slot_orders, axis=1).reshape(REQS).astype(jnp.int32)


def draw_hidden_state(key, part):
    key = jax.random.fold_in(key, 21)
    key_entries, key_rows, key_cols = jax.random.split(key, 3)
    column_axis = jnp.arange(D, dtype=jnp.float32) / D
    rough_cols = jnp.exp(jax.random.uniform(key_cols, (D,), minval=math.log(0.7), maxval=math.log(1.4)))
    column_scale = 10.0 ** (column_axis - 0.5) * rough_cols
    entries = jnp.clip(jax.random.normal(key_entries, (REQS, D)), -6.0, 6.0)
    row_scale = jnp.exp(jax.random.uniform(key_rows, (REQS, 1), minval=math.log(0.4), maxval=math.log(4.0)))
    return (0.3 * entries * row_scale * column_scale).astype(jnp.bfloat16)


def draw_queries(key, part):
    key = jax.random.fold_in(key, 31)
    key_entries = jax.random.fold_in(key, 0)
    entries = jnp.clip(jax.random.normal(key_entries, (REQS, HQ, HD)), -6.0, 6.0)
    return entries.reshape(REQS, HQ * HD).astype(jnp.bfloat16)


def draw_key_cache(key, part):
    key = jax.random.fold_in(key, 41)
    key_entries = jax.random.fold_in(key, 0)
    cache_rows = POOL * (REQS // R_DEV)
    entries = jnp.clip(jax.random.normal(key_entries, (cache_rows, KVH, HD)), -6.0, 6.0)
    return entries.reshape(cache_rows, KVH * HD).astype(jnp.bfloat16)


def raised(values, rng, source, target, blocks, factor):
    owner, partner = [(jnp.arange(values.shape[dim]) // (values.shape[dim] // blocks)).reshape([-1 if axis == dim else 1 for axis in range(values.ndim)]) for dim in (source, target)]
    chosen = jax.random.permutation(rng, blocks)[partner]
    strong = (owner == chosen) | (owner == (partner + blocks // 2) % blocks)
    return jnp.where(strong, factor * values, values)


def block_scale(rng, dims, shards, least, largest):
    gain = 1.0
    for axis_at, parts in shards:
        steps = jax.random.uniform(jax.random.fold_in(jax.random.fold_in(rng, 6), axis_at), (parts,), jnp.float32, least / len(shards), largest / len(shards))
        gain = gain * jnp.repeat(jnp.exp(steps), dims[axis_at] // parts).reshape((-1,) + (1,) * (len(dims) - 1 - axis_at))
    return gain


def normal_values(key, dims, width, most, cuts=(), kind=jnp.bfloat16):
    result = jax.random.normal(key, dims, jnp.float32) * width
    if len(cuts) > 0:
        result = block_scale(key, dims, cuts, -0.22, 0.18) * result
    return jnp.clip(result, min=-most, max=most).astype(kind)


def noise_with(key, extent, spread, limit, cuts, heavy, kind=jnp.bfloat16):
    array = spread * jax.random.normal(key, extent, jnp.float32)
    if cuts:
        array = array * block_scale(key, extent, cuts, -0.22, 0.18)
    return jnp.clip(raised(array, jax.random.fold_in(key, 3), *heavy), -limit, limit).astype(kind)


def setup_inputs(seed: int = 0, part: int = 0) -> dict:
    key_of = jax.random.split(jax.random.key(seed), 12)
    own_keys = jax.random.split(jax.random.fold_in(key_of[11], part), 12)
    hidden_state = draw_hidden_state(jax.random.fold_in(jax.random.fold_in(key_of[11], part), 71), part)
    queries = draw_queries(jax.random.fold_in(jax.random.fold_in(key_of[11], part), 71), part)
    key_cache = draw_key_cache(jax.random.fold_in(jax.random.fold_in(key_of[11], part), 71), part)
    value_cache = normal_values(own_keys[3], (ROWS, KVH * HD), 1.0, 6.0, ((0, 4), (1, 4)))
    lengths = draw_lengths(jax.random.fold_in(jax.random.fold_in(key_of[11], part), 71), part)
    assignment = jax.random.permutation(own_keys[5], REQS).astype(jnp.int32)
    out_weight = normal_values(key_of[6], (KVH, HQ // KVH * HD, D), (2 * HD) ** -0.5, 0.375, ((1, 4), (2, 4)))
    norm_gain = jnp.clip(1.0 + 0.18 * jax.random.normal(key_of[7], (D,), jnp.float32), 0.099609375, 1.8984375).astype(jnp.bfloat16)
    gate_weight = normal_values(key_of[8], (FF, D), D ** -0.5, 0.0625, ((0, 4), (1, 4)))
    up_weight = normal_values(key_of[9], (FF, D), D ** -0.5, 0.0625, ((0, 4), (1, 4)))
    down_weight = noise_with(key_of[10], (FF, D), FF ** -0.5, 0.0625, ((0, 4), (1, 4)), (0, 1, 4, 2.0))
    return dict(hidden_state=hidden_state, queries=queries, key_cache=key_cache, value_cache=value_cache, lengths=lengths, assignment=assignment, out_weight=out_weight, norm_gain=norm_gain, gate_weight=gate_weight, up_weight=up_weight, down_weight=down_weight)


epsilon = 1e-05
masked_score = -1e+30

def attend_device(inputs):
    dev_queries, dev_keys, dev_values, dev_lengths = inputs
    slot_starts = jnp.cumsum(dev_lengths) - dev_lengths
    slot_ends = slot_starts + dev_lengths
    positions = jnp.arange(POOL, dtype=jnp.int32)
    owned_rows = (positions[None, :] >= slot_starts[:, None]) & (positions[None, :] < slot_ends[:, None])
    scores = jnp.einsum('rkgc,pkc->rkgp', dev_queries.astype(jnp.float32), dev_keys.astype(jnp.float32))
    scores = scores * (1.0 / jnp.sqrt(jnp.float32(HD)))
    scores = jnp.where(owned_rows[:, None, None, :], scores, masked_score)
    row_top = lax.optimization_barrier(jnp.max(scores, axis=-1, keepdims=True))
    shifted = jnp.exp(scores - row_top)
    totals = lax.optimization_barrier(jnp.sum(shifted, axis=-1, keepdims=True))
    weights = (shifted / totals).astype(jnp.bfloat16)
    attended = jnp.einsum('rkgp,pkc->rkgc', weights.astype(jnp.float32), dev_values.astype(jnp.float32))
    return attended.astype(jnp.bfloat16)

def reference(hidden_state, queries, key_cache, value_cache, lengths, assignment, out_weight, norm_gain, gate_weight, up_weight, down_weight):
    per_group = HQ // KVH
    slot_queries = jnp.take(queries, assignment, axis=0).reshape(N_ATT, R_DEV, KVH, per_group, HD)
    keys_grid = key_cache.reshape(N_ATT, POOL, KVH, HD)
    values_grid = value_cache.reshape(N_ATT, POOL, KVH, HD)
    lengths_grid = lengths.reshape(N_ATT, R_DEV)
    attended = lax.map(attend_device, (slot_queries, keys_grid, values_grid, lengths_grid))
    attended = attended.reshape(REQS, HQ * HD)
    inverse = jnp.zeros((REQS,), jnp.int32).at[assignment].set(jnp.arange(REQS, dtype=jnp.int32))
    request_heads = jnp.take(attended, inverse, axis=0)
    projected = jnp.dot(request_heads, out_weight.reshape(HQ * HD, D), preferred_element_type=jnp.float32)
    middle_short = (hidden_state.astype(jnp.float32) + projected).astype(jnp.bfloat16)
    middle = lax.optimization_barrier(middle_short).astype(jnp.float32)
    squares = lax.optimization_barrier(jnp.sum(middle * middle, axis=1, keepdims=True))
    normed = (middle * lax.rsqrt(squares / D + epsilon) * norm_gain.astype(jnp.float32)).astype(jnp.bfloat16)
    contract = (((1,), (1,)), ((), ()))
    gate_values = lax.dot_general(normed, gate_weight, contract, preferred_element_type=jnp.float32)
    upward = lax.dot_general(normed, up_weight, contract, preferred_element_type=jnp.float32)
    active = (jax.nn.silu(gate_values) * upward).astype(jnp.bfloat16)
    down_values = jnp.dot(active, down_weight, preferred_element_type=jnp.float32)
    return (middle + down_values).astype(jnp.bfloat16)
```

```python
import functools
import math

import jax
import jax.numpy as jnp
from jax import lax
from jax.experimental import pallas as pl
from jax.experimental.pallas import tpu as pltpu
from jax.sharding import PartitionSpec as P

epsilon = 1e-05
masked_score = -1e30
lanes = 128
sublanes = 16
max_context = 1279
contract_minor = (((1,), (1,)), ((), ()))
F32 = jnp.float32
BF16 = jnp.bfloat16
vmem = pl.BlockSpec(memory_space=pltpu.VMEM)
smem = pl.BlockSpec(memory_space=pltpu.SMEM)
anywhere = pl.BlockSpec(memory_space=pl.ANY)


def softmax_rounded(scores):
    row_top = jnp.max(scores, axis=-1, keepdims=True)
    shifted = jnp.exp(scores - row_top)
    totals = jnp.sum(shifted, axis=-1, keepdims=True)
    return (shifted / totals).astype(jnp.bfloat16)


def general_device(
    hidden_state,
    queries,
    key_cache,
    value_cache,
    lengths,
    assignment,
    out_weight,
    norm_gain,
    gate_weight,
    up_weight,
    down_weight,
):
    rows_dev = hidden_state.shape[0]
    columns = hidden_state.shape[1]
    att_count = lax.axis_size("att")
    ffn_count = lax.axis_size("ffn")
    requests = rows_dev * att_count
    kv_total = out_weight.shape[0]
    kv_local = kv_total // ffn_count
    model_width = columns * ffn_count
    pool_rows = key_cache.shape[0]
    head_size = key_cache.shape[1] // kv_local
    per_group = queries.shape[1] // (kv_local * head_size)
    score_scale = 1.0 / math.sqrt(head_size)
    att_place = lax.axis_index("att")
    every_query = lax.all_gather(queries, "att", axis=0, tiled=True)
    own_slots = lax.dynamic_slice_in_dim(assignment, att_place * rows_dev, rows_dev)
    slot_queries = jnp.take(every_query, own_slots, axis=0).reshape(
        rows_dev, kv_local, per_group, head_size
    )
    keys_local = key_cache.reshape(pool_rows, kv_local, head_size)
    values_local = value_cache.reshape(pool_rows, kv_local, head_size)
    slot_starts = jnp.cumsum(lengths) - lengths
    slot_ends = slot_starts + lengths
    positions = jnp.arange(pool_rows, dtype=jnp.int32)
    owned_rows = (positions[None, :] >= slot_starts[:, None]) & (
        positions[None, :] < slot_ends[:, None]
    )
    owned_rows = owned_rows[:, None, None, :]
    raw_scores = (
        jnp.einsum("rkgc,pkc->rkgp", slot_queries, keys_local, preferred_element_type=jnp.float32)
        * score_scale
    )
    weights = softmax_rounded(jnp.where(owned_rows, raw_scores, masked_score))
    attended = jnp.einsum(
        "rkgp,pkc->rkgc", weights, values_local, preferred_element_type=jnp.float32
    )
    attended = attended.astype(jnp.bfloat16).reshape(rows_dev, kv_local, per_group * head_size)
    spread = lax.all_to_all(attended, "att", split_axis=2, concat_axis=0, tiled=True)
    pieces = lax.all_gather(spread, "ffn", axis=1, tiled=True)
    inverse = (
        jnp.zeros((requests,), jnp.int32).at[assignment].set(jnp.arange(requests, dtype=jnp.int32))
    )
    request_pieces = jnp.take(pieces, inverse, axis=0)
    block = request_pieces
    projected = lax.psum_scatter(
        jnp.einsum("rkc,kcd->rd", block, out_weight, preferred_element_type=jnp.float32).astype(
            jnp.bfloat16
        ),
        "att",
        scatter_dimension=0,
        tiled=True,
    ).astype(jnp.float32)
    middle_short = (hidden_state.astype(jnp.float32) + projected).astype(jnp.bfloat16)
    middle = lax.optimization_barrier(middle_short).astype(jnp.float32)
    squares = lax.psum(jnp.sum(middle * middle, axis=1), "ffn")
    normed = (
        middle * lax.rsqrt(squares[:, None] / model_width + epsilon) * norm_gain.astype(jnp.float32)
    ).astype(jnp.bfloat16)
    every_row = lax.all_gather(normed, "att", axis=0, tiled=True)
    contract = (((1,), (1,)), ((), ()))
    gate_part = lax.dot_general(
        gate_weight, every_row, contract, preferred_element_type=jnp.float32
    )
    up_part = lax.dot_general(up_weight, every_row, contract, preferred_element_type=jnp.float32)
    totals = lax.psum(
        jnp.concatenate([gate_part, up_part], axis=1).astype(jnp.bfloat16), "ffn"
    ).astype(jnp.float32)
    unit_active = (jax.nn.silu(totals[:, :requests]) * totals[:, requests:]).astype(jnp.bfloat16)
    block = unit_active
    returned = lax.psum_scatter(
        lax.dot_general(
            block, down_weight, (((0,), (0,)), ((), ())), preferred_element_type=jnp.float32
        ).astype(jnp.bfloat16),
        "att",
        scatter_dimension=0,
        tiled=True,
    ).astype(jnp.float32)
    return (middle + returned).astype(jnp.bfloat16)


def pair_swap(value, axis, bit):
    count = lax.axis_size(axis)
    return lax.ppermute(value, axis, [(i, i ^ bit) for i in range(count)])


def up_to(value, multiple):
    return -(-value // multiple) * multiple


def attention_kernel(place, assignment, lengths, *refs, slots, count, chunk, scale, unroll):
    query_blocks, (keys, values), outs = refs[:count], refs[count : count + 2], refs[count + 2 : -2]
    queries, attended = refs[-2:]
    pool = keys.shape[0]
    heads = queries.shape[1]
    half = heads // 2
    own = place[0]
    for k in range(count):
        queries[k * slots : (k + 1) * slots] = query_blocks[k][...]
    top_half = lax.broadcasted_iota(jnp.int32, (heads, lanes), 0) < half

    def slot(s, start):
        length = lengths[s]
        request = assignment[own * slots + s]
        owner = sum((request >= k * slots).astype(jnp.int32) for k in range(1, count))
        query = queries[(owner ^ own) * slots + request - owner * slots]
        first = pl.multiple_of(
            jnp.minimum((start // sublanes) * sublanes, pool - chunk), sublanes
        )
        zero = jnp.zeros_like(query)
        both = jnp.concatenate(
            [jnp.where(top_half, query, zero), jnp.where(top_half, zero, query)], axis=1
        )
        scores = (
            lax.dot_general(
                both, keys[pl.ds(first, chunk), :], contract_minor, preferred_element_type=F32
            )
            * scale
        )
        rows = first + lax.broadcasted_iota(jnp.int32, (heads, chunk), 1)
        scores = jnp.where((rows >= start) & (rows < start + length), scores, masked_score)
        top = jnp.max(scores, axis=-1, keepdims=True)
        shifted = jnp.exp(scores - top)
        total = jnp.sum(shifted, axis=-1, keepdims=True)
        weights = (shifted / total).astype(BF16)
        out = jnp.dot(weights, values[pl.ds(first, chunk), :], preferred_element_type=F32)
        attended[pl.ds(pl.multiple_of(s * heads, heads), heads), :] = jnp.where(
            top_half, out[:, :lanes], out[:, lanes:]
        )
        return start + length

    def body(step, start):
        for u in range(unroll):
            start = slot(step * unroll + u, start)
        return start

    lax.fori_loop(0, slots // unroll, body, jnp.int32(0))
    per_block = half // count
    for k in range(count):
        outs[k][...] = jnp.zeros(outs[k].shape, BF16)
        for kv in range(2):
            for j in range(per_block):
                head = kv * half + (own ^ k) * per_block + j
                at = (kv * per_block + j) * lanes
                outs[k][:slots, at : at + lanes] = attended[
                    pl.ds(head, slots, stride=heads), :
                ].astype(BF16)


def attention(place, assignment, lengths, query_blocks, keys, values):
    count = len(query_blocks)
    slots, heads, _ = query_blocks[0].shape
    pool = keys.shape[0]
    chunk = min(up_to(max_context + sublanes - 1, lanes), pool)
    unroll = 4 if slots % 4 == 0 else 1
    width = heads // count * lanes
    return pl.pallas_call(
        functools.partial(
            attention_kernel,
            slots=slots,
            count=count,
            chunk=chunk,
            scale=1.0 / math.sqrt(lanes),
            unroll=unroll,
        ),
        in_specs=[smem] * 3 + [vmem] * (count + 2),
        out_specs=[vmem] * count,
        out_shape=[jax.ShapeDtypeStruct((up_to(slots, 8), width), BF16)] * count,
        scratch_shapes=[
            pltpu.VMEM((count * slots, heads, lanes), BF16),
            pltpu.VMEM((slots * heads, lanes), F32),
        ],
        compiler_params=pltpu.CompilerParams(vmem_limit_bytes=20 << 20),
        cost_estimate=pl.CostEstimate(
            flops=4 * pool * heads * lanes * 2, bytes_accessed=pool * lanes * 8, transcendentals=0
        ),
        name="attention",
    )(place, assignment, lengths, *query_blocks, keys, values)


def projection_kernel(place, choose, *refs, count, parts):
    pieces, weight, outs = refs[:parts], refs[parts], refs[parts + 1 : -2]
    buffer, sems = refs[-2:]
    own = place[1]
    depth = buffer.shape[1]
    copies = [
        pltpu.make_async_copy(
            weight.at[pl.ds(pl.multiple_of((own ^ k) * depth, depth), depth)],
            buffer.at[k],
            sems.at[k],
        )
        for k in range(parts)
    ]
    for copy in copies:
        copy.start()
    total = None
    for k in range(parts):
        rows = jnp.dot(choose[...], pieces[k][...], preferred_element_type=F32).astype(BF16)
        copies[k].wait()
        term = jnp.dot(rows, buffer[k], preferred_element_type=F32)
        total = term if k == 0 else total + term
    rows = total.shape[0] // count
    for k in range(count):
        outs[k][...] = total[k * rows : (k + 1) * rows].astype(BF16)


def projection(place, choose, pieces, weight, count):
    parts = len(pieces)
    requests = choose.shape[0]
    depth, width = weight.shape
    return pl.pallas_call(
        functools.partial(projection_kernel, count=count, parts=parts),
        in_specs=[smem] + [vmem] * (1 + parts) + [anywhere],
        out_specs=[vmem] * count,
        out_shape=[jax.ShapeDtypeStruct((requests // count, width), BF16)] * count,
        scratch_shapes=[
            pltpu.VMEM((parts, depth // parts, width), BF16),
            pltpu.SemaphoreType.DMA((parts,)),
        ],
        compiler_params=pltpu.CompilerParams(vmem_limit_bytes=24 << 20),
        cost_estimate=pl.CostEstimate(
            flops=2 * requests * depth * width, bytes_accessed=2 * depth * width, transcendentals=0
        ),
        name="projection",
    )(place, choose, *pieces, weight)


def hidden_kernel(place, *refs, count, masks, square):
    blocks, (gain, gate, up), rest = refs[:count], refs[count : count + 3], refs[count + 3 :]
    send, keep = rest[:2]
    if square:
        squares = rest[2]
    joined, buffer, sems = rest[-3:]
    own = place[1]
    units = buffer.shape[2]
    copies = {}
    for m in range(2):
        for t, weight in enumerate((gate, up)):
            copies[m, t] = pltpu.make_async_copy(
                weight.at[pl.ds(pl.multiple_of((own ^ masks[m]) * units, units), units)],
                buffer.at[m, t],
                sems.at[m, t],
            )
            copies[m, t].start()
    rows = blocks[0].shape[0]
    for k in range(count):
        joined[k * rows : (k + 1) * rows, :] = blocks[k][...].astype(F32)
    middle = joined[...]
    if square:
        squares[...] = jnp.broadcast_to(
            jnp.sum(middle * middle, axis=1, keepdims=True), squares.shape
        )
    scaled = (middle * gain[...].astype(F32)).astype(BF16)
    for m in range(2):
        for t in range(2):
            copies[m, t].wait()
            out = lax.dot_general(
                scaled, buffer[m, t], contract_minor, preferred_element_type=F32
            )
            target = send if m == 0 else keep
            target[:, t * units : (t + 1) * units] = out.astype(target.dtype)


def hidden_part(place, blocks, gain, gate, up, owners, masks, square):
    count = len(blocks)
    rows, width = blocks[0].shape
    requests = rows * count
    units = gate.shape[0] // owners
    outs = [
        jax.ShapeDtypeStruct((requests, 2 * units), BF16),
        jax.ShapeDtypeStruct((requests, 2 * units), F32),
    ]
    if square:
        outs.append(jax.ShapeDtypeStruct((requests, lanes), F32))
    return pl.pallas_call(
        functools.partial(hidden_kernel, count=count, masks=masks, square=square),
        in_specs=[smem] + [vmem] * (count + 1) + [anywhere] * 2,
        out_specs=[vmem] * len(outs),
        out_shape=outs,
        scratch_shapes=[
            pltpu.VMEM((requests, width), F32),
            pltpu.VMEM((2, 2, units, width), BF16),
            pltpu.SemaphoreType.DMA((2, 2)),
        ],
        compiler_params=pltpu.CompilerParams(vmem_limit_bytes=32 << 20),
        cost_estimate=pl.CostEstimate(
            flops=8 * requests * units * width,
            bytes_accessed=8 * units * width,
            transcendentals=0,
        ),
        name="hidden_units",
    )(place, *blocks, gain, gate, up)


def down_kernel(place, *refs, masks, count, first):
    pieces, weight = refs[:2], refs[2]
    rest = refs[3:]
    if not first:
        before, rest = rest[0], rest[1:]
    outs, (buffer, sems) = rest[:-2], rest[-2:]
    own = place[1]
    units = buffer.shape[1]
    copies = [
        pltpu.make_async_copy(
            weight.at[pl.ds(pl.multiple_of((own ^ masks[m]) * units, units), units)],
            buffer.at[m],
            sems.at[m],
        )
        for m in range(2)
    ]
    for copy in copies:
        copy.start()
    total = None if first else before[...]
    for m in range(2):
        copies[m].wait()
        term = jnp.dot(pieces[m][...], buffer[m], preferred_element_type=F32)
        total = term if total is None else total + term
    if first:
        outs[0][...] = total
    else:
        rows = total.shape[0] // count
        for k in range(count):
            outs[k][...] = total[k * rows : (k + 1) * rows].astype(BF16)


def down_part(place, pieces, weight, masks, count, before=None):
    first = before is None
    requests, units = pieces[0].shape
    width = weight.shape[1]
    if first:
        outs = [jax.ShapeDtypeStruct((requests, width), F32)]
    else:
        outs = [jax.ShapeDtypeStruct((requests // count, width), BF16)] * count
    return pl.pallas_call(
        functools.partial(down_kernel, masks=masks, count=count, first=first),
        in_specs=[smem] + [vmem] * 2 + [anywhere] + [vmem] * (0 if first else 1),
        out_specs=[vmem] * len(outs),
        out_shape=outs,
        scratch_shapes=[
            pltpu.VMEM((2, units, width), BF16),
            pltpu.SemaphoreType.DMA((2,)),
        ],
        compiler_params=pltpu.CompilerParams(vmem_limit_bytes=24 << 20),
        cost_estimate=pl.CostEstimate(
            flops=4 * requests * units * width, bytes_accessed=4 * units * width, transcendentals=0
        ),
        name="down",
    )(place, *pieces, weight, *([] if first else [before]))


def exchanged_sum(blocks, axis):
    total = blocks[0].astype(F32)
    arrived = [pair_swap(blocks[k], axis, k) for k in range(1, len(blocks))]
    for block in arrived:
        total = total + block.astype(F32)
    return total


def per_device(
    hidden_state,
    queries,
    key_cache,
    value_cache,
    lengths,
    assignment,
    out_weight,
    norm_gain,
    gate_weight,
    up_weight,
    down_weight,
):
    rows_dev, columns = hidden_state.shape
    count = lax.axis_size("att")
    parts = lax.axis_size("ffn")
    requests = rows_dev * count
    model_width = columns * parts
    heads = queries.shape[1] // lanes
    place = jnp.stack([lax.axis_index("att"), lax.axis_index("ffn")]).astype(jnp.int32)
    swaps = range(1, count)

    own_queries = queries.reshape(rows_dev, heads, lanes)
    query_blocks = [own_queries] + [pair_swap(own_queries, "att", k) for k in swaps]
    blocks = attention(place, assignment, lengths, query_blocks, key_cache, value_cache)

    padded = blocks[0].shape[0]
    order = place[0] ^ jnp.arange(count, dtype=jnp.int32)
    served = jnp.pad(
        assignment.reshape(count, rows_dev)[order],
        ((0, 0), (0, padded - rows_dev)),
        constant_values=-1,
    ).reshape(1, -1)
    wanted = (order[:, None] * rows_dev + jnp.arange(rows_dev, dtype=jnp.int32)[None]).reshape(-1, 1)
    choose = (wanted == served).astype(BF16)

    blocks = [blocks[0]] + [pair_swap(blocks[k], "att", k) for k in swaps]
    piece = jnp.concatenate(blocks, axis=0)
    across = pair_swap(piece, "ffn", 2)
    beside = pair_swap(piece, "ffn", 1)
    corner = pair_swap(across, "ffn", 1)
    weight = out_weight.reshape(-1, columns)
    partial = projection(place, choose, [piece, beside, across, corner], weight, count)
    middle = (exchanged_sum(partial, "att") + hidden_state.astype(F32)).astype(BF16)
    middle = lax.optimization_barrier(middle)

    rows = [middle] + [pair_swap(middle, "att", k) for k in swaps]
    gain = norm_gain.reshape(1, columns)
    hidden = functools.partial(hidden_part, place, rows, gain, gate_weight, up_weight, parts)
    far_send, far_keep, squares = hidden((3, 2), True)
    far = (pair_swap(far_send, "ffn", 1).astype(F32) + far_keep).astype(BF16)
    far = pair_swap(far, "ffn", 2)
    squares = squares + pair_swap(squares, "ffn", 1)
    squares = squares + pair_swap(squares, "ffn", 2)
    near_send, near_keep = hidden((1, 0), False)
    totals = near_keep + pair_swap(near_send, "ffn", 1).astype(F32) + far.astype(F32)
    totals = totals * lax.rsqrt(squares[:, :1] / model_width + epsilon)
    units = totals.shape[1] // 2
    active = (jax.nn.silu(totals[:, :units]) * totals[:, units:]).astype(BF16)

    across = pair_swap(active, "ffn", 2)
    beside = pair_swap(active, "ffn", 1)
    corner = pair_swap(across, "ffn", 1)
    (before,) = down_part(place, [active, beside], down_weight, (0, 1), count)
    partial = down_part(place, [across, corner], down_weight, (2, 3), count, before)
    return (exchanged_sum(partial, "att") + middle.astype(F32)).astype(BF16)


def exchanges_fit(mesh, per_group):
    count, parts = mesh.shape["att"], mesh.shape["ffn"]
    return parts == 4 and count & (count - 1) == 0 and per_group % count == 0


def solution(mesh):
    in_specs = (
        P(("group", "att"), "ffn"),
        P(("group", "att"), "ffn"),
        P(("group", "att"), "ffn"),
        P(("group", "att"), "ffn"),
        P(("group", "att")),
        P("group"),
        P(None, "att", "ffn"),
        P("ffn"),
        P("att", "ffn"),
        P("att", "ffn"),
        P("att", "ffn"),
    )
    out_specs = P(("group", "att"), "ffn")

    def step(*args):
        queries, keys, out_weight = args[1], args[2], args[6]
        kv_heads, group_width, _ = out_weight.shape
        fits = (
            exchanges_fit(mesh, group_width // lanes)
            and keys.shape[1] == kv_heads * lanes
            and kv_heads == 2 * mesh.shape["ffn"]
            and queries.shape[1] == kv_heads * group_width
        )
        return jax.shard_map(
            per_device if fits else general_device,
            mesh=mesh,
            in_specs=in_specs,
            out_specs=out_specs,
            check_vma=False,
        )(*args)

    return step
```

```python
import functools
import math

import jax
import jax.numpy as jnp
from jax import lax
from jax.experimental import pallas as pl
from jax.experimental.pallas import tpu as pltpu
from jax.sharding import PartitionSpec as P

epsilon = 1e-05
masked_score = -1e30
lanes = 128
block_rows = 256
slot_group = 2
contract_minor = (((1,), (1,)), ((), ()))
F32 = jnp.float32
BF16 = jnp.bfloat16
I32 = jnp.int32
vmem = pl.BlockSpec(memory_space=pltpu.VMEM)
smem = pl.BlockSpec(memory_space=pltpu.SMEM)
hbm = pl.BlockSpec(memory_space=pltpu.HBM)


def softmax_rounded(scores):
    row_top = jnp.max(scores, axis=-1, keepdims=True)
    shifted = jnp.exp(scores - row_top)
    totals = jnp.sum(shifted, axis=-1, keepdims=True)
    return (shifted / totals).astype(jnp.bfloat16)


def general_device(
    hidden_state,
    queries,
    key_cache,
    value_cache,
    lengths,
    assignment,
    out_weight,
    norm_gain,
    gate_weight,
    up_weight,
    down_weight,
):
    rows_dev = hidden_state.shape[0]
    columns = hidden_state.shape[1]
    att_count = lax.axis_size("att")
    ffn_count = lax.axis_size("ffn")
    requests = rows_dev * att_count
    kv_total = out_weight.shape[0]
    kv_local = kv_total // ffn_count
    model_width = columns * ffn_count
    pool_rows = key_cache.shape[0]
    head_size = key_cache.shape[1] // kv_local
    per_group = queries.shape[1] // (kv_local * head_size)
    score_scale = 1.0 / math.sqrt(head_size)
    att_place = lax.axis_index("att")
    every_query = lax.all_gather(queries, "att", axis=0, tiled=True)
    own_slots = lax.dynamic_slice_in_dim(assignment, att_place * rows_dev, rows_dev)
    slot_queries = jnp.take(every_query, own_slots, axis=0).reshape(
        rows_dev, kv_local, per_group, head_size
    )
    keys_local = key_cache.reshape(pool_rows, kv_local, head_size)
    values_local = value_cache.reshape(pool_rows, kv_local, head_size)
    slot_starts = jnp.cumsum(lengths) - lengths
    slot_ends = slot_starts + lengths
    positions = jnp.arange(pool_rows, dtype=jnp.int32)
    owned_rows = (positions[None, :] >= slot_starts[:, None]) & (
        positions[None, :] < slot_ends[:, None]
    )
    owned_rows = owned_rows[:, None, None, :]
    raw_scores = (
        jnp.einsum("rkgc,pkc->rkgp", slot_queries, keys_local, preferred_element_type=jnp.float32)
        * score_scale
    )
    weights = softmax_rounded(jnp.where(owned_rows, raw_scores, masked_score))
    attended = jnp.einsum(
        "rkgp,pkc->rkgc", weights, values_local, preferred_element_type=jnp.float32
    )
    attended = attended.astype(jnp.bfloat16).reshape(rows_dev, kv_local, per_group * head_size)
    spread = lax.all_to_all(attended, "att", split_axis=2, concat_axis=0, tiled=True)
    pieces = lax.all_gather(spread, "ffn", axis=1, tiled=True)
    inverse = (
        jnp.zeros((requests,), jnp.int32).at[assignment].set(jnp.arange(requests, dtype=jnp.int32))
    )
    request_pieces = jnp.take(pieces, inverse, axis=0)
    block = request_pieces
    projected = lax.psum_scatter(
        jnp.einsum("rkc,kcd->rd", block, out_weight, preferred_element_type=jnp.float32).astype(
            jnp.bfloat16
        ),
        "att",
        scatter_dimension=0,
        tiled=True,
    ).astype(jnp.float32)
    middle_short = (hidden_state.astype(jnp.float32) + projected).astype(jnp.bfloat16)
    middle = lax.optimization_barrier(middle_short).astype(jnp.float32)
    squares = lax.psum(jnp.sum(middle * middle, axis=1), "ffn")
    normed = (
        middle * lax.rsqrt(squares[:, None] / model_width + epsilon) * norm_gain.astype(jnp.float32)
    ).astype(jnp.bfloat16)
    every_row = lax.all_gather(normed, "att", axis=0, tiled=True)
    contract = (((1,), (1,)), ((), ()))
    gate_part = lax.dot_general(
        gate_weight, every_row, contract, preferred_element_type=jnp.float32
    )
    up_part = lax.dot_general(up_weight, every_row, contract, preferred_element_type=jnp.float32)
    totals = lax.psum(
        jnp.concatenate([gate_part, up_part], axis=1).astype(jnp.bfloat16), "ffn"
    ).astype(jnp.float32)
    unit_active = (jax.nn.silu(totals[:, :requests]) * totals[:, requests:]).astype(jnp.bfloat16)
    block = unit_active
    returned = lax.psum_scatter(
        lax.dot_general(
            block, down_weight, (((0,), (0,)), ((), ())), preferred_element_type=jnp.float32
        ).astype(jnp.bfloat16),
        "att",
        scatter_dimension=0,
        tiled=True,
    ).astype(jnp.float32)
    return (middle + returned).astype(jnp.bfloat16)


def pair_swap(value, axis, bit):
    count = lax.axis_size(axis)
    return lax.ppermute(value, axis, [(i, i ^ bit) for i in range(count)])


def up_to(value, multiple):
    return -(-value // multiple) * multiple


def params(megabytes):
    return pltpu.CompilerParams(vmem_limit_bytes=megabytes << 20)


def halves_joined(block):
    block = block.astype(F32)
    rows = block.shape[0] // 2
    return jnp.concatenate([block[:rows], block[rows:]], axis=1)


def halves_stacked(block):
    half = block.shape[1] // 2
    return jnp.concatenate([block[:, :half], block[:, half:]], axis=0)


def high_low(value):
    high = value.astype(BF16).astype(F32)
    low = value - high
    lane = lax.broadcasted_iota(I32, (value.shape[0], lanes), 1)
    return jnp.where(lane < lanes // 2, high, low)


def in_hbm(value):
    return pltpu.with_memory_space_constraint(value, pltpu.HBM)


def in_vmem(value):
    return pltpu.with_memory_space_constraint(value, pltpu.VMEM)


def fetch_kernel(*refs):
    count = len(refs) // 2
    sems = refs[-1]
    copies = [
        pltpu.make_async_copy(refs[i], refs[count + i], sems.at[i]) for i in range(count)
    ]
    for copy in copies:
        copy.start()
    for copy in copies:
        copy.wait()


def fetch(arrays):
    moved = sum(a.size * 2 for a in arrays)
    return pl.pallas_call(
        fetch_kernel,
        in_specs=[hbm] * len(arrays),
        out_specs=[vmem] * len(arrays),
        out_shape=[pltpu.VMEM(a.shape, a.dtype) for a in arrays],
        scratch_shapes=[pltpu.SemaphoreType.DMA((len(arrays),))],
        compiler_params=params(1),
        cost_estimate=pl.CostEstimate(flops=0, bytes_accessed=2 * moved, transcendentals=0),
        name="fetch",
    )(*[in_hbm(a) for a in arrays])


def folded(combine, value):
    parts = [value[:, i : i + lanes] for i in range(0, value.shape[1], lanes)]
    return functools.reduce(combine, parts)


def attention_kernel(table, *refs, slots, count, scale, unroll):
    query_blocks, (keys, values, ahead) = refs[:count], refs[count : count + 3]
    outs, landed = refs[count + 3 : 2 * count + 3], refs[2 * count + 3]
    queries, both, begins, ends, tops, sums, scores, total, attended, items, sem = refs[
        2 * count + 4 :
    ]
    copy = pltpu.make_async_copy(ahead, landed, sem)
    copy.start()
    pool, width = keys.shape
    heads = queries.shape[1]
    half = heads // 2
    own = table[0]
    group_rows = slot_group * heads
    top_half = lax.broadcasted_iota(I32, (heads, lanes), 0) < half
    for k in range(count):
        queries[k * slots : (k + 1) * slots] = query_blocks[k][...]

    tops[...] = jnp.full(tops.shape, masked_score, F32)
    sums[...] = jnp.zeros(sums.shape, F32)
    total[...] = jnp.zeros(total.shape, F32)
    spare = slots * heads
    both[spare:, :] = jnp.zeros((both.shape[0] - spare, width), BF16)
    begins[spare:, :] = jnp.full((begins.shape[0] - spare, lanes), pool, I32)
    ends[spare:, :] = jnp.zeros((ends.shape[0] - spare, lanes), I32)

    def slot(s, carry):
        start, made, last_block, last_slot = carry
        end = start + table[2 + s]
        request = table[2 + slots + own * slots + s]
        owner = sum((request >= k * slots).astype(I32) for k in range(1, count))
        query = queries[(owner ^ own) * slots + request - owner * slots]
        zero = jnp.zeros_like(query)
        at = pl.ds(pl.multiple_of(s * heads, heads), heads)
        both[at, :lanes] = jnp.where(top_half, query, zero)
        both[at, lanes:] = jnp.where(top_half, zero, query)
        begins[at, :] = jnp.full((heads, lanes), start, I32)
        ends[at, :] = jnp.full((heads, lanes), end, I32)
        first = start // block_rows
        covered = (first == last_block) & (s < last_slot + slot_group)
        first = jnp.where(covered, first + 1, first)
        last = (end - 1) // block_rows

        def item(block, made):
            items[2 * made] = block
            items[2 * made + 1] = s
            return made + 1

        made_now = lax.fori_loop(first, last + 1, item, made)
        new = made_now > made
        return (
            end,
            made_now,
            jnp.where(new, last, last_block),
            jnp.where(new, s, last_slot),
        )

    none = jnp.int32(-1)
    _, made, _, _ = lax.fori_loop(0, slots, slot, (jnp.int32(0), jnp.int32(0), none, none))
    for u in range(unroll):
        items[2 * (made + u)] = 0
        items[2 * (made + u) + 1] = slots
    steps = (made + unroll - 1) // unroll
    across = lax.broadcasted_iota(I32, (group_rows, block_rows), 1)

    def place_of(i):
        block = pl.multiple_of(items[2 * i] * block_rows, block_rows)
        rows = pl.multiple_of(items[2 * i + 1] * heads, heads)
        return block, pl.ds(block, block_rows), pl.ds(rows, group_rows)

    def score_step(step, carry):
        for u in range(unroll):
            i = step * unroll + u
            block, cache, rows = place_of(i)
            raw = lax.dot_general(
                both[rows, :], keys[cache, :], contract_minor, preferred_element_type=F32
            )
            position = block + across
            begin, end = (jnp.concatenate([b[rows, :]] * (block_rows // lanes), axis=1) for b in (begins, ends))
            inside = (position >= begin) & (position < end)
            masked = jnp.where(inside, raw * scale, masked_score)
            scores[i] = masked
            tops[rows, :] = jnp.maximum(tops[rows, :], folded(jnp.maximum, masked))
        return carry

    def value_step(step, carry):
        for u in range(unroll):
            i = step * unroll + u
            _, cache, rows = place_of(i)
            top = tops[rows, :]
            shifted = jnp.exp(scores[i] - jnp.concatenate([top] * (block_rows // lanes), axis=1))
            sums[rows, :] += folded(jnp.add, shifted)
            total[rows, :] += jnp.dot(
                shifted.astype(BF16), values[cache, :], preferred_element_type=F32
            )
        return carry

    lax.fori_loop(0, steps, score_step, 0)
    top = jnp.max(tops[...], axis=1, keepdims=True)
    tops[...] = jnp.broadcast_to(top, tops.shape)
    lax.fori_loop(0, steps, value_step, 0)

    real = slots * heads
    row = lax.broadcasted_iota(I32, (real, lanes), 0)
    upper = row % heads < half
    picked = jnp.where(upper, total[:real, :lanes], total[:real, lanes:])
    attended[...] = picked / jnp.sum(sums[:real, :], axis=1, keepdims=True)
    per_block = half // count
    for k in range(count):
        outs[k][...] = jnp.zeros(outs[k].shape, BF16)
        for kv in range(2):
            for j in range(per_block):
                head = kv * half + (own ^ k) * per_block + j
                at = (kv * per_block + j) * lanes
                outs[k][:slots, at : at + lanes] = attended[
                    pl.ds(head, slots, stride=heads), :
                ].astype(BF16)
    copy.wait()


def attention(table, query_blocks, keys, values, ahead, unroll=8):
    count = len(query_blocks)
    slots, heads, _ = query_blocks[0].shape
    pool, width = keys.shape
    most = pool // block_rows + slots + unroll
    rows = (slots + slot_group) * heads
    return pl.pallas_call(
        functools.partial(
            attention_kernel, slots=slots, count=count, scale=1.0 / math.sqrt(lanes), unroll=unroll
        ),
        in_specs=[smem] + [vmem] * (count + 2) + [hbm],
        out_specs=[vmem] * (count + 1),
        out_shape=[jax.ShapeDtypeStruct((up_to(slots, 8), heads // count * lanes), BF16)] * count
        + [pltpu.VMEM(ahead.shape, ahead.dtype)],
        scratch_shapes=[
            pltpu.VMEM((count * slots, heads, lanes), BF16),
            pltpu.VMEM((rows, width), BF16),
            pltpu.VMEM((rows, lanes), I32),
            pltpu.VMEM((rows, lanes), I32),
            pltpu.VMEM((rows, lanes), F32),
            pltpu.VMEM((rows, lanes), F32),
            pltpu.VMEM((most, slot_group * heads, block_rows), F32),
            pltpu.VMEM((rows, width), F32),
            pltpu.VMEM((slots * heads, lanes), F32),
            pltpu.SMEM((2 * most,), I32),
            pltpu.SemaphoreType.DMA,
        ],
        compiler_params=params(12),
        cost_estimate=pl.CostEstimate(
            flops=4 * pool * heads * lanes, bytes_accessed=pool * width * 4, transcendentals=0
        ),
        name="attention",
    )(table, *query_blocks, in_vmem(keys), in_vmem(values), in_hbm(ahead))


def projection_kernel(table, *refs, slots, count, parts):
    pieces, weight, outs = refs[:parts], refs[parts], refs[parts + 1 :]
    own_att, own_ffn = table[0], table[1]
    requests = slots * count
    padded = pieces[0].shape[0] // count
    depth = weight.shape[0] // parts
    row = lax.broadcasted_iota(I32, (requests, padded), 0)
    wanted = row
    for k in range(count):
        moved = row + ((own_att ^ k) - k) * slots
        wanted = jnp.where((row >= k * slots) & (row < (k + 1) * slots), moved, wanted)
    choose = []
    lane = lax.broadcasted_iota(I32, (1, padded), 1)
    for k in range(count):
        served = jnp.full((1, padded), -1, I32)
        for i in range(slots):
            request = table[2 + slots + (own_att ^ k) * slots + i]
            served = jnp.where(lane == i, request, served)
        choose.append((wanted == served).astype(F32).astype(BF16))
    total = None
    for p in range(parts):
        rows = None
        for k in range(count):
            term = jnp.dot(
                choose[k],
                pieces[p][k * padded : (k + 1) * padded, :],
                preferred_element_type=F32,
            )
            rows = term if rows is None else rows + term
        at = pl.ds(pl.multiple_of((own_ffn ^ p) * depth, depth), depth)
        term = jnp.dot(rows.astype(BF16), weight[at, :], preferred_element_type=F32)
        total = term if total is None else total + term
    for k in range(count):
        outs[k][...] = halves_stacked(total[k * slots : (k + 1) * slots]).astype(BF16)


def projection(table, pieces, weight, slots, count):
    parts = len(pieces)
    depth, width = weight.shape
    return pl.pallas_call(
        functools.partial(projection_kernel, slots=slots, count=count, parts=parts),
        in_specs=[smem] + [vmem] * (1 + parts),
        out_specs=[vmem] * count,
        out_shape=[jax.ShapeDtypeStruct((2 * slots, width // 2), BF16)] * count,
        compiler_params=params(8),
        cost_estimate=pl.CostEstimate(
            flops=2 * slots * count * depth * width, bytes_accessed=depth * width, transcendentals=0
        ),
        name="projection",
    )(table, *pieces, in_vmem(weight))


def residual_kernel(*refs, joined):
    base, blocks, out = refs[0], refs[1:-1], refs[-1]
    total = base[...].astype(F32)
    if not joined:
        total = halves_stacked(total)
    for block in blocks:
        total = total + block[...].astype(F32)
    out[...] = (halves_joined(total) if joined else total).astype(BF16)


def residual(base, blocks, joined):
    rows, half = blocks[0].shape
    shape = (rows // 2, 2 * half) if joined else (rows, half)
    return pl.pallas_call(
        functools.partial(residual_kernel, joined=joined),
        in_specs=[vmem] * (1 + len(blocks)),
        out_specs=vmem,
        out_shape=jax.ShapeDtypeStruct(shape, BF16),
        compiler_params=params(2),
        name="residual",
    )(base, *blocks)


def hidden_kernel(table, *refs, count, masks, ahead_masks, far):
    own = table[1]
    sem = refs[-1]
    if far:
        blocks, (gain, gate, up, ahead, send, keep, scaled, landed, joined, _) = (
            refs[:count],
            refs[count:],
        )
    else:
        scaled, gate, up, ahead, send, keep, landed, _ = refs
    width = keep.shape[1]
    units = (width - lanes if far else width) // 2
    copies = [
        pltpu.make_async_copy(
            ahead.at[pl.ds(pl.multiple_of((own ^ mask) * units, units), units)],
            landed.at[m],
            sem.at[m],
        )
        for m, mask in enumerate(ahead_masks)
    ]
    for copy in copies:
        copy.start()
    if far:
        rows = blocks[0].shape[0] // 2
        for k in range(count):
            joined[k * rows : (k + 1) * rows, :] = halves_joined(blocks[k][...])
        middle = joined[...]
        squares = jnp.sum(middle * middle, axis=1, keepdims=True)
        scaled[...] = (middle * gain[...].astype(F32)).astype(BF16)
    for m, target in enumerate((send, keep)):
        at = pl.ds(pl.multiple_of((own ^ masks[m]) * units, units), units)
        for t, weight in enumerate((gate, up)):
            out = lax.dot_general(
                scaled[...], weight[at, :], contract_minor, preferred_element_type=F32
            )
            target[:, t * units : (t + 1) * units] = out.astype(target.dtype)
    if far:
        send[:, 2 * units :] = high_low(squares).astype(BF16)
        keep[:, 2 * units :] = jnp.broadcast_to(squares, (squares.shape[0], lanes))
    for copy in copies:
        copy.wait()


def hidden_cost(requests, units, width):
    return pl.CostEstimate(
        flops=8 * requests * units * width, bytes_accessed=4 * units * width, transcendentals=0
    )


def hidden_far(table, blocks, gain, gate, up, ahead, owners):
    count = len(blocks)
    rows, half = blocks[0].shape
    requests, width = rows // 2 * count, 2 * half
    units = gate.shape[0] // owners
    across = 2 * units + lanes
    return pl.pallas_call(
        functools.partial(
            hidden_kernel, count=count, masks=(3, 2), ahead_masks=(0, 1), far=True
        ),
        in_specs=[smem] + [vmem] * (count + 3) + [hbm],
        out_specs=[vmem] * 4,
        out_shape=[
            jax.ShapeDtypeStruct((requests, across), BF16),
            jax.ShapeDtypeStruct((requests, across), F32),
            jax.ShapeDtypeStruct((requests, width), BF16),
            pltpu.VMEM((2, units, ahead.shape[1]), BF16),
        ],
        scratch_shapes=[pltpu.VMEM((requests, width), F32), pltpu.SemaphoreType.DMA((2,))],
        compiler_params=params(8),
        cost_estimate=hidden_cost(requests, units, width),
        name="hidden_far",
    )(table, *blocks, gain, in_vmem(gate), in_vmem(up), in_hbm(ahead))


def hidden_near(table, scaled, gate, up, ahead, owners):
    requests, width = scaled.shape
    units = gate.shape[0] // owners
    return pl.pallas_call(
        functools.partial(
            hidden_kernel, count=0, masks=(1, 0), ahead_masks=(2, 3), far=False
        ),
        in_specs=[smem] + [vmem] * 3 + [hbm],
        out_specs=[vmem] * 3,
        out_shape=[
            jax.ShapeDtypeStruct((requests, 2 * units), BF16),
            jax.ShapeDtypeStruct((requests, 2 * units), F32),
            pltpu.VMEM((2, units, ahead.shape[1]), BF16),
        ],
        scratch_shapes=[pltpu.SemaphoreType.DMA((2,))],
        compiler_params=params(8),
        cost_estimate=hidden_cost(requests, units, width),
        name="hidden_near",
    )(table, scaled, in_vmem(gate), in_vmem(up), in_hbm(ahead))


def chip_sum_kernel(keep, arrived, out, squares):
    width = keep.shape[1] - lanes
    out[:, :width] = (keep[:, :width] + arrived[:, :width].astype(F32)).astype(BF16)
    tail = arrived[:, width:].astype(F32)
    chip = keep[:, width:] + (tail[:, :1] + tail[:, lanes // 2 : lanes // 2 + 1])
    squares[...] = chip
    out[:, width:] = high_low(chip).astype(BF16)


def chip_sum(keep, arrived):
    requests, width = keep.shape
    return pl.pallas_call(
        chip_sum_kernel,
        in_specs=[vmem] * 2,
        out_specs=[vmem] * 2,
        out_shape=[
            jax.ShapeDtypeStruct((requests, width), BF16),
            jax.ShapeDtypeStruct((requests, lanes), F32),
        ],
        compiler_params=params(2),
        name="chip_sum",
    )(keep, arrived)


def active_kernel(near, beside, far, squares, out, *, model_width):
    units = near.shape[1] // 2
    tail = far[:, 2 * units :].astype(F32)
    square = squares[:, :1] + (tail[:, :1] + tail[:, lanes // 2 : lanes // 2 + 1])
    scale = lax.rsqrt(square / model_width + epsilon)

    def total(at):
        both = near[:, at : at + units] + beside[:, at : at + units].astype(F32)
        return (both + far[:, at : at + units].astype(F32)) * scale

    gate = total(0)
    out[...] = (gate / (1.0 + jnp.exp(-gate)) * total(units)).astype(BF16)


def active_units(near, beside, far, squares, model_width):
    requests, width = near.shape
    return pl.pallas_call(
        functools.partial(active_kernel, model_width=model_width),
        in_specs=[vmem] * 4,
        out_specs=vmem,
        out_shape=jax.ShapeDtypeStruct((requests, width // 2), BF16),
        compiler_params=params(4),
        name="active",
    )(near, beside, far, squares)


def down_kernel(*refs, count, first, last):
    pieces, weight, rest = refs[:2], refs[2], refs[3:]
    total = None if first else rest[0][...]
    outs = rest if first else rest[1:]
    for m, piece in enumerate(pieces):
        term = jnp.dot(piece[...], weight[m], preferred_element_type=F32)
        total = term if total is None else total + term
    if last:
        rows = total.shape[0] // count
        for k in range(count):
            outs[k][...] = halves_stacked(total[k * rows : (k + 1) * rows]).astype(BF16)
    else:
        outs[0][...] = total


def down_part(pieces, weight, count, before=None, last=False):
    first = before is None
    requests, units = pieces[0].shape
    width = weight.shape[2]
    if last:
        outs = [jax.ShapeDtypeStruct((2 * requests // count, width // 2), BF16)] * count
    else:
        outs = [jax.ShapeDtypeStruct((requests, width), F32)]
    return pl.pallas_call(
        functools.partial(down_kernel, count=count, first=first, last=last),
        in_specs=[vmem] * (3 if first else 4),
        out_specs=[vmem] * len(outs),
        out_shape=outs,
        compiler_params=params(8),
        cost_estimate=pl.CostEstimate(
            flops=4 * requests * units * width,
            bytes_accessed=2 * units * width,
            transcendentals=0,
        ),
        name="down",
    )(*pieces, in_vmem(weight), *([] if first else [before]))


def swaps_of(blocks):
    count = len(blocks)
    arrived = {k: pair_swap(blocks[k], "att", k) for k in reversed(range(1, count))}
    return [blocks[0]] + [arrived[k] for k in range(1, count)]


def exchanging_device(*args):
    return exchanging_layer(*args)


def exchanging_layer(
    hidden_state,
    queries,
    key_cache,
    value_cache,
    lengths,
    assignment,
    out_weight,
    norm_gain,
    gate_weight,
    up_weight,
    down_weight,
):
    slots, columns = hidden_state.shape
    count = lax.axis_size("att")
    parts = lax.axis_size("ffn")
    model_width = columns * parts
    heads = queries.shape[1] // lanes
    own = jnp.stack([lax.axis_index("att"), lax.axis_index("ffn")]).astype(I32)
    table = jnp.concatenate([own, lengths, assignment])
    own_queries = queries.reshape(slots, heads, lanes)
    query_blocks = swaps_of([own_queries] * count)
    keys, values = fetch([key_cache, value_cache])
    *blocks, weight = attention(
        table, query_blocks, keys, values, out_weight.reshape(-1, columns)
    )

    blocks = swaps_of(blocks)
    piece = jnp.concatenate(blocks, axis=0)
    across = pair_swap(piece, "ffn", 2)
    beside = pair_swap(piece, "ffn", 1)
    corner = pair_swap(across, "ffn", 1)
    partial = projection(table, [piece, beside, across, corner], weight, slots, count)
    (gate,) = fetch([gate_weight])
    middle = residual(hidden_state, swaps_of(partial), False)

    rows = swaps_of([middle] * count)
    (up,) = fetch([up_weight])
    gain = norm_gain.reshape(1, columns)
    far_send, far_keep, scaled, down_chip = hidden_far(
        table, rows, gain, gate, up, down_weight, parts
    )
    far, squares = chip_sum(far_keep, pair_swap(far_send, "ffn", 1))
    far = pair_swap(far, "ffn", 2)
    near_send, near_keep, down_other = hidden_near(
        table, scaled, gate, up, down_weight, parts
    )
    near_beside = pair_swap(near_send, "ffn", 1)
    active = active_units(near_keep, near_beside, far, squares, model_width)

    across = pair_swap(active, "ffn", 2)
    beside = pair_swap(active, "ffn", 1)
    (before,) = down_part([active, beside], down_chip, count)
    corner = pair_swap(across, "ffn", 1)
    partial = down_part([across, corner], down_other, count, before, True)
    return residual_joined(middle, swaps_of(partial))


def residual_joined(middle, blocks):
    return residual(middle, blocks, True)


def solution(mesh):
    count, parts = mesh.shape["att"], mesh.shape["ffn"]
    paired = count == 4 and parts == 4
    in_specs = (
        P(("group", "att"), "ffn"),
        P(("group", "att"), "ffn"),
        P(("group", "att"), "ffn"),
        P(("group", "att"), "ffn"),
        P(("group", "att")),
        P("group"),
        P(None, "att", "ffn"),
        P("ffn"),
        P("att", "ffn"),
        P("att", "ffn"),
        P("att", "ffn"),
    )
    out_specs = P(("group", "att"), "ffn")
    return jax.shard_map(
        exchanging_device if paired else general_device,
        mesh=mesh,
        in_specs=in_specs,
        out_specs=out_specs,
        check_vma=False,
    )
```

```python
import functools
import math

import jax
import jax.numpy as jnp
from jax import lax
from jax.experimental import pallas as pl
from jax.experimental.pallas import tpu as pltpu
from jax.sharding import PartitionSpec as P

epsilon = 1e-05
masked_score = -1e30
lanes = 128
block_rows = 256
slot_group = 2
contract_minor = (((1,), (1,)), ((), ()))
F32 = jnp.float32
BF16 = jnp.bfloat16
I32 = jnp.int32
vmem = pl.BlockSpec(memory_space=pltpu.VMEM)
smem = pl.BlockSpec(memory_space=pltpu.SMEM)
hbm = pl.BlockSpec(memory_space=pltpu.HBM)


def softmax_rounded(scores):
    row_top = jnp.max(scores, axis=-1, keepdims=True)
    shifted = jnp.exp(scores - row_top)
    totals = jnp.sum(shifted, axis=-1, keepdims=True)
    return (shifted / totals).astype(jnp.bfloat16)


def general_device(
    hidden_state,
    queries,
    key_cache,
    value_cache,
    lengths,
    assignment,
    out_weight,
    norm_gain,
    gate_weight,
    up_weight,
    down_weight,
):
    rows_dev = hidden_state.shape[0]
    columns = hidden_state.shape[1]
    att_count = lax.axis_size("att")
    ffn_count = lax.axis_size("ffn")
    requests = rows_dev * att_count
    kv_total = out_weight.shape[0]
    kv_local = kv_total // ffn_count
    model_width = columns * ffn_count
    pool_rows = key_cache.shape[0]
    head_size = key_cache.shape[1] // kv_local
    per_group = queries.shape[1] // (kv_local * head_size)
    score_scale = 1.0 / math.sqrt(head_size)
    att_place = lax.axis_index("att")
    every_query = lax.all_gather(queries, "att", axis=0, tiled=True)
    own_slots = lax.dynamic_slice_in_dim(assignment, att_place * rows_dev, rows_dev)
    slot_queries = jnp.take(every_query, own_slots, axis=0).reshape(
        rows_dev, kv_local, per_group, head_size
    )
    keys_local = key_cache.reshape(pool_rows, kv_local, head_size)
    values_local = value_cache.reshape(pool_rows, kv_local, head_size)
    slot_starts = jnp.cumsum(lengths) - lengths
    slot_ends = slot_starts + lengths
    positions = jnp.arange(pool_rows, dtype=jnp.int32)
    owned_rows = (positions[None, :] >= slot_starts[:, None]) & (
        positions[None, :] < slot_ends[:, None]
    )
    owned_rows = owned_rows[:, None, None, :]
    raw_scores = (
        jnp.einsum("rkgc,pkc->rkgp", slot_queries, keys_local, preferred_element_type=jnp.float32)
        * score_scale
    )
    weights = softmax_rounded(jnp.where(owned_rows, raw_scores, masked_score))
    attended = jnp.einsum(
        "rkgp,pkc->rkgc", weights, values_local, preferred_element_type=jnp.float32
    )
    attended = attended.astype(jnp.bfloat16).reshape(rows_dev, kv_local, per_group * head_size)
    spread = lax.all_to_all(attended, "att", split_axis=2, concat_axis=0, tiled=True)
    pieces = lax.all_gather(spread, "ffn", axis=1, tiled=True)
    inverse = (
        jnp.zeros((requests,), jnp.int32).at[assignment].set(jnp.arange(requests, dtype=jnp.int32))
    )
    request_pieces = jnp.take(pieces, inverse, axis=0)
    block = request_pieces
    projected = lax.psum_scatter(
        jnp.einsum("rkc,kcd->rd", block, out_weight, preferred_element_type=jnp.float32).astype(
            jnp.bfloat16
        ),
        "att",
        scatter_dimension=0,
        tiled=True,
    ).astype(jnp.float32)
    middle_short = (hidden_state.astype(jnp.float32) + projected).astype(jnp.bfloat16)
    middle = lax.optimization_barrier(middle_short).astype(jnp.float32)
    squares = lax.psum(jnp.sum(middle * middle, axis=1), "ffn")
    normed = (
        middle * lax.rsqrt(squares[:, None] / model_width + epsilon) * norm_gain.astype(jnp.float32)
    ).astype(jnp.bfloat16)
    every_row = lax.all_gather(normed, "att", axis=0, tiled=True)
    contract = (((1,), (1,)), ((), ()))
    gate_part = lax.dot_general(
        gate_weight, every_row, contract, preferred_element_type=jnp.float32
    )
    up_part = lax.dot_general(up_weight, every_row, contract, preferred_element_type=jnp.float32)
    totals = lax.psum(
        jnp.concatenate([gate_part, up_part], axis=1).astype(jnp.bfloat16), "ffn"
    ).astype(jnp.float32)
    unit_active = (jax.nn.silu(totals[:, :requests]) * totals[:, requests:]).astype(jnp.bfloat16)
    block = unit_active
    returned = lax.psum_scatter(
        lax.dot_general(
            block, down_weight, (((0,), (0,)), ((), ())), preferred_element_type=jnp.float32
        ).astype(jnp.bfloat16),
        "att",
        scatter_dimension=0,
        tiled=True,
    ).astype(jnp.float32)
    return (middle + returned).astype(jnp.bfloat16)


def pair_swap(value, axis, bit):
    count = lax.axis_size(axis)
    return lax.ppermute(value, axis, [(i, i ^ bit) for i in range(count)])


def up_to(value, multiple):
    return -(-value // multiple) * multiple


def params(megabytes):
    return pltpu.CompilerParams(vmem_limit_bytes=megabytes << 20)


def halves_joined(block):
    block = block.astype(F32)
    rows = block.shape[0] // 2
    return jnp.concatenate([block[:rows], block[rows:]], axis=1)


def halves_stacked(block):
    half = block.shape[1] // 2
    return jnp.concatenate([block[:, :half], block[:, half:]], axis=0)


def high_low(value):
    high = value.astype(BF16).astype(F32)
    low = value - high
    lane = lax.broadcasted_iota(I32, (value.shape[0], lanes), 1)
    return jnp.where(lane < lanes // 2, high, low)


def in_hbm(value):
    return pltpu.with_memory_space_constraint(value, pltpu.HBM)


def in_vmem(value):
    return pltpu.with_memory_space_constraint(value, pltpu.VMEM)


def job_shapes(jobs, parts):
    shapes = []
    for array, masks in jobs:
        if masks is None:
            shapes.append(pltpu.VMEM(array.shape, array.dtype))
        else:
            rows, width = array.shape
            shapes.append(pltpu.VMEM((len(masks), rows // parts, width), array.dtype))
    return shapes


def job_count(jobs):
    return sum(1 if masks is None else len(masks) for _, masks in jobs)


def job_copies(own, masks_of, sources, targets, sems):
    copies = []
    for masks, source, target in zip(masks_of, sources, targets):
        if masks is None:
            copies.append(pltpu.make_async_copy(source, target, sems.at[len(copies)]))
            continue
        rows = target.shape[1]
        for m, mask in enumerate(masks):
            at = pl.ds(pl.multiple_of((own ^ mask) * rows, rows), rows)
            copies.append(
                pltpu.make_async_copy(source.at[at], target.at[m], sems.at[len(copies)])
            )
    return copies


def masks_in(jobs):
    return tuple(masks for _, masks in jobs)


def fetch_kernel(table, *refs, masks_of):
    count = len(masks_of)
    copies = job_copies(table[1], masks_of, refs[:count], refs[count:-1], refs[-1])
    for copy in copies:
        copy.start()
    for copy in copies:
        copy.wait()


def fetch(table, jobs, parts):
    shapes = job_shapes(jobs, parts)
    moved = sum(2 * math.prod(shape.shape) for shape in shapes)
    return pl.pallas_call(
        functools.partial(fetch_kernel, masks_of=masks_in(jobs)),
        in_specs=[smem] + [hbm] * len(jobs),
        out_specs=[vmem] * len(jobs),
        out_shape=shapes,
        scratch_shapes=[pltpu.SemaphoreType.DMA((job_count(jobs),))],
        compiler_params=params(1),
        cost_estimate=pl.CostEstimate(flops=0, bytes_accessed=2 * moved, transcendentals=0),
        name="fetch",
    )(table, *[in_hbm(array) for array, _ in jobs])


def folded(combine, value):
    parts = [value[:, i : i + lanes] for i in range(0, value.shape[1], lanes)]
    return functools.reduce(combine, parts)


def attention_kernel(table, *refs, slots, count, scale, unroll, masks_of):
    jobs = len(masks_of)
    query_blocks, (keys, values), sources = (
        refs[:count],
        refs[count : count + 2],
        refs[count + 2 : count + 2 + jobs],
    )
    outs, targets = (
        refs[count + 2 + jobs : 2 * count + 2 + jobs],
        refs[2 * count + 2 + jobs : 2 * count + 2 + 2 * jobs],
    )
    queries, both, begins, ends, tops, sums, scores, total, attended, items, sems = refs[
        2 * count + 2 + 2 * jobs :
    ]
    copies = job_copies(table[1], masks_of, sources, targets, sems)
    for copy in copies:
        copy.start()
    pool, width = keys.shape
    heads = queries.shape[1]
    half = heads // 2
    own = table[0]
    group_rows = slot_group * heads
    top_half = lax.broadcasted_iota(I32, (heads, lanes), 0) < half
    for k in range(count):
        queries[k * slots : (k + 1) * slots] = query_blocks[k][...]

    tops[...] = jnp.full(tops.shape, masked_score, F32)
    sums[...] = jnp.zeros(sums.shape, F32)
    total[...] = jnp.zeros(total.shape, F32)
    spare = slots * heads
    both[spare:, :] = jnp.zeros((both.shape[0] - spare, width), BF16)
    begins[spare:, :] = jnp.full((begins.shape[0] - spare, lanes), pool, I32)
    ends[spare:, :] = jnp.zeros((ends.shape[0] - spare, lanes), I32)

    def slot(s, carry):
        start, made, last_block, last_slot = carry
        end = start + table[2 + s]
        request = table[2 + slots + own * slots + s]
        owner = sum((request >= k * slots).astype(I32) for k in range(1, count))
        query = queries[(owner ^ own) * slots + request - owner * slots]
        zero = jnp.zeros_like(query)
        at = pl.ds(pl.multiple_of(s * heads, heads), heads)
        both[at, :lanes] = jnp.where(top_half, query, zero)
        both[at, lanes:] = jnp.where(top_half, zero, query)
        begins[at, :] = jnp.full((heads, lanes), start, I32)
        ends[at, :] = jnp.full((heads, lanes), end, I32)
        first = start // block_rows
        covered = (first == last_block) & (s < last_slot + slot_group)
        first = jnp.where(covered, first + 1, first)
        last = (end - 1) // block_rows

        def item(block, made):
            items[2 * made] = block
            items[2 * made + 1] = s
            return made + 1

        made_now = lax.fori_loop(first, last + 1, item, made)
        new = made_now > made
        return (
            end,
            made_now,
            jnp.where(new, last, last_block),
            jnp.where(new, s, last_slot),
        )

    none = jnp.int32(-1)
    _, made, _, _ = lax.fori_loop(0, slots, slot, (jnp.int32(0), jnp.int32(0), none, none))
    for u in range(unroll):
        items[2 * (made + u)] = 0
        items[2 * (made + u) + 1] = slots
    steps = (made + unroll - 1) // unroll
    across = lax.broadcasted_iota(I32, (group_rows, block_rows), 1)

    def place_of(i):
        block = pl.multiple_of(items[2 * i] * block_rows, block_rows)
        rows = pl.multiple_of(items[2 * i + 1] * heads, heads)
        return block, pl.ds(block, block_rows), pl.ds(rows, group_rows)

    def score_step(step, carry):
        for u in range(unroll):
            i = step * unroll + u
            block, cache, rows = place_of(i)
            raw = lax.dot_general(
                both[rows, :], keys[cache, :], contract_minor, preferred_element_type=F32
            )
            position = block + across
            begin, end = (jnp.concatenate([b[rows, :]] * (block_rows // lanes), axis=1) for b in (begins, ends))
            inside = (position >= begin) & (position < end)
            masked = jnp.where(inside, raw * scale, masked_score)
            scores[i] = masked
            tops[rows, :] = jnp.maximum(tops[rows, :], folded(jnp.maximum, masked))
        return carry

    def value_step(step, carry):
        for u in range(unroll):
            i = step * unroll + u
            _, cache, rows = place_of(i)
            top = tops[rows, :]
            shifted = jnp.exp(scores[i] - jnp.concatenate([top] * (block_rows // lanes), axis=1))
            sums[rows, :] += folded(jnp.add, shifted)
            total[rows, :] += jnp.dot(
                shifted.astype(BF16), values[cache, :], preferred_element_type=F32
            )
        return carry

    lax.fori_loop(0, steps, score_step, 0)
    top = jnp.max(tops[...], axis=1, keepdims=True)
    tops[...] = jnp.broadcast_to(top, tops.shape)
    lax.fori_loop(0, steps, value_step, 0)

    real = slots * heads
    row = lax.broadcasted_iota(I32, (real, lanes), 0)
    upper = row % heads < half
    picked = jnp.where(upper, total[:real, :lanes], total[:real, lanes:])
    attended[...] = picked / jnp.sum(sums[:real, :], axis=1, keepdims=True)
    per_block = half // count
    for k in range(count):
        outs[k][...] = jnp.zeros(outs[k].shape, BF16)
        for kv in range(2):
            for j in range(per_block):
                head = kv * half + (own ^ k) * per_block + j
                at = (kv * per_block + j) * lanes
                outs[k][:slots, at : at + lanes] = attended[
                    pl.ds(head, slots, stride=heads), :
                ].astype(BF16)
    for copy in copies:
        copy.wait()


def attention(table, query_blocks, keys, values, jobs, parts, unroll=8):
    count = len(query_blocks)
    slots, heads, _ = query_blocks[0].shape
    pool, width = keys.shape
    most = pool // block_rows + slots + unroll
    rows = (slots + slot_group) * heads
    return pl.pallas_call(
        functools.partial(
            attention_kernel,
            slots=slots,
            count=count,
            scale=1.0 / math.sqrt(lanes),
            unroll=unroll,
            masks_of=masks_in(jobs),
        ),
        in_specs=[smem] + [vmem] * (count + 2) + [hbm] * len(jobs),
        out_specs=[vmem] * (count + len(jobs)),
        out_shape=[jax.ShapeDtypeStruct((up_to(slots, 8), heads // count * lanes), BF16)] * count
        + job_shapes(jobs, parts),
        scratch_shapes=[
            pltpu.VMEM((count * slots, heads, lanes), BF16),
            pltpu.VMEM((rows, width), BF16),
            pltpu.VMEM((rows, lanes), I32),
            pltpu.VMEM((rows, lanes), I32),
            pltpu.VMEM((rows, lanes), F32),
            pltpu.VMEM((rows, lanes), F32),
            pltpu.VMEM((most, slot_group * heads, block_rows), F32),
            pltpu.VMEM((rows, width), F32),
            pltpu.VMEM((slots * heads, lanes), F32),
            pltpu.SMEM((2 * most,), I32),
            pltpu.SemaphoreType.DMA((job_count(jobs),)),
        ],
        compiler_params=params(12),
        cost_estimate=pl.CostEstimate(
            flops=4 * pool * heads * lanes, bytes_accessed=pool * width * 4, transcendentals=0
        ),
        name="attention",
    )(
        table,
        *query_blocks,
        in_vmem(keys),
        in_vmem(values),
        *[in_hbm(array) for array, _ in jobs],
    )


def projection_kernel(table, *refs, slots, count, parts, masks_of):
    pieces, weight, source = refs[:parts], refs[parts], refs[parts + 1]
    outs, target, sems = refs[parts + 2 : -2], refs[-2], refs[-1]
    copies = job_copies(table[1], masks_of, [source], [target], sems)
    for copy in copies:
        copy.start()
    own_att = table[0]
    requests = slots * count
    padded = pieces[0].shape[0] // count
    row = lax.broadcasted_iota(I32, (requests, padded), 0)
    wanted = row
    for k in range(count):
        moved = row + ((own_att ^ k) - k) * slots
        wanted = jnp.where((row >= k * slots) & (row < (k + 1) * slots), moved, wanted)
    choose = []
    lane = lax.broadcasted_iota(I32, (1, padded), 1)
    for k in range(count):
        served = jnp.full((1, padded), -1, I32)
        for i in range(slots):
            request = table[2 + slots + (own_att ^ k) * slots + i]
            served = jnp.where(lane == i, request, served)
        choose.append((wanted == served).astype(F32).astype(BF16))
    total = None
    for p in range(parts):
        rows = None
        for k in range(count):
            term = jnp.dot(
                choose[k],
                pieces[p][k * padded : (k + 1) * padded, :],
                preferred_element_type=F32,
            )
            rows = term if rows is None else rows + term
        term = jnp.dot(rows.astype(BF16), weight[p], preferred_element_type=F32)
        total = term if total is None else total + term
    for k in range(count):
        outs[k][...] = halves_stacked(total[k * slots : (k + 1) * slots]).astype(BF16)
    for copy in copies:
        copy.wait()


def projection(table, pieces, weight, slots, count, jobs):
    parts, depth, width = weight.shape
    return pl.pallas_call(
        functools.partial(
            projection_kernel, slots=slots, count=count, parts=parts, masks_of=masks_in(jobs)
        ),
        in_specs=[smem] + [vmem] * (1 + parts) + [hbm],
        out_specs=[vmem] * (count + 1),
        out_shape=[jax.ShapeDtypeStruct((2 * slots, width // 2), BF16)] * count
        + job_shapes(jobs, parts),
        scratch_shapes=[pltpu.SemaphoreType.DMA((job_count(jobs),))],
        compiler_params=params(8),
        cost_estimate=pl.CostEstimate(
            flops=2 * slots * count * parts * depth * width,
            bytes_accessed=parts * depth * width,
            transcendentals=0,
        ),
        name="projection",
    )(table, *pieces, in_vmem(weight), in_hbm(jobs[0][0]))


def residual_kernel(*refs, joined):
    base, blocks, out = refs[0], refs[1:-1], refs[-1]
    total = base[...].astype(F32)
    if not joined:
        total = halves_stacked(total)
    for block in blocks:
        total = total + block[...].astype(F32)
    out[...] = (halves_joined(total) if joined else total).astype(BF16)


def residual(base, blocks, joined):
    rows, half = blocks[0].shape
    shape = (rows // 2, 2 * half) if joined else (rows, half)
    return pl.pallas_call(
        functools.partial(residual_kernel, joined=joined),
        in_specs=[vmem] * (1 + len(blocks)),
        out_specs=vmem,
        out_shape=jax.ShapeDtypeStruct(shape, BF16),
        compiler_params=params(2),
        name="residual",
    )(base, *blocks)


def unit_product(scaled, weight, part):
    return lax.dot_general(scaled, weight[part], contract_minor, preferred_element_type=F32)


def product_cost(requests, units, width):
    return pl.CostEstimate(
        flops=2 * requests * units * width, bytes_accessed=units * width, transcendentals=0
    )


def hidden_first_kernel(*refs, count, part):
    blocks, (gain, weight, send, scaled, squares, joined) = refs[:count], refs[count:]
    rows = blocks[0].shape[0] // 2
    for k in range(count):
        joined[k * rows : (k + 1) * rows, :] = halves_joined(blocks[k][...])
    middle = joined[...]
    square = jnp.sum(middle * middle, axis=1, keepdims=True)
    scaled[...] = (middle * gain[...].astype(F32)).astype(BF16)
    units = weight.shape[1]
    send[:, :units] = unit_product(scaled[...], weight, part).astype(BF16)
    send[:, units:] = high_low(square).astype(BF16)
    squares[...] = jnp.broadcast_to(square, squares.shape)


def hidden_first(blocks, gain, weight, part):
    count = len(blocks)
    rows, half = blocks[0].shape
    requests, width = rows // 2 * count, 2 * half
    units = weight.shape[1]
    return pl.pallas_call(
        functools.partial(hidden_first_kernel, count=count, part=part),
        in_specs=[vmem] * (count + 2),
        out_specs=[vmem] * 3,
        out_shape=[
            jax.ShapeDtypeStruct((requests, units + lanes), BF16),
            jax.ShapeDtypeStruct((requests, width), BF16),
            jax.ShapeDtypeStruct((requests, lanes), F32),
        ],
        scratch_shapes=[pltpu.VMEM((requests, width), F32)],
        compiler_params=params(6),
        cost_estimate=product_cost(requests, units, width),
        name="hidden_first",
    )(*blocks, gain, in_vmem(weight))


def hidden_kernel(scaled, *refs, parts):
    weights, out = refs[:-1], refs[-1]
    for t, (weight, part) in enumerate(zip(weights, parts)):
        units = weight.shape[1]
        out[:, t * units : (t + 1) * units] = unit_product(scaled[...], weight, part).astype(
            out.dtype
        )


def hidden_next(scaled, chosen, kind):
    requests, width = scaled.shape
    units = chosen[0][0].shape[1]
    return pl.pallas_call(
        functools.partial(hidden_kernel, parts=tuple(part for _, part in chosen)),
        in_specs=[vmem] * (1 + len(chosen)),
        out_specs=vmem,
        out_shape=jax.ShapeDtypeStruct((requests, len(chosen) * units), kind),
        compiler_params=params(6),
        cost_estimate=product_cost(requests, len(chosen) * units, width),
        name="hidden_next",
    )(scaled, *[in_vmem(weight) for weight, _ in chosen])


def squares_sum_kernel(keep, own_squares, arrived, out, squares):
    width = keep.shape[1]
    out[:, :width] = (keep[...] + arrived[:, :width].astype(F32)).astype(BF16)
    tail = arrived[:, width:].astype(F32)
    chip = own_squares[...] + (tail[:, :1] + tail[:, lanes // 2 : lanes // 2 + 1])
    squares[...] = chip
    out[:, width:] = high_low(chip).astype(BF16)


def squares_sum(keep, own_squares, arrived):
    requests, width = arrived.shape
    return pl.pallas_call(
        squares_sum_kernel,
        in_specs=[vmem] * 3,
        out_specs=[vmem] * 2,
        out_shape=[
            jax.ShapeDtypeStruct((requests, width), BF16),
            jax.ShapeDtypeStruct((requests, lanes), F32),
        ],
        compiler_params=params(2),
        name="squares_sum",
    )(keep, own_squares, arrived)


def chip_sum_kernel(keep, arrived, out):
    out[...] = (keep[...] + arrived[...].astype(F32)).astype(BF16)


def chip_sum(keep, arrived):
    return pl.pallas_call(
        chip_sum_kernel,
        in_specs=[vmem] * 2,
        out_specs=vmem,
        out_shape=jax.ShapeDtypeStruct(arrived.shape, BF16),
        compiler_params=params(2),
        name="chip_sum",
    )(keep, arrived)


def active_kernel(near, beside, far_gate, far_up, squares, out, *, model_width):
    units = far_up.shape[1]
    tail = far_gate[:, units:].astype(F32)
    square = squares[:, :1] + (tail[:, :1] + tail[:, lanes // 2 : lanes // 2 + 1])
    scale = lax.rsqrt(square / model_width + epsilon)

    def total(at, far):
        both = near[:, at : at + units] + beside[:, at : at + units].astype(F32)
        return (both + far.astype(F32)) * scale

    gate = total(0, far_gate[:, :units])
    out[...] = (gate / (1.0 + jnp.exp(-gate)) * total(units, far_up[...])).astype(BF16)


def active_units(near, beside, far_gate, far_up, squares, model_width):
    requests, width = near.shape
    return pl.pallas_call(
        functools.partial(active_kernel, model_width=model_width),
        in_specs=[vmem] * 5,
        out_specs=vmem,
        out_shape=jax.ShapeDtypeStruct((requests, width // 2), BF16),
        compiler_params=params(4),
        name="active",
    )(near, beside, far_gate, far_up, squares)


def down_kernel(*refs, parts, count, first, last):
    terms = len(parts)
    pieces, weights, rest = refs[:terms], refs[terms : 2 * terms], refs[2 * terms :]
    total = None if first else rest[0][...]
    outs = rest if first else rest[1:]
    for piece, weight, part in zip(pieces, weights, parts):
        term = jnp.dot(piece[...], weight[part], preferred_element_type=F32)
        total = term if total is None else total + term
    if last:
        rows = total.shape[0] // count
        for k in range(count):
            outs[k][...] = halves_stacked(total[k * rows : (k + 1) * rows]).astype(BF16)
    else:
        outs[0][...] = total


def down_part(chosen, count, before, last):
    requests, units = chosen[0][0].shape
    width = chosen[0][1].shape[2]
    if last:
        outs = [jax.ShapeDtypeStruct((2 * requests // count, width // 2), BF16)] * count
    else:
        outs = [jax.ShapeDtypeStruct((requests, width), F32)]
    before = [] if before is None else [before]
    return pl.pallas_call(
        functools.partial(
            down_kernel,
            parts=tuple(part for _, _, part in chosen),
            count=count,
            first=not before,
            last=last,
        ),
        in_specs=[vmem] * (2 * len(chosen) + len(before)),
        out_specs=[vmem] * len(outs),
        out_shape=outs,
        compiler_params=params(8),
        cost_estimate=product_cost(requests, len(chosen) * units, width),
        name="down",
    )(*[piece for piece, _, _ in chosen], *[in_vmem(w) for _, w, _ in chosen], *before)


def swaps_of(blocks):
    count = len(blocks)
    arrived = {k: pair_swap(blocks[k], "att", k) for k in reversed(range(1, count))}
    return [blocks[0]] + [arrived[k] for k in range(1, count)]


def exchanging_device(*args):
    return exchanging_layer(*args)


def exchanging_layer(
    hidden_state,
    queries,
    key_cache,
    value_cache,
    lengths,
    assignment,
    out_weight,
    norm_gain,
    gate_weight,
    up_weight,
    down_weight,
):
    slots, columns = hidden_state.shape
    count = lax.axis_size("att")
    parts = lax.axis_size("ffn")
    model_width = columns * parts
    heads = queries.shape[1] // lanes
    own = jnp.stack([lax.axis_index("att"), lax.axis_index("ffn")]).astype(I32)
    table = jnp.concatenate([own, lengths, assignment])
    own_queries = queries.reshape(slots, heads, lanes)
    query_blocks = swaps_of([own_queries] * count)
    keys, values = fetch(table, [(key_cache, None), (value_cache, None)], parts)
    jobs = [(out_weight.reshape(-1, columns), (0, 1, 2, 3)), (down_weight, (0, 1))]
    *blocks, project, down_near = attention(table, query_blocks, keys, values, jobs, parts)

    blocks = swaps_of(blocks)
    piece = jnp.concatenate(blocks, axis=0)
    across = pair_swap(piece, "ffn", 2)
    beside = pair_swap(piece, "ffn", 1)
    corner = pair_swap(across, "ffn", 1)
    *partial, down_far = projection(
        table, [piece, beside, across, corner], project, slots, count, [(down_weight, (2, 3))]
    )
    jobs = [(gate_weight, (0, 1, 2, 3)), (up_weight, (3,))]
    gate, up_corner = fetch(table, jobs, parts)
    middle = residual(hidden_state, swaps_of(partial), False)

    rows = swaps_of([middle] * count)
    (up,) = fetch(table, [(up_weight, (0, 1, 2))], parts)
    send, scaled, squares = hidden_first(rows, norm_gain.reshape(1, columns), gate, 3)
    arrived = pair_swap(send, "ffn", 1)
    keep = hidden_next(scaled, [(gate, 2)], F32)
    far_gate, squares = squares_sum(keep, squares, arrived)
    far_gate = pair_swap(far_gate, "ffn", 2)
    send = hidden_next(scaled, [(up_corner, 0)], BF16)
    arrived = pair_swap(send, "ffn", 1)
    keep = hidden_next(scaled, [(up, 2)], F32)
    far_up = pair_swap(chip_sum(keep, arrived), "ffn", 2)
    send = hidden_next(scaled, [(gate, 1), (up, 1)], BF16)
    arrived = pair_swap(send, "ffn", 1)
    keep = hidden_next(scaled, [(gate, 0), (up, 0)], F32)
    active = active_units(keep, arrived, far_gate, far_up, squares, model_width)

    across = pair_swap(active, "ffn", 2)
    beside = pair_swap(active, "ffn", 1)
    chosen = [(active, down_near, 0), (beside, down_near, 1)]
    (before,) = down_part(chosen, count, None, False)
    corner = pair_swap(across, "ffn", 1)
    (before,) = down_part([(across, down_far, 0)], count, before, False)
    partial = down_part([(corner, down_far, 1)], count, before, True)
    return residual(middle, swaps_of(partial), True)


def solution(mesh):
    count, parts = mesh.shape["att"], mesh.shape["ffn"]
    paired = count == 4 and parts == 4
    in_specs = (
        P(("group", "att"), "ffn"),
        P(("group", "att"), "ffn"),
        P(("group", "att"), "ffn"),
        P(("group", "att"), "ffn"),
        P(("group", "att")),
        P("group"),
        P(None, "att", "ffn"),
        P("ffn"),
        P("att", "ffn"),
        P("att", "ffn"),
        P("att", "ffn"),
    )
    out_specs = P(("group", "att"), "ffn")
    return jax.shard_map(
        exchanging_device if paired else general_device,
        mesh=mesh,
        in_specs=in_specs,
        out_specs=out_specs,
        check_vma=False,
    )
```

```python
import functools
import math

import jax
import jax.numpy as jnp
from jax import lax
from jax.experimental import pallas as pl
from jax.experimental.pallas import tpu as pltpu
from jax.sharding import PartitionSpec as P

epsilon = 1e-05
masked_score = -1e30
lanes = 128
block_rows = 256
slot_group = 2
contract_minor = (((1,), (1,)), ((), ()))
F32 = jnp.float32
BF16 = jnp.bfloat16
I32 = jnp.int32
vmem = pl.BlockSpec(memory_space=pltpu.VMEM)
smem = pl.BlockSpec(memory_space=pltpu.SMEM)
hbm = pl.BlockSpec(memory_space=pltpu.HBM)


def softmax_rounded(scores):
    row_top = jnp.max(scores, axis=-1, keepdims=True)
    shifted = jnp.exp(scores - row_top)
    totals = jnp.sum(shifted, axis=-1, keepdims=True)
    return (shifted / totals).astype(jnp.bfloat16)


def general_device(
    hidden_state,
    queries,
    key_cache,
    value_cache,
    lengths,
    assignment,
    out_weight,
    norm_gain,
    gate_weight,
    up_weight,
    down_weight,
):
    rows_dev = hidden_state.shape[0]
    columns = hidden_state.shape[1]
    att_count = lax.axis_size("att")
    ffn_count = lax.axis_size("ffn")
    requests = rows_dev * att_count
    kv_total = out_weight.shape[0]
    kv_local = kv_total // ffn_count
    model_width = columns * ffn_count
    pool_rows = key_cache.shape[0]
    head_size = key_cache.shape[1] // kv_local
    per_group = queries.shape[1] // (kv_local * head_size)
    score_scale = 1.0 / math.sqrt(head_size)
    att_place = lax.axis_index("att")
    every_query = lax.all_gather(queries, "att", axis=0, tiled=True)
    own_slots = lax.dynamic_slice_in_dim(assignment, att_place * rows_dev, rows_dev)
    slot_queries = jnp.take(every_query, own_slots, axis=0).reshape(
        rows_dev, kv_local, per_group, head_size
    )
    keys_local = key_cache.reshape(pool_rows, kv_local, head_size)
    values_local = value_cache.reshape(pool_rows, kv_local, head_size)
    slot_starts = jnp.cumsum(lengths) - lengths
    slot_ends = slot_starts + lengths
    positions = jnp.arange(pool_rows, dtype=jnp.int32)
    owned_rows = (positions[None, :] >= slot_starts[:, None]) & (
        positions[None, :] < slot_ends[:, None]
    )
    owned_rows = owned_rows[:, None, None, :]
    raw_scores = (
        jnp.einsum("rkgc,pkc->rkgp", slot_queries, keys_local, preferred_element_type=jnp.float32)
        * score_scale
    )
    weights = softmax_rounded(jnp.where(owned_rows, raw_scores, masked_score))
    attended = jnp.einsum(
        "rkgp,pkc->rkgc", weights, values_local, preferred_element_type=jnp.float32
    )
    attended = attended.astype(jnp.bfloat16).reshape(rows_dev, kv_local, per_group * head_size)
    spread = lax.all_to_all(attended, "att", split_axis=2, concat_axis=0, tiled=True)
    pieces = lax.all_gather(spread, "ffn", axis=1, tiled=True)
    inverse = (
        jnp.zeros((requests,), jnp.int32).at[assignment].set(jnp.arange(requests, dtype=jnp.int32))
    )
    request_pieces = jnp.take(pieces, inverse, axis=0)
    block = request_pieces
    projected = lax.psum_scatter(
        jnp.einsum("rkc,kcd->rd", block, out_weight, preferred_element_type=jnp.float32).astype(
            jnp.bfloat16
        ),
        "att",
        scatter_dimension=0,
        tiled=True,
    ).astype(jnp.float32)
    middle_short = (hidden_state.astype(jnp.float32) + projected).astype(jnp.bfloat16)
    middle = lax.optimization_barrier(middle_short).astype(jnp.float32)
    squares = lax.psum(jnp.sum(middle * middle, axis=1), "ffn")
    normed = (
        middle * lax.rsqrt(squares[:, None] / model_width + epsilon) * norm_gain.astype(jnp.float32)
    ).astype(jnp.bfloat16)
    every_row = lax.all_gather(normed, "att", axis=0, tiled=True)
    contract = (((1,), (1,)), ((), ()))
    gate_part = lax.dot_general(
        gate_weight, every_row, contract, preferred_element_type=jnp.float32
    )
    up_part = lax.dot_general(up_weight, every_row, contract, preferred_element_type=jnp.float32)
    totals = lax.psum(
        jnp.concatenate([gate_part, up_part], axis=1).astype(jnp.bfloat16), "ffn"
    ).astype(jnp.float32)
    unit_active = (jax.nn.silu(totals[:, :requests]) * totals[:, requests:]).astype(jnp.bfloat16)
    block = unit_active
    returned = lax.psum_scatter(
        lax.dot_general(
            block, down_weight, (((0,), (0,)), ((), ())), preferred_element_type=jnp.float32
        ).astype(jnp.bfloat16),
        "att",
        scatter_dimension=0,
        tiled=True,
    ).astype(jnp.float32)
    return (middle + returned).astype(jnp.bfloat16)


def pair_swap(value, axis, bit):
    count = lax.axis_size(axis)
    return lax.ppermute(value, axis, [(i, i ^ bit) for i in range(count)])


def up_to(value, multiple):
    return -(-value // multiple) * multiple


def params(megabytes):
    return pltpu.CompilerParams(vmem_limit_bytes=megabytes << 20)


def halves_joined(block):
    block = block.astype(F32)
    rows = block.shape[0] // 2
    return jnp.concatenate([block[:rows], block[rows:]], axis=1)


def halves_stacked(block):
    half = block.shape[1] // 2
    return jnp.concatenate([block[:, :half], block[:, half:]], axis=0)


def high_low(value):
    high = value.astype(BF16).astype(F32)
    low = value - high
    lane = lax.broadcasted_iota(I32, (value.shape[0], lanes), 1)
    return jnp.where(lane < lanes // 2, high, low)


def in_hbm(value):
    return pltpu.with_memory_space_constraint(value, pltpu.HBM)


def in_vmem(value):
    return pltpu.with_memory_space_constraint(value, pltpu.VMEM)


def job_shapes(jobs, parts):
    shapes = []
    for array, masks in jobs:
        if masks is None:
            shapes.append(pltpu.VMEM(array.shape, array.dtype))
        else:
            rows, width = array.shape
            shapes.append(pltpu.VMEM((len(masks), rows // parts, width), array.dtype))
    return shapes


def job_count(jobs):
    return sum(1 if masks is None else len(masks) for _, masks in jobs)


def job_copies(own, masks_of, sources, targets, sems):
    copies = []
    for masks, source, target in zip(masks_of, sources, targets):
        if masks is None:
            copies.append(pltpu.make_async_copy(source, target, sems.at[len(copies)]))
            continue
        rows = target.shape[1]
        for m, mask in enumerate(masks):
            at = pl.ds(pl.multiple_of((own ^ mask) * rows, rows), rows)
            copies.append(
                pltpu.make_async_copy(source.at[at], target.at[m], sems.at[len(copies)])
            )
    return copies


def masks_in(jobs):
    return tuple(masks for _, masks in jobs)


def fetch_kernel(*refs, masks_of, placed):
    own = refs[0][1] if placed else None
    refs = refs[1:] if placed else refs
    count = len(masks_of)
    copies = job_copies(own, masks_of, refs[:count], refs[count:-1], refs[-1])
    for copy in copies:
        copy.start()
    for copy in copies:
        copy.wait()


def fetch(table, jobs, parts):
    shapes = job_shapes(jobs, parts)
    placed = any(masks is not None for _, masks in jobs)
    moved = sum(2 * math.prod(shape.shape) for shape in shapes)
    return pl.pallas_call(
        functools.partial(fetch_kernel, masks_of=masks_in(jobs), placed=placed),
        in_specs=([smem] if placed else []) + [hbm] * len(jobs),
        out_specs=[vmem] * len(jobs),
        out_shape=shapes,
        scratch_shapes=[pltpu.SemaphoreType.DMA((job_count(jobs),))],
        compiler_params=params(1),
        cost_estimate=pl.CostEstimate(flops=0, bytes_accessed=2 * moved, transcendentals=0),
        name="fetch",
    )(*([table] if placed else []), *[in_hbm(array) for array, _ in jobs])


def folded(combine, value):
    parts = [value[:, i : i + lanes] for i in range(0, value.shape[1], lanes)]
    return functools.reduce(combine, parts)


def attention_kernel(table, *refs, slots, count, scale, unroll, masks_of):
    jobs = len(masks_of)
    query_blocks, (keys, values), sources = (
        refs[:count],
        refs[count : count + 2],
        refs[count + 2 : count + 2 + jobs],
    )
    outs, targets = (
        refs[count + 2 + jobs : 2 * count + 2 + jobs],
        refs[2 * count + 2 + jobs : 2 * count + 2 + 2 * jobs],
    )
    queries, both, begins, ends, tops, sums, scores, total, attended, items, sems = refs[
        2 * count + 2 + 2 * jobs :
    ]
    copies = job_copies(table[1], masks_of, sources, targets, sems)
    for copy in copies:
        copy.start()
    pool, width = keys.shape
    heads = queries.shape[1]
    half = heads // 2
    own = table[0]
    group_rows = slot_group * heads
    top_half = lax.broadcasted_iota(I32, (heads, lanes), 0) < half
    for k in range(count):
        queries[k * slots : (k + 1) * slots] = query_blocks[k][...]

    tops[...] = jnp.full(tops.shape, masked_score, F32)
    sums[...] = jnp.zeros(sums.shape, F32)
    total[...] = jnp.zeros(total.shape, F32)
    spare = slots * heads
    both[spare:, :] = jnp.zeros((both.shape[0] - spare, width), BF16)
    begins[spare:, :] = jnp.full((begins.shape[0] - spare, lanes), pool, I32)
    ends[spare:, :] = jnp.zeros((ends.shape[0] - spare, lanes), I32)

    def slot(s, carry):
        start, made, last_block, last_slot = carry
        end = start + table[2 + s]
        request = table[2 + slots + own * slots + s]
        owner = sum((request >= k * slots).astype(I32) for k in range(1, count))
        query = queries[(owner ^ own) * slots + request - owner * slots]
        zero = jnp.zeros_like(query)
        at = pl.ds(pl.multiple_of(s * heads, heads), heads)
        both[at, :lanes] = jnp.where(top_half, query, zero)
        both[at, lanes:] = jnp.where(top_half, zero, query)
        begins[at, :] = jnp.full((heads, lanes), start, I32)
        ends[at, :] = jnp.full((heads, lanes), end, I32)
        first = start // block_rows
        covered = (first == last_block) & (s < last_slot + slot_group)
        first = jnp.where(covered, first + 1, first)
        last = (end - 1) // block_rows

        def item(block, made):
            items[2 * made] = block
            items[2 * made + 1] = s
            return made + 1

        made_now = lax.fori_loop(first, last + 1, item, made)
        new = made_now > made
        return (
            end,
            made_now,
            jnp.where(new, last, last_block),
            jnp.where(new, s, last_slot),
        )

    none = jnp.int32(-1)
    _, made, _, _ = lax.fori_loop(0, slots, slot, (jnp.int32(0), jnp.int32(0), none, none))
    for u in range(unroll):
        items[2 * (made + u)] = 0
        items[2 * (made + u) + 1] = slots
    steps = (made + unroll - 1) // unroll
    across = lax.broadcasted_iota(I32, (group_rows, block_rows), 1)

    def place_of(i):
        block = pl.multiple_of(items[2 * i] * block_rows, block_rows)
        rows = pl.multiple_of(items[2 * i + 1] * heads, heads)
        return block, pl.ds(block, block_rows), pl.ds(rows, group_rows)

    def score_step(step, carry):
        for u in range(unroll):
            i = step * unroll + u
            block, cache, rows = place_of(i)
            raw = lax.dot_general(
                both[rows, :], keys[cache, :], contract_minor, preferred_element_type=F32
            )
            position = block + across
            begin, end = (jnp.concatenate([b[rows, :]] * (block_rows // lanes), axis=1) for b in (begins, ends))
            inside = (position >= begin) & (position < end)
            masked = jnp.where(inside, raw * scale, masked_score)
            scores[i] = masked
            tops[rows, :] = jnp.maximum(tops[rows, :], folded(jnp.maximum, masked))
        return carry

    def value_step(step, carry):
        for u in range(unroll):
            i = step * unroll + u
            _, cache, rows = place_of(i)
            top = tops[rows, :]
            shifted = jnp.exp(scores[i] - jnp.concatenate([top] * (block_rows // lanes), axis=1))
            sums[rows, :] += folded(jnp.add, shifted)
            total[rows, :] += jnp.dot(
                shifted.astype(BF16), values[cache, :], preferred_element_type=F32
            )
        return carry

    lax.fori_loop(0, steps, score_step, 0)
    top = jnp.max(tops[...], axis=1, keepdims=True)
    tops[...] = jnp.broadcast_to(top, tops.shape)
    lax.fori_loop(0, steps, value_step, 0)

    real = slots * heads
    row = lax.broadcasted_iota(I32, (real, lanes), 0)
    upper = row % heads < half
    picked = jnp.where(upper, total[:real, :lanes], total[:real, lanes:])
    attended[...] = picked / jnp.sum(sums[:real, :], axis=1, keepdims=True)
    per_block = half // count
    for k in range(count):
        outs[k][...] = jnp.zeros(outs[k].shape, BF16)
        for kv in range(2):
            for j in range(per_block):
                head = kv * half + (own ^ k) * per_block + j
                at = (kv * per_block + j) * lanes
                outs[k][:slots, at : at + lanes] = attended[
                    pl.ds(head, slots, stride=heads), :
                ].astype(BF16)
    for copy in copies:
        copy.wait()


def attention(table, query_blocks, keys, values, jobs, parts, unroll=8):
    count = len(query_blocks)
    slots, heads, _ = query_blocks[0].shape
    pool, width = keys.shape
    most = pool // block_rows + slots + unroll
    rows = (slots + slot_group) * heads
    return pl.pallas_call(
        functools.partial(
            attention_kernel,
            slots=slots,
            count=count,
            scale=1.0 / math.sqrt(lanes),
            unroll=unroll,
            masks_of=masks_in(jobs),
        ),
        in_specs=[smem] + [vmem] * (count + 2) + [hbm] * len(jobs),
        out_specs=[vmem] * (count + len(jobs)),
        out_shape=[jax.ShapeDtypeStruct((up_to(slots, 8), heads // count * lanes), BF16)] * count
        + job_shapes(jobs, parts),
        scratch_shapes=[
            pltpu.VMEM((count * slots, heads, lanes), BF16),
            pltpu.VMEM((rows, width), BF16),
            pltpu.VMEM((rows, lanes), I32),
            pltpu.VMEM((rows, lanes), I32),
            pltpu.VMEM((rows, lanes), F32),
            pltpu.VMEM((rows, lanes), F32),
            pltpu.VMEM((most, slot_group * heads, block_rows), F32),
            pltpu.VMEM((rows, width), F32),
            pltpu.VMEM((slots * heads, lanes), F32),
            pltpu.SMEM((2 * most,), I32),
            pltpu.SemaphoreType.DMA((job_count(jobs),)),
        ],
        compiler_params=params(12),
        cost_estimate=pl.CostEstimate(
            flops=4 * pool * heads * lanes, bytes_accessed=pool * width * 4, transcendentals=0
        ),
        name="attention",
    )(
        table,
        *query_blocks,
        in_vmem(keys),
        in_vmem(values),
        *[in_hbm(array) for array, _ in jobs],
    )


def projection_kernel(table, *refs, slots, count, parts):
    pieces, weight, outs = refs[:parts], refs[parts], refs[parts + 1 :]
    own_att = table[0]
    requests = slots * count
    padded = pieces[0].shape[0] // count
    row = lax.broadcasted_iota(I32, (requests, padded), 0)
    wanted = row
    for k in range(count):
        moved = row + ((own_att ^ k) - k) * slots
        wanted = jnp.where((row >= k * slots) & (row < (k + 1) * slots), moved, wanted)
    choose = []
    lane = lax.broadcasted_iota(I32, (1, padded), 1)
    for k in range(count):
        served = jnp.full((1, padded), -1, I32)
        for i in range(slots):
            request = table[2 + slots + (own_att ^ k) * slots + i]
            served = jnp.where(lane == i, request, served)
        choose.append((wanted == served).astype(F32).astype(BF16))
    total = None
    for p in range(parts):
        rows = None
        for k in range(count):
            term = jnp.dot(
                choose[k],
                pieces[p][k * padded : (k + 1) * padded, :],
                preferred_element_type=F32,
            )
            rows = term if rows is None else rows + term
        term = jnp.dot(rows.astype(BF16), weight[p], preferred_element_type=F32)
        total = term if total is None else total + term
    for k in range(count):
        outs[k][...] = halves_stacked(total[k * slots : (k + 1) * slots]).astype(BF16)


def projection(table, pieces, weight, slots, count):
    parts, depth, width = weight.shape
    return pl.pallas_call(
        functools.partial(projection_kernel, slots=slots, count=count, parts=parts),
        in_specs=[smem] + [vmem] * (1 + parts),
        out_specs=[vmem] * count,
        out_shape=[jax.ShapeDtypeStruct((2 * slots, width // 2), BF16)] * count,
        compiler_params=params(8),
        cost_estimate=pl.CostEstimate(
            flops=2 * slots * count * parts * depth * width,
            bytes_accessed=parts * depth * width,
            transcendentals=0,
        ),
        name="projection",
    )(table, *pieces, in_vmem(weight))


def residual_kernel(*refs, joined):
    base, blocks, out = refs[0], refs[1:-1], refs[-1]
    total = base[...].astype(F32)
    if not joined:
        total = halves_stacked(total)
    for block in blocks:
        total = total + block[...].astype(F32)
    out[...] = (halves_joined(total) if joined else total).astype(BF16)


def residual(base, blocks, joined):
    rows, half = blocks[0].shape
    shape = (rows // 2, 2 * half) if joined else (rows, half)
    return pl.pallas_call(
        functools.partial(residual_kernel, joined=joined),
        in_specs=[vmem] * (1 + len(blocks)),
        out_specs=vmem,
        out_shape=jax.ShapeDtypeStruct(shape, BF16),
        compiler_params=params(2),
        name="residual",
    )(base, *blocks)


def unit_product(scaled, weight, part):
    return lax.dot_general(scaled, weight[part], contract_minor, preferred_element_type=F32)


def product_cost(requests, units, width):
    return pl.CostEstimate(
        flops=2 * requests * units * width, bytes_accessed=units * width, transcendentals=0
    )


def hidden_first_kernel(*refs, count, part):
    blocks, (gain, weight, send, scaled, squares, joined) = refs[:count], refs[count:]
    rows = blocks[0].shape[0] // 2
    for k in range(count):
        joined[k * rows : (k + 1) * rows, :] = halves_joined(blocks[k][...])
    middle = joined[...]
    square = jnp.sum(middle * middle, axis=1, keepdims=True)
    scaled[...] = (middle * gain[...].astype(F32)).astype(BF16)
    units = weight.shape[1]
    send[:, :units] = unit_product(scaled[...], weight, part).astype(BF16)
    send[:, units:] = high_low(square).astype(BF16)
    squares[...] = jnp.broadcast_to(square, squares.shape)


def hidden_first(blocks, gain, weight, part):
    count = len(blocks)
    rows, half = blocks[0].shape
    requests, width = rows // 2 * count, 2 * half
    units = weight.shape[1]
    return pl.pallas_call(
        functools.partial(hidden_first_kernel, count=count, part=part),
        in_specs=[vmem] * (count + 2),
        out_specs=[vmem] * 3,
        out_shape=[
            jax.ShapeDtypeStruct((requests, units + lanes), BF16),
            jax.ShapeDtypeStruct((requests, width), BF16),
            jax.ShapeDtypeStruct((requests, lanes), F32),
        ],
        scratch_shapes=[pltpu.VMEM((requests, width), F32)],
        compiler_params=params(6),
        cost_estimate=product_cost(requests, units, width),
        name="hidden_first",
    )(*blocks, gain, in_vmem(weight))


def hidden_kernel(scaled, *refs, parts):
    weights, out = refs[:-1], refs[-1]
    for t, (weight, part) in enumerate(zip(weights, parts)):
        units = weight.shape[1]
        out[:, t * units : (t + 1) * units] = unit_product(scaled[...], weight, part).astype(
            out.dtype
        )


def hidden_next(scaled, chosen, kind):
    requests, width = scaled.shape
    units = chosen[0][0].shape[1]
    return pl.pallas_call(
        functools.partial(hidden_kernel, parts=tuple(part for _, part in chosen)),
        in_specs=[vmem] * (1 + len(chosen)),
        out_specs=vmem,
        out_shape=jax.ShapeDtypeStruct((requests, len(chosen) * units), kind),
        compiler_params=params(6),
        cost_estimate=product_cost(requests, len(chosen) * units, width),
        name="hidden_next",
    )(scaled, *[in_vmem(weight) for weight, _ in chosen])


def squares_sum_kernel(keep, own_squares, arrived, out, squares):
    width = keep.shape[1]
    out[:, :width] = (keep[...] + arrived[:, :width].astype(F32)).astype(BF16)
    tail = arrived[:, width:].astype(F32)
    chip = own_squares[...] + (tail[:, :1] + tail[:, lanes // 2 : lanes // 2 + 1])
    squares[...] = chip
    out[:, width:] = high_low(chip).astype(BF16)


def squares_sum(keep, own_squares, arrived):
    requests, width = arrived.shape
    return pl.pallas_call(
        squares_sum_kernel,
        in_specs=[vmem] * 3,
        out_specs=[vmem] * 2,
        out_shape=[
            jax.ShapeDtypeStruct((requests, width), BF16),
            jax.ShapeDtypeStruct((requests, lanes), F32),
        ],
        compiler_params=params(2),
        name="squares_sum",
    )(keep, own_squares, arrived)


def chip_sum_kernel(keep, arrived, out):
    out[...] = (keep[...] + arrived[...].astype(F32)).astype(BF16)


def chip_sum(keep, arrived):
    return pl.pallas_call(
        chip_sum_kernel,
        in_specs=[vmem] * 2,
        out_specs=vmem,
        out_shape=jax.ShapeDtypeStruct(arrived.shape, BF16),
        compiler_params=params(2),
        name="chip_sum",
    )(keep, arrived)


def active_kernel(near, beside, far_gate, far_up, squares, out, *, model_width):
    units = far_up.shape[1]
    tail = far_gate[:, units:].astype(F32)
    square = squares[:, :1] + (tail[:, :1] + tail[:, lanes // 2 : lanes // 2 + 1])
    scale = lax.rsqrt(square / model_width + epsilon)

    def total(at, far):
        both = near[:, at : at + units] + beside[:, at : at + units].astype(F32)
        return (both + far.astype(F32)) * scale

    gate = total(0, far_gate[:, :units])
    out[...] = (gate / (1.0 + jnp.exp(-gate)) * total(units, far_up[...])).astype(BF16)


def active_units(near, beside, far_gate, far_up, squares, model_width):
    requests, width = near.shape
    return pl.pallas_call(
        functools.partial(active_kernel, model_width=model_width),
        in_specs=[vmem] * 5,
        out_specs=vmem,
        out_shape=jax.ShapeDtypeStruct((requests, width // 2), BF16),
        compiler_params=params(4),
        name="active",
    )(near, beside, far_gate, far_up, squares)


def down_kernel(*refs, parts, count, first, last):
    terms = len(parts)
    pieces, weights, rest = refs[:terms], refs[terms : 2 * terms], refs[2 * terms :]
    total = None if first else rest[0][...]
    outs = rest if first else rest[1:]
    for piece, weight, part in zip(pieces, weights, parts):
        term = jnp.dot(piece[...], weight[part], preferred_element_type=F32)
        total = term if total is None else total + term
    if last:
        rows = total.shape[0] // count
        for k in range(count):
            outs[k][...] = halves_stacked(total[k * rows : (k + 1) * rows]).astype(BF16)
    else:
        outs[0][...] = total


def down_part(chosen, count, before, last):
    requests, units = chosen[0][0].shape
    width = chosen[0][1].shape[2]
    if last:
        outs = [jax.ShapeDtypeStruct((2 * requests // count, width // 2), BF16)] * count
    else:
        outs = [jax.ShapeDtypeStruct((requests, width), F32)]
    before = [] if before is None else [before]
    return pl.pallas_call(
        functools.partial(
            down_kernel,
            parts=tuple(part for _, _, part in chosen),
            count=count,
            first=not before,
            last=last,
        ),
        in_specs=[vmem] * (2 * len(chosen) + len(before)),
        out_specs=[vmem] * len(outs),
        out_shape=outs,
        compiler_params=params(8),
        cost_estimate=product_cost(requests, len(chosen) * units, width),
        name="down",
    )(*[piece for piece, _, _ in chosen], *[in_vmem(w) for _, w, _ in chosen], *before)


def swaps_of(blocks):
    count = len(blocks)
    arrived = {k: pair_swap(blocks[k], "att", k) for k in reversed(range(1, count))}
    return [blocks[0]] + [arrived[k] for k in range(1, count)]


def exchanging_device(*args):
    return exchanging_layer(*args)


def exchanging_layer(
    hidden_state,
    queries,
    key_cache,
    value_cache,
    lengths,
    assignment,
    out_weight,
    norm_gain,
    gate_weight,
    up_weight,
    down_weight,
):
    slots, columns = hidden_state.shape
    count = lax.axis_size("att")
    parts = lax.axis_size("ffn")
    model_width = columns * parts
    heads = queries.shape[1] // lanes
    own = jnp.stack([lax.axis_index("att"), lax.axis_index("ffn")]).astype(I32)
    table = jnp.concatenate([own, lengths, assignment])
    own_queries = queries.reshape(slots, heads, lanes)
    query_blocks = swaps_of([own_queries] * count)
    keys, values = fetch(table, [(key_cache, None), (value_cache, None)], parts)
    jobs = [(out_weight.reshape(-1, columns), (0, 1, 2, 3)), (down_weight, (0, 1))]
    *blocks, project, down_near = attention(table, query_blocks, keys, values, jobs, parts)

    blocks = swaps_of(blocks)
    (down_across,) = fetch(table, [(down_weight, (2,))], parts)
    piece = jnp.concatenate(blocks, axis=0)
    across = pair_swap(piece, "ffn", 2)
    beside = pair_swap(piece, "ffn", 1)
    corner = pair_swap(across, "ffn", 1)
    (down_corner,) = fetch(table, [(down_weight, (3,))], parts)
    gain = norm_gain.reshape(1, columns)
    partial = projection(table, [piece, beside, across, corner], project, slots, count)
    jobs = [(gate_weight, (0, 1, 2, 3)), (up_weight, (3,))]
    gate, up_corner = fetch(table, jobs, parts)
    middle = residual(hidden_state, swaps_of(partial), False)

    rows = swaps_of([middle] * count)
    (up,) = fetch(table, [(up_weight, (0, 1, 2))], parts)
    send, scaled, squares = hidden_first(rows, gain, gate, 3)
    arrived = pair_swap(send, "ffn", 1)
    keep = hidden_next(scaled, [(gate, 2)], F32)
    far_gate, squares = squares_sum(keep, squares, arrived)
    far_gate = pair_swap(far_gate, "ffn", 2)
    send = hidden_next(scaled, [(up_corner, 0)], BF16)
    arrived = pair_swap(send, "ffn", 1)
    keep = hidden_next(scaled, [(up, 2)], F32)
    far_up = pair_swap(chip_sum(keep, arrived), "ffn", 2)
    send = hidden_next(scaled, [(gate, 1), (up, 1)], BF16)
    arrived = pair_swap(send, "ffn", 1)
    keep = hidden_next(scaled, [(gate, 0), (up, 0)], F32)
    active = active_units(keep, arrived, far_gate, far_up, squares, model_width)

    across = pair_swap(active, "ffn", 2)
    beside = pair_swap(active, "ffn", 1)
    chosen = [(active, down_near, 0), (beside, down_near, 1)]
    (before,) = down_part(chosen, count, None, False)
    corner = pair_swap(across, "ffn", 1)
    (before,) = down_part([(across, down_across, 0)], count, before, False)
    partial = down_part([(corner, down_corner, 0)], count, before, True)
    return residual(middle, swaps_of(partial), True)


def solution(mesh):
    count, parts = mesh.shape["att"], mesh.shape["ffn"]
    paired = count == 4 and parts == 4
    in_specs = (
        P(("group", "att"), "ffn"),
        P(("group", "att"), "ffn"),
        P(("group", "att"), "ffn"),
        P(("group", "att"), "ffn"),
        P(("group", "att")),
        P("group"),
        P(None, "att", "ffn"),
        P("ffn"),
        P("att", "ffn"),
        P("att", "ffn"),
        P("att", "ffn"),
    )
    out_specs = P(("group", "att"), "ffn")
    return jax.shard_map(
        exchanging_device if paired else general_device,
        mesh=mesh,
        in_specs=in_specs,
        out_specs=out_specs,
        check_vma=False,
    )
```

```python
import functools
import math

import jax
import jax.numpy as jnp
from jax import lax
from jax.experimental import pallas as pl
from jax.experimental.pallas import tpu as pltpu
from jax.sharding import PartitionSpec as P

epsilon = 1e-05
masked_score = -1e30
lanes = 128
block_rows = 256
slot_group = 2
contract_minor = (((1,), (1,)), ((), ()))
F32 = jnp.float32
BF16 = jnp.bfloat16
I32 = jnp.int32
vmem = pl.BlockSpec(memory_space=pltpu.VMEM)
smem = pl.BlockSpec(memory_space=pltpu.SMEM)
hbm = pl.BlockSpec(memory_space=pltpu.HBM)


def softmax_rounded(scores):
    row_top = jnp.max(scores, axis=-1, keepdims=True)
    shifted = jnp.exp(scores - row_top)
    totals = jnp.sum(shifted, axis=-1, keepdims=True)
    return (shifted / totals).astype(jnp.bfloat16)


def general_device(
    hidden_state,
    queries,
    key_cache,
    value_cache,
    lengths,
    assignment,
    out_weight,
    norm_gain,
    gate_weight,
    up_weight,
    down_weight,
):
    rows_dev = hidden_state.shape[0]
    columns = hidden_state.shape[1]
    att_count = lax.axis_size("att")
    ffn_count = lax.axis_size("ffn")
    requests = rows_dev * att_count
    kv_total = out_weight.shape[0]
    kv_local = kv_total // ffn_count
    model_width = columns * ffn_count
    pool_rows = key_cache.shape[0]
    head_size = key_cache.shape[1] // kv_local
    per_group = queries.shape[1] // (kv_local * head_size)
    score_scale = 1.0 / math.sqrt(head_size)
    att_place = lax.axis_index("att")
    every_query = lax.all_gather(queries, "att", axis=0, tiled=True)
    own_slots = lax.dynamic_slice_in_dim(assignment, att_place * rows_dev, rows_dev)
    slot_queries = jnp.take(every_query, own_slots, axis=0).reshape(
        rows_dev, kv_local, per_group, head_size
    )
    keys_local = key_cache.reshape(pool_rows, kv_local, head_size)
    values_local = value_cache.reshape(pool_rows, kv_local, head_size)
    slot_starts = jnp.cumsum(lengths) - lengths
    slot_ends = slot_starts + lengths
    positions = jnp.arange(pool_rows, dtype=jnp.int32)
    owned_rows = (positions[None, :] >= slot_starts[:, None]) & (
        positions[None, :] < slot_ends[:, None]
    )
    owned_rows = owned_rows[:, None, None, :]
    raw_scores = (
        jnp.einsum("rkgc,pkc->rkgp", slot_queries, keys_local, preferred_element_type=jnp.float32)
        * score_scale
    )
    weights = softmax_rounded(jnp.where(owned_rows, raw_scores, masked_score))
    attended = jnp.einsum(
        "rkgp,pkc->rkgc", weights, values_local, preferred_element_type=jnp.float32
    )
    attended = attended.astype(jnp.bfloat16).reshape(rows_dev, kv_local, per_group * head_size)
    spread = lax.all_to_all(attended, "att", split_axis=2, concat_axis=0, tiled=True)
    pieces = lax.all_gather(spread, "ffn", axis=1, tiled=True)
    inverse = (
        jnp.zeros((requests,), jnp.int32).at[assignment].set(jnp.arange(requests, dtype=jnp.int32))
    )
    request_pieces = jnp.take(pieces, inverse, axis=0)
    block = request_pieces
    projected = lax.psum_scatter(
        jnp.einsum("rkc,kcd->rd", block, out_weight, preferred_element_type=jnp.float32).astype(
            jnp.bfloat16
        ),
        "att",
        scatter_dimension=0,
        tiled=True,
    ).astype(jnp.float32)
    middle_short = (hidden_state.astype(jnp.float32) + projected).astype(jnp.bfloat16)
    middle = lax.optimization_barrier(middle_short).astype(jnp.float32)
    squares = lax.psum(jnp.sum(middle * middle, axis=1), "ffn")
    normed = (
        middle * lax.rsqrt(squares[:, None] / model_width + epsilon) * norm_gain.astype(jnp.float32)
    ).astype(jnp.bfloat16)
    every_row = lax.all_gather(normed, "att", axis=0, tiled=True)
    contract = (((1,), (1,)), ((), ()))
    gate_part = lax.dot_general(
        gate_weight, every_row, contract, preferred_element_type=jnp.float32
    )
    up_part = lax.dot_general(up_weight, every_row, contract, preferred_element_type=jnp.float32)
    totals = lax.psum(
        jnp.concatenate([gate_part, up_part], axis=1).astype(jnp.bfloat16), "ffn"
    ).astype(jnp.float32)
    unit_active = (jax.nn.silu(totals[:, :requests]) * totals[:, requests:]).astype(jnp.bfloat16)
    block = unit_active
    returned = lax.psum_scatter(
        lax.dot_general(
            block, down_weight, (((0,), (0,)), ((), ())), preferred_element_type=jnp.float32
        ).astype(jnp.bfloat16),
        "att",
        scatter_dimension=0,
        tiled=True,
    ).astype(jnp.float32)
    return (middle + returned).astype(jnp.bfloat16)


def pair_swap(value, axis, bit):
    count = lax.axis_size(axis)
    return lax.ppermute(value, axis, [(i, i ^ bit) for i in range(count)])


def up_to(value, multiple):
    return -(-value // multiple) * multiple


def params(megabytes):
    return pltpu.CompilerParams(vmem_limit_bytes=megabytes << 20)


def halves_joined(block):
    block = block.astype(F32)
    rows = block.shape[0] // 2
    return jnp.concatenate([block[:rows], block[rows:]], axis=1)


def halves_stacked(block):
    half = block.shape[1] // 2
    return jnp.concatenate([block[:, :half], block[:, half:]], axis=0)


def high_low(value):
    high = value.astype(BF16).astype(F32)
    low = value - high
    lane = lax.broadcasted_iota(I32, (value.shape[0], lanes), 1)
    return jnp.where(lane < lanes // 2, high, low)


def in_hbm(value):
    return pltpu.with_memory_space_constraint(value, pltpu.HBM)


def in_vmem(value):
    return pltpu.with_memory_space_constraint(value, pltpu.VMEM)


def job_shapes(jobs, parts):
    shapes = []
    for array, masks in jobs:
        if masks is None:
            shapes.append(pltpu.VMEM(array.shape, array.dtype))
        else:
            rows, width = array.shape
            shapes.append(pltpu.VMEM((len(masks), rows // parts, width), array.dtype))
    return shapes


def job_count(jobs):
    return sum(1 if masks is None else len(masks) for _, masks in jobs)


def job_copies(own, masks_of, sources, targets, sems):
    copies = []
    for masks, source, target in zip(masks_of, sources, targets):
        if masks is None:
            copies.append(pltpu.make_async_copy(source, target, sems.at[len(copies)]))
            continue
        rows = target.shape[1]
        for m, mask in enumerate(masks):
            at = pl.ds(pl.multiple_of((own ^ mask) * rows, rows), rows)
            copies.append(
                pltpu.make_async_copy(source.at[at], target.at[m], sems.at[len(copies)])
            )
    return copies


def masks_in(jobs):
    return tuple(masks for _, masks in jobs)


def fetch_kernel(*refs, masks_of, placed):
    own = refs[0][1] if placed else None
    refs = refs[1:] if placed else refs
    count = len(masks_of)
    copies = job_copies(own, masks_of, refs[:count], refs[count:-1], refs[-1])
    for copy in copies:
        copy.start()
    for copy in copies:
        copy.wait()


def fetch(table, jobs, parts):
    shapes = job_shapes(jobs, parts)
    placed = any(masks is not None for _, masks in jobs)
    moved = sum(2 * math.prod(shape.shape) for shape in shapes)
    return pl.pallas_call(
        functools.partial(fetch_kernel, masks_of=masks_in(jobs), placed=placed),
        in_specs=([smem] if placed else []) + [hbm] * len(jobs),
        out_specs=[vmem] * len(jobs),
        out_shape=shapes,
        scratch_shapes=[pltpu.SemaphoreType.DMA((job_count(jobs),))],
        compiler_params=params(1),
        cost_estimate=pl.CostEstimate(flops=0, bytes_accessed=2 * moved, transcendentals=0),
        name="fetch",
    )(*([table] if placed else []), *[in_hbm(array) for array, _ in jobs])


def folded(combine, value):
    parts = [value[:, i : i + lanes] for i in range(0, value.shape[1], lanes)]
    return functools.reduce(combine, parts)


def attention_kernel(table, *refs, slots, count, scale, unroll, masks_of):
    jobs = len(masks_of)
    query_blocks, (keys, values), sources = (
        refs[:count],
        refs[count : count + 2],
        refs[count + 2 : count + 2 + jobs],
    )
    outs, targets = (
        refs[count + 2 + jobs : 2 * count + 2 + jobs],
        refs[2 * count + 2 + jobs : 2 * count + 2 + 2 * jobs],
    )
    queries, both, begins, ends, tops, sums, scores, total, attended, items, sems = refs[
        2 * count + 2 + 2 * jobs :
    ]
    copies = job_copies(table[1], masks_of, sources, targets, sems)
    for copy in copies:
        copy.start()
    pool, width = keys.shape
    heads = queries.shape[1]
    half = heads // 2
    own = table[0]
    group_rows = slot_group * heads
    top_half = lax.broadcasted_iota(I32, (heads, lanes), 0) < half
    for k in range(count):
        queries[k * slots : (k + 1) * slots] = query_blocks[k][...]

    tops[...] = jnp.full(tops.shape, masked_score, F32)
    sums[...] = jnp.zeros(sums.shape, F32)
    total[...] = jnp.zeros(total.shape, F32)
    spare = slots * heads
    both[spare:, :] = jnp.zeros((both.shape[0] - spare, width), BF16)
    begins[spare:, :] = jnp.full((begins.shape[0] - spare, lanes), pool, I32)
    ends[spare:, :] = jnp.zeros((ends.shape[0] - spare, lanes), I32)

    def slot(s, carry):
        start, made, last_block, last_slot = carry
        end = start + table[2 + s]
        request = table[2 + slots + own * slots + s]
        owner = sum((request >= k * slots).astype(I32) for k in range(1, count))
        query = queries[(owner ^ own) * slots + request - owner * slots]
        zero = jnp.zeros_like(query)
        at = pl.ds(pl.multiple_of(s * heads, heads), heads)
        both[at, :lanes] = jnp.where(top_half, query, zero)
        both[at, lanes:] = jnp.where(top_half, zero, query)
        begins[at, :] = jnp.full((heads, lanes), start, I32)
        ends[at, :] = jnp.full((heads, lanes), end, I32)
        first = start // block_rows
        covered = (first == last_block) & (s < last_slot + slot_group)
        first = jnp.where(covered, first + 1, first)
        last = (end - 1) // block_rows

        def item(block, made):
            items[2 * made] = block
            items[2 * made + 1] = s
            return made + 1

        made_now = lax.fori_loop(first, last + 1, item, made)
        new = made_now > made
        return (
            end,
            made_now,
            jnp.where(new, last, last_block),
            jnp.where(new, s, last_slot),
        )

    none = jnp.int32(-1)
    _, made, _, _ = lax.fori_loop(0, slots, slot, (jnp.int32(0), jnp.int32(0), none, none))
    for u in range(unroll):
        items[2 * (made + u)] = 0
        items[2 * (made + u) + 1] = slots
    steps = (made + unroll - 1) // unroll
    across = lax.broadcasted_iota(I32, (group_rows, block_rows), 1)

    def place_of(i):
        block = pl.multiple_of(items[2 * i] * block_rows, block_rows)
        rows = pl.multiple_of(items[2 * i + 1] * heads, heads)
        return block, pl.ds(block, block_rows), pl.ds(rows, group_rows)

    def score_step(step, carry):
        for u in range(unroll):
            i = step * unroll + u
            block, cache, rows = place_of(i)
            raw = lax.dot_general(
                both[rows, :], keys[cache, :], contract_minor, preferred_element_type=F32
            )
            position = block + across
            begin, end = (jnp.concatenate([b[rows, :]] * (block_rows // lanes), axis=1) for b in (begins, ends))
            inside = (position >= begin) & (position < end)
            masked = jnp.where(inside, raw * scale, masked_score)
            scores[i] = masked
            tops[rows, :] = jnp.maximum(tops[rows, :], folded(jnp.maximum, masked))
        return carry

    def value_step(step, carry):
        for u in range(unroll):
            i = step * unroll + u
            _, cache, rows = place_of(i)
            top = tops[rows, :]
            shifted = jnp.exp(scores[i] - jnp.concatenate([top] * (block_rows // lanes), axis=1))
            sums[rows, :] += folded(jnp.add, shifted)
            total[rows, :] += jnp.dot(
                shifted.astype(BF16), values[cache, :], preferred_element_type=F32
            )
        return carry

    lax.fori_loop(0, steps, score_step, 0)
    top = jnp.max(tops[...], axis=1, keepdims=True)
    tops[...] = jnp.broadcast_to(top, tops.shape)
    lax.fori_loop(0, steps, value_step, 0)

    real = slots * heads
    row = lax.broadcasted_iota(I32, (real, lanes), 0)
    upper = row % heads < half
    picked = jnp.where(upper, total[:real, :lanes], total[:real, lanes:])
    attended[...] = picked / jnp.sum(sums[:real, :], axis=1, keepdims=True)
    per_block = half // count
    for k in range(count):
        outs[k][...] = jnp.zeros(outs[k].shape, BF16)
        for kv in range(2):
            for j in range(per_block):
                head = kv * half + (own ^ k) * per_block + j
                at = (kv * per_block + j) * lanes
                outs[k][:slots, at : at + lanes] = attended[
                    pl.ds(head, slots, stride=heads), :
                ].astype(BF16)
    for copy in copies:
        copy.wait()


def attention(table, query_blocks, keys, values, jobs, parts, unroll=8):
    count = len(query_blocks)
    slots, heads, _ = query_blocks[0].shape
    pool, width = keys.shape
    most = pool // block_rows + slots + unroll
    rows = (slots + slot_group) * heads
    return pl.pallas_call(
        functools.partial(
            attention_kernel,
            slots=slots,
            count=count,
            scale=1.0 / math.sqrt(lanes),
            unroll=unroll,
            masks_of=masks_in(jobs),
        ),
        in_specs=[smem] + [vmem] * (count + 2) + [hbm] * len(jobs),
        out_specs=[vmem] * (count + len(jobs)),
        out_shape=[jax.ShapeDtypeStruct((up_to(slots, 8), heads // count * lanes), BF16)] * count
        + job_shapes(jobs, parts),
        scratch_shapes=[
            pltpu.VMEM((count * slots, heads, lanes), BF16),
            pltpu.VMEM((rows, width), BF16),
            pltpu.VMEM((rows, lanes), I32),
            pltpu.VMEM((rows, lanes), I32),
            pltpu.VMEM((rows, lanes), F32),
            pltpu.VMEM((rows, lanes), F32),
            pltpu.VMEM((most, slot_group * heads, block_rows), F32),
            pltpu.VMEM((rows, width), F32),
            pltpu.VMEM((slots * heads, lanes), F32),
            pltpu.SMEM((2 * most,), I32),
            pltpu.SemaphoreType.DMA((job_count(jobs),)),
        ],
        compiler_params=params(6),
        cost_estimate=pl.CostEstimate(
            flops=4 * pool * heads * lanes, bytes_accessed=pool * width * 4, transcendentals=0
        ),
        name="attention",
    )(
        table,
        *query_blocks,
        in_vmem(keys),
        in_vmem(values),
        *[in_hbm(array) for array, _ in jobs],
    )


def selection_kernel(table, source, target, choose, sems, *, slots, count, masks_of):
    copies = job_copies(table[1], masks_of, [source], [target], sems)
    for copy in copies:
        copy.start()
    own = table[0]
    requests, padded = choose.shape[1:]
    row = lax.broadcasted_iota(I32, (requests, padded), 0)
    wanted = row
    for k in range(count):
        moved = row + ((own ^ k) - k) * slots
        wanted = jnp.where((row >= k * slots) & (row < (k + 1) * slots), moved, wanted)
    lane = lax.broadcasted_iota(I32, (1, padded), 1)
    for k in range(count):
        served = jnp.full((1, padded), -1, I32)
        for i in range(slots):
            request = table[2 + slots + (own ^ k) * slots + i]
            served = jnp.where(lane == i, request, served)
        choose[k] = (wanted == served).astype(F32).astype(BF16)
    for copy in copies:
        copy.wait()


def selection(table, jobs, parts, slots, padded, count):
    shapes = job_shapes(jobs, parts)
    moved = sum(2 * math.prod(shape.shape) for shape in shapes)
    return pl.pallas_call(
        functools.partial(
            selection_kernel, slots=slots, count=count, masks_of=masks_in(jobs)
        ),
        in_specs=[smem, hbm],
        out_specs=[vmem] * 2,
        out_shape=shapes + [jax.ShapeDtypeStruct((count, slots * count, padded), BF16)],
        scratch_shapes=[pltpu.SemaphoreType.DMA((job_count(jobs),))],
        compiler_params=params(1),
        cost_estimate=pl.CostEstimate(flops=0, bytes_accessed=2 * moved, transcendentals=0),
        name="selection",
    )(table, in_hbm(jobs[0][0]))


def ordered_kernel(choose, *refs):
    blocks, out = refs[:-1], refs[-1]
    total = None
    for k, block in enumerate(blocks):
        term = jnp.dot(choose[k], block[...], preferred_element_type=F32)
        total = term if total is None else total + term
    out[...] = total.astype(BF16)


def ordered(choose, blocks):
    return pl.pallas_call(
        ordered_kernel,
        in_specs=[vmem] * (1 + len(blocks)),
        out_specs=vmem,
        out_shape=jax.ShapeDtypeStruct((choose.shape[1], blocks[0].shape[1]), BF16),
        compiler_params=params(2),
        name="ordered",
    )(choose, *blocks)


def projection_kernel(*refs, slots, parts):
    pieces, weight, outs = refs[:parts], refs[parts], refs[parts + 1 :]
    total = None
    for p in range(parts):
        term = jnp.dot(pieces[p][...], weight[p], preferred_element_type=F32)
        total = term if total is None else total + term
    for k, out in enumerate(outs):
        out[...] = halves_stacked(total[k * slots : (k + 1) * slots]).astype(BF16)


def projection(pieces, weight, slots, count):
    parts, depth, width = weight.shape
    return pl.pallas_call(
        functools.partial(projection_kernel, slots=slots, parts=parts),
        in_specs=[vmem] * (1 + parts),
        out_specs=[vmem] * count,
        out_shape=[jax.ShapeDtypeStruct((2 * slots, width // 2), BF16)] * count,
        compiler_params=params(2),
        cost_estimate=pl.CostEstimate(
            flops=2 * slots * count * parts * depth * width,
            bytes_accessed=parts * depth * width,
            transcendentals=0,
        ),
        name="projection",
    )(*pieces, in_vmem(weight))


def residual_kernel(*refs, joined):
    base, blocks, out = refs[0], refs[1:-1], refs[-1]
    total = base[...].astype(F32)
    if not joined:
        total = halves_stacked(total)
    for block in blocks:
        total = total + block[...].astype(F32)
    out[...] = (halves_joined(total) if joined else total).astype(BF16)


def residual(base, blocks, joined):
    rows, half = blocks[0].shape
    shape = (rows // 2, 2 * half) if joined else (rows, half)
    return pl.pallas_call(
        functools.partial(residual_kernel, joined=joined),
        in_specs=[vmem] * (1 + len(blocks)),
        out_specs=vmem,
        out_shape=jax.ShapeDtypeStruct(shape, BF16),
        compiler_params=params(2),
        name="residual",
    )(base, *blocks)


def unit_product(scaled, weight, part):
    return lax.dot_general(scaled, weight[part], contract_minor, preferred_element_type=F32)


def product_cost(requests, units, width):
    return pl.CostEstimate(
        flops=2 * requests * units * width, bytes_accessed=units * width, transcendentals=0
    )


def hidden_first_kernel(*refs, count, part):
    blocks, (gain, weight, send, scaled, squares, joined) = refs[:count], refs[count:]
    rows = blocks[0].shape[0] // 2
    for k in range(count):
        joined[k * rows : (k + 1) * rows, :] = halves_joined(blocks[k][...])
    middle = joined[...]
    square = jnp.sum(middle * middle, axis=1, keepdims=True)
    scaled[...] = (middle * gain[...].astype(F32)).astype(BF16)
    units = weight.shape[1]
    send[:, :units] = unit_product(scaled[...], weight, part).astype(BF16)
    send[:, units:] = high_low(square).astype(BF16)
    squares[...] = jnp.broadcast_to(square, squares.shape)


def hidden_first(blocks, gain, weight, part):
    count = len(blocks)
    rows, half = blocks[0].shape
    requests, width = rows // 2 * count, 2 * half
    units = weight.shape[1]
    return pl.pallas_call(
        functools.partial(hidden_first_kernel, count=count, part=part),
        in_specs=[vmem] * (count + 2),
        out_specs=[vmem] * 3,
        out_shape=[
            jax.ShapeDtypeStruct((requests, units + lanes), BF16),
            jax.ShapeDtypeStruct((requests, width), BF16),
            jax.ShapeDtypeStruct((requests, lanes), F32),
        ],
        scratch_shapes=[pltpu.VMEM((requests, width), F32)],
        compiler_params=params(2),
        cost_estimate=product_cost(requests, units, width),
        name="hidden_first",
    )(*blocks, gain, in_vmem(weight))


def hidden_kernel(scaled, *refs, parts):
    weights, out = refs[:-1], refs[-1]
    for t, (weight, part) in enumerate(zip(weights, parts)):
        units = weight.shape[1]
        out[:, t * units : (t + 1) * units] = unit_product(scaled[...], weight, part).astype(
            out.dtype
        )


def hidden_next(scaled, chosen, kind):
    requests, width = scaled.shape
    units = chosen[0][0].shape[1]
    return pl.pallas_call(
        functools.partial(hidden_kernel, parts=tuple(part for _, part in chosen)),
        in_specs=[vmem] * (1 + len(chosen)),
        out_specs=vmem,
        out_shape=jax.ShapeDtypeStruct((requests, len(chosen) * units), kind),
        compiler_params=params(2),
        cost_estimate=product_cost(requests, len(chosen) * units, width),
        name="hidden_next",
    )(scaled, *[in_vmem(weight) for weight, _ in chosen])


def squares_sum_kernel(keep, own_squares, arrived, out, squares):
    width = keep.shape[1]
    out[:, :width] = (keep[...] + arrived[:, :width].astype(F32)).astype(BF16)
    tail = arrived[:, width:].astype(F32)
    chip = own_squares[...] + (tail[:, :1] + tail[:, lanes // 2 : lanes // 2 + 1])
    squares[...] = chip
    out[:, width:] = high_low(chip).astype(BF16)


def squares_sum(keep, own_squares, arrived):
    requests, width = arrived.shape
    return pl.pallas_call(
        squares_sum_kernel,
        in_specs=[vmem] * 3,
        out_specs=[vmem] * 2,
        out_shape=[
            jax.ShapeDtypeStruct((requests, width), BF16),
            jax.ShapeDtypeStruct((requests, lanes), F32),
        ],
        compiler_params=params(2),
        name="squares_sum",
    )(keep, own_squares, arrived)


def chip_sum_kernel(keep, arrived, out):
    out[...] = (keep[...] + arrived[...].astype(F32)).astype(BF16)


def chip_sum(keep, arrived):
    return pl.pallas_call(
        chip_sum_kernel,
        in_specs=[vmem] * 2,
        out_specs=vmem,
        out_shape=jax.ShapeDtypeStruct(arrived.shape, BF16),
        compiler_params=params(2),
        name="chip_sum",
    )(keep, arrived)


def active_kernel(near, beside, far_gate, far_up, squares, out, *, model_width):
    units = far_up.shape[1]
    tail = far_gate[:, units:].astype(F32)
    square = squares[:, :1] + (tail[:, :1] + tail[:, lanes // 2 : lanes // 2 + 1])
    scale = lax.rsqrt(square / model_width + epsilon)

    def total(at, far):
        both = near[:, at : at + units] + beside[:, at : at + units].astype(F32)
        return (both + far.astype(F32)) * scale

    gate = total(0, far_gate[:, :units])
    out[...] = (gate / (1.0 + jnp.exp(-gate)) * total(units, far_up[...])).astype(BF16)


def active_units(near, beside, far_gate, far_up, squares, model_width):
    requests, width = near.shape
    return pl.pallas_call(
        functools.partial(active_kernel, model_width=model_width),
        in_specs=[vmem] * 5,
        out_specs=vmem,
        out_shape=jax.ShapeDtypeStruct((requests, width // 2), BF16),
        compiler_params=params(2),
        name="active",
    )(near, beside, far_gate, far_up, squares)


def down_kernel(*refs, parts, count, first, last):
    terms = len(parts)
    pieces, weights, rest = refs[:terms], refs[terms : 2 * terms], refs[2 * terms :]
    total = None if first else rest[0][...]
    outs = rest if first else rest[1:]
    for piece, weight, part in zip(pieces, weights, parts):
        term = jnp.dot(piece[...], weight[part], preferred_element_type=F32)
        total = term if total is None else total + term
    if last:
        rows = total.shape[0] // count
        for k in range(count):
            outs[k][...] = halves_stacked(total[k * rows : (k + 1) * rows]).astype(BF16)
    else:
        outs[0][...] = total


def down_part(chosen, count, before, last):
    requests, units = chosen[0][0].shape
    width = chosen[0][1].shape[2]
    if last:
        outs = [jax.ShapeDtypeStruct((2 * requests // count, width // 2), BF16)] * count
    else:
        outs = [jax.ShapeDtypeStruct((requests, width), F32)]
    before = [] if before is None else [before]
    return pl.pallas_call(
        functools.partial(
            down_kernel,
            parts=tuple(part for _, _, part in chosen),
            count=count,
            first=not before,
            last=last,
        ),
        in_specs=[vmem] * (2 * len(chosen) + len(before)),
        out_specs=[vmem] * len(outs),
        out_shape=outs,
        compiler_params=params(2),
        cost_estimate=product_cost(requests, len(chosen) * units, width),
        name="down",
    )(*[piece for piece, _, _ in chosen], *[in_vmem(w) for _, w, _ in chosen], *before)


def swaps_of(blocks):
    count = len(blocks)
    arrived = {k: pair_swap(blocks[k], "att", k) for k in reversed(range(1, count))}
    return [blocks[0]] + [arrived[k] for k in range(1, count)]


def exchanging_device(*args):
    return exchanging_layer(*args)


def exchanging_layer(
    hidden_state,
    queries,
    key_cache,
    value_cache,
    lengths,
    assignment,
    out_weight,
    norm_gain,
    gate_weight,
    up_weight,
    down_weight,
):
    slots, columns = hidden_state.shape
    count = lax.axis_size("att")
    parts = lax.axis_size("ffn")
    model_width = columns * parts
    heads = queries.shape[1] // lanes
    own = jnp.stack([lax.axis_index("att"), lax.axis_index("ffn")]).astype(I32)
    table = jnp.concatenate([own, lengths, assignment])
    own_queries = queries.reshape(slots, heads, lanes)
    query_blocks = swaps_of([own_queries] * count)
    keys, values = fetch(table, [(key_cache, None), (value_cache, None)], parts)
    jobs = [(out_weight.reshape(-1, columns), (0, 1, 2, 3)), (down_weight, (0, 1))]
    *blocks, project, down_near = attention(table, query_blocks, keys, values, jobs, parts)

    blocks = swaps_of(blocks)
    padded = blocks[0].shape[0]
    jobs = [(down_weight, (2,))]
    down_across, choose = selection(table, jobs, parts, slots, padded, count)
    piece = ordered(choose, blocks)
    across = pair_swap(piece, "ffn", 2)
    beside = pair_swap(piece, "ffn", 1)
    corner = pair_swap(across, "ffn", 1)
    (down_corner,) = fetch(table, [(down_weight, (3,))], parts)
    gain = norm_gain.reshape(1, columns)
    partial = projection([piece, beside, across, corner], project, slots, count)
    jobs = [(gate_weight, (0, 1, 2, 3)), (up_weight, (3,))]
    gate, up_corner = fetch(table, jobs, parts)
    middle = residual(hidden_state, swaps_of(partial), False)

    rows = swaps_of([middle] * count)
    (up,) = fetch(table, [(up_weight, (0, 1, 2))], parts)
    send, scaled, squares = hidden_first(rows, gain, gate, 3)
    arrived = pair_swap(send, "ffn", 1)
    keep = hidden_next(scaled, [(gate, 2)], F32)
    far_gate, squares = squares_sum(keep, squares, arrived)
    far_gate = pair_swap(far_gate, "ffn", 2)
    send = hidden_next(scaled, [(up_corner, 0)], BF16)
    arrived = pair_swap(send, "ffn", 1)
    keep = hidden_next(scaled, [(up, 2)], F32)
    far_up = pair_swap(chip_sum(keep, arrived), "ffn", 2)
    send = hidden_next(scaled, [(gate, 1), (up, 1)], BF16)
    arrived = pair_swap(send, "ffn", 1)
    keep = hidden_next(scaled, [(gate, 0), (up, 0)], F32)
    active = active_units(keep, arrived, far_gate, far_up, squares, model_width)

    across = pair_swap(active, "ffn", 2)
    beside = pair_swap(active, "ffn", 1)
    chosen = [(active, down_near, 0), (beside, down_near, 1)]
    (before,) = down_part(chosen, count, None, False)
    corner = pair_swap(across, "ffn", 1)
    (before,) = down_part([(across, down_across, 0)], count, before, False)
    partial = down_part([(corner, down_corner, 0)], count, before, True)
    return residual(middle, swaps_of(partial), True)


def solution(mesh):
    count, parts = mesh.shape["att"], mesh.shape["ffn"]
    paired = count == 4 and parts == 4
    in_specs = (
        P(("group", "att"), "ffn"),
        P(("group", "att"), "ffn"),
        P(("group", "att"), "ffn"),
        P(("group", "att"), "ffn"),
        P(("group", "att")),
        P("group"),
        P(None, "att", "ffn"),
        P("ffn"),
        P("att", "ffn"),
        P("att", "ffn"),
        P("att", "ffn"),
    )
    out_specs = P(("group", "att"), "ffn")
    return jax.shard_map(
        exchanging_device if paired else general_device,
        mesh=mesh,
        in_specs=in_specs,
        out_specs=out_specs,
        check_vma=False,
    )
```

```python
import functools
import math

import jax
import jax.numpy as jnp
from jax import lax
from jax.experimental import pallas as pl
from jax.experimental.pallas import tpu as pltpu
from jax.sharding import PartitionSpec as P

epsilon = 1e-05
masked_score = -1e30
lanes = 128
block_rows = 256
slot_group = 2
contract_minor = (((1,), (1,)), ((), ()))
F32 = jnp.float32
BF16 = jnp.bfloat16
I32 = jnp.int32
vmem = pl.BlockSpec(memory_space=pltpu.VMEM)
smem = pl.BlockSpec(memory_space=pltpu.SMEM)
hbm = pl.BlockSpec(memory_space=pltpu.HBM)


def softmax_rounded(scores):
    row_top = jnp.max(scores, axis=-1, keepdims=True)
    shifted = jnp.exp(scores - row_top)
    totals = jnp.sum(shifted, axis=-1, keepdims=True)
    return (shifted / totals).astype(jnp.bfloat16)


def general_device(
    hidden_state,
    queries,
    key_cache,
    value_cache,
    lengths,
    assignment,
    out_weight,
    norm_gain,
    gate_weight,
    up_weight,
    down_weight,
):
    rows_dev = hidden_state.shape[0]
    columns = hidden_state.shape[1]
    att_count = lax.axis_size("att")
    ffn_count = lax.axis_size("ffn")
    requests = rows_dev * att_count
    kv_total = out_weight.shape[0]
    kv_local = kv_total // ffn_count
    model_width = columns * ffn_count
    pool_rows = key_cache.shape[0]
    head_size = key_cache.shape[1] // kv_local
    per_group = queries.shape[1] // (kv_local * head_size)
    score_scale = 1.0 / math.sqrt(head_size)
    att_place = lax.axis_index("att")
    every_query = lax.all_gather(queries, "att", axis=0, tiled=True)
    own_slots = lax.dynamic_slice_in_dim(assignment, att_place * rows_dev, rows_dev)
    slot_queries = jnp.take(every_query, own_slots, axis=0).reshape(
        rows_dev, kv_local, per_group, head_size
    )
    keys_local = key_cache.reshape(pool_rows, kv_local, head_size)
    values_local = value_cache.reshape(pool_rows, kv_local, head_size)
    slot_starts = jnp.cumsum(lengths) - lengths
    slot_ends = slot_starts + lengths
    positions = jnp.arange(pool_rows, dtype=jnp.int32)
    owned_rows = (positions[None, :] >= slot_starts[:, None]) & (
        positions[None, :] < slot_ends[:, None]
    )
    owned_rows = owned_rows[:, None, None, :]
    raw_scores = (
        jnp.einsum("rkgc,pkc->rkgp", slot_queries, keys_local, preferred_element_type=jnp.float32)
        * score_scale
    )
    weights = softmax_rounded(jnp.where(owned_rows, raw_scores, masked_score))
    attended = jnp.einsum(
        "rkgp,pkc->rkgc", weights, values_local, preferred_element_type=jnp.float32
    )
    attended = attended.astype(jnp.bfloat16).reshape(rows_dev, kv_local, per_group * head_size)
    spread = lax.all_to_all(attended, "att", split_axis=2, concat_axis=0, tiled=True)
    pieces = lax.all_gather(spread, "ffn", axis=1, tiled=True)
    inverse = (
        jnp.zeros((requests,), jnp.int32).at[assignment].set(jnp.arange(requests, dtype=jnp.int32))
    )
    request_pieces = jnp.take(pieces, inverse, axis=0)
    block = request_pieces
    projected = lax.psum_scatter(
        jnp.einsum("rkc,kcd->rd", block, out_weight, preferred_element_type=jnp.float32).astype(
            jnp.bfloat16
        ),
        "att",
        scatter_dimension=0,
        tiled=True,
    ).astype(jnp.float32)
    middle_short = (hidden_state.astype(jnp.float32) + projected).astype(jnp.bfloat16)
    middle = lax.optimization_barrier(middle_short).astype(jnp.float32)
    squares = lax.psum(jnp.sum(middle * middle, axis=1), "ffn")
    normed = (
        middle * lax.rsqrt(squares[:, None] / model_width + epsilon) * norm_gain.astype(jnp.float32)
    ).astype(jnp.bfloat16)
    every_row = lax.all_gather(normed, "att", axis=0, tiled=True)
    contract = (((1,), (1,)), ((), ()))
    gate_part = lax.dot_general(
        gate_weight, every_row, contract, preferred_element_type=jnp.float32
    )
    up_part = lax.dot_general(up_weight, every_row, contract, preferred_element_type=jnp.float32)
    totals = lax.psum(
        jnp.concatenate([gate_part, up_part], axis=1).astype(jnp.bfloat16), "ffn"
    ).astype(jnp.float32)
    unit_active = (jax.nn.silu(totals[:, :requests]) * totals[:, requests:]).astype(jnp.bfloat16)
    block = unit_active
    returned = lax.psum_scatter(
        lax.dot_general(
            block, down_weight, (((0,), (0,)), ((), ())), preferred_element_type=jnp.float32
        ).astype(jnp.bfloat16),
        "att",
        scatter_dimension=0,
        tiled=True,
    ).astype(jnp.float32)
    return (middle + returned).astype(jnp.bfloat16)


def pair_swap(value, axis, bit):
    count = lax.axis_size(axis)
    return lax.ppermute(value, axis, [(i, i ^ bit) for i in range(count)])


def up_to(value, multiple):
    return -(-value // multiple) * multiple


def params(megabytes):
    return pltpu.CompilerParams(vmem_limit_bytes=megabytes << 20)


def halves_joined(block):
    block = block.astype(F32)
    rows = block.shape[0] // 2
    return jnp.concatenate([block[:rows], block[rows:]], axis=1)


def halves_stacked(block):
    half = block.shape[1] // 2
    return jnp.concatenate([block[:, :half], block[:, half:]], axis=0)


def high_low(value):
    high = value.astype(BF16).astype(F32)
    low = value - high
    lane = lax.broadcasted_iota(I32, (value.shape[0], lanes), 1)
    return jnp.where(lane < lanes // 2, high, low)


def in_hbm(value):
    return pltpu.with_memory_space_constraint(value, pltpu.HBM)


def in_vmem(value):
    return pltpu.with_memory_space_constraint(value, pltpu.VMEM)


def job_shapes(jobs, parts):
    shapes = []
    for array, masks in jobs:
        if masks is None:
            shapes.append(pltpu.VMEM(array.shape, array.dtype))
        else:
            rows, width = array.shape
            shapes.append(pltpu.VMEM((len(masks), rows // parts, width), array.dtype))
    return shapes


def job_count(jobs):
    return sum(1 if masks is None else len(masks) for _, masks in jobs)


def job_copies(own, masks_of, sources, targets, sems):
    copies = []
    for masks, source, target in zip(masks_of, sources, targets):
        if masks is None:
            copies.append(pltpu.make_async_copy(source, target, sems.at[len(copies)]))
            continue
        rows = target.shape[1]
        for m, mask in enumerate(masks):
            at = pl.ds(pl.multiple_of((own ^ mask) * rows, rows), rows)
            copies.append(
                pltpu.make_async_copy(source.at[at], target.at[m], sems.at[len(copies)])
            )
    return copies


def masks_in(jobs):
    return tuple(masks for _, masks in jobs)


def fetch_kernel(*refs, masks_of, placed):
    own = refs[0][1] if placed else None
    refs = refs[1:] if placed else refs
    count = len(masks_of)
    copies = job_copies(own, masks_of, refs[:count], refs[count:-1], refs[-1])
    for copy in copies:
        copy.start()
    for copy in copies:
        copy.wait()


def fetch(table, jobs, parts):
    shapes = job_shapes(jobs, parts)
    placed = any(masks is not None for _, masks in jobs)
    moved = sum(2 * math.prod(shape.shape) for shape in shapes)
    return pl.pallas_call(
        functools.partial(fetch_kernel, masks_of=masks_in(jobs), placed=placed),
        in_specs=([smem] if placed else []) + [hbm] * len(jobs),
        out_specs=[vmem] * len(jobs),
        out_shape=shapes,
        scratch_shapes=[pltpu.SemaphoreType.DMA((job_count(jobs),))],
        compiler_params=params(1),
        cost_estimate=pl.CostEstimate(flops=0, bytes_accessed=2 * moved, transcendentals=0),
        name="fetch",
    )(*([table] if placed else []), *[in_hbm(array) for array, _ in jobs])


def folded(combine, value):
    parts = [value[:, i : i + lanes] for i in range(0, value.shape[1], lanes)]
    return functools.reduce(combine, parts)


def attention_kernel(table, *refs, slots, count, scale, unroll, masks_of):
    jobs = len(masks_of)
    query_blocks, (keys, values), sources = (
        refs[:count],
        refs[count : count + 2],
        refs[count + 2 : count + 2 + jobs],
    )
    outs, targets = (
        refs[count + 2 + jobs : 2 * count + 2 + jobs],
        refs[2 * count + 2 + jobs : 2 * count + 2 + 2 * jobs],
    )
    queries, both, begins, ends, tops, sums, scores, total, attended, items, sems = refs[
        2 * count + 2 + 2 * jobs :
    ]
    copies = job_copies(table[1], masks_of, sources, targets, sems)
    for copy in copies:
        copy.start()
    pool, width = keys.shape
    heads = queries.shape[1]
    half = heads // 2
    own = table[0]
    group_rows = slot_group * heads
    top_half = lax.broadcasted_iota(I32, (heads, lanes), 0) < half
    for k in range(count):
        queries[k * slots : (k + 1) * slots] = query_blocks[k][...]

    tops[...] = jnp.full(tops.shape, masked_score, F32)
    sums[...] = jnp.zeros(sums.shape, F32)
    total[...] = jnp.zeros(total.shape, F32)
    spare = slots * heads
    both[spare:, :] = jnp.zeros((both.shape[0] - spare, width), BF16)
    begins[spare:, :] = jnp.full((begins.shape[0] - spare, lanes), pool, I32)
    ends[spare:, :] = jnp.zeros((ends.shape[0] - spare, lanes), I32)

    def slot(s, carry):
        start, made, last_block, last_slot = carry
        end = start + table[2 + s]
        request = table[2 + slots + own * slots + s]
        owner = sum((request >= k * slots).astype(I32) for k in range(1, count))
        query = queries[(owner ^ own) * slots + request - owner * slots]
        zero = jnp.zeros_like(query)
        at = pl.ds(pl.multiple_of(s * heads, heads), heads)
        both[at, :lanes] = jnp.where(top_half, query, zero)
        both[at, lanes:] = jnp.where(top_half, zero, query)
        begins[at, :] = jnp.full((heads, lanes), start, I32)
        ends[at, :] = jnp.full((heads, lanes), end, I32)
        first = start // block_rows
        covered = (first == last_block) & (s < last_slot + slot_group)
        first = jnp.where(covered, first + 1, first)
        last = (end - 1) // block_rows

        def item(block, made):
            items[2 * made] = block
            items[2 * made + 1] = s
            return made + 1

        made_now = lax.fori_loop(first, last + 1, item, made)
        new = made_now > made
        return (
            end,
            made_now,
            jnp.where(new, last, last_block),
            jnp.where(new, s, last_slot),
        )

    none = jnp.int32(-1)
    _, made, _, _ = lax.fori_loop(0, slots, slot, (jnp.int32(0), jnp.int32(0), none, none))
    for u in range(unroll):
        items[2 * (made + u)] = 0
        items[2 * (made + u) + 1] = slots
    steps = (made + unroll - 1) // unroll
    across = lax.broadcasted_iota(I32, (group_rows, block_rows), 1)

    def place_of(i):
        block = pl.multiple_of(items[2 * i] * block_rows, block_rows)
        rows = pl.multiple_of(items[2 * i + 1] * heads, heads)
        return block, pl.ds(block, block_rows), pl.ds(rows, group_rows)

    def score_step(step, carry):
        for u in range(unroll):
            i = step * unroll + u
            block, cache, rows = place_of(i)
            raw = lax.dot_general(
                both[rows, :], keys[cache, :], contract_minor, preferred_element_type=F32
            )
            position = block + across
            begin, end = (jnp.concatenate([b[rows, :]] * (block_rows // lanes), axis=1) for b in (begins, ends))
            inside = (position >= begin) & (position < end)
            masked = jnp.where(inside, raw * scale, masked_score)
            scores[i] = masked
            tops[rows, :] = jnp.maximum(tops[rows, :], folded(jnp.maximum, masked))
        return carry

    def value_step(step, carry):
        for u in range(unroll):
            i = step * unroll + u
            _, cache, rows = place_of(i)
            top = tops[rows, :]
            shifted = jnp.exp(scores[i] - jnp.concatenate([top] * (block_rows // lanes), axis=1))
            sums[rows, :] += folded(jnp.add, shifted)
            total[rows, :] += jnp.dot(
                shifted.astype(BF16), values[cache, :], preferred_element_type=F32
            )
        return carry

    lax.fori_loop(0, steps, score_step, 0)
    top = jnp.max(tops[...], axis=1, keepdims=True)
    tops[...] = jnp.broadcast_to(top, tops.shape)
    lax.fori_loop(0, steps, value_step, 0)

    real = slots * heads
    row = lax.broadcasted_iota(I32, (real, lanes), 0)
    upper = row % heads < half
    picked = jnp.where(upper, total[:real, :lanes], total[:real, lanes:])
    attended[...] = picked / jnp.sum(sums[:real, :], axis=1, keepdims=True)
    per_block = half // count
    for k in range(count):
        outs[k][...] = jnp.zeros(outs[k].shape, BF16)
        for kv in range(2):
            for j in range(per_block):
                head = kv * half + (own ^ k) * per_block + j
                at = (kv * per_block + j) * lanes
                outs[k][:slots, at : at + lanes] = attended[
                    pl.ds(head, slots, stride=heads), :
                ].astype(BF16)
    for copy in copies:
        copy.wait()


def attention(table, query_blocks, keys, values, jobs, parts, unroll=8):
    count = len(query_blocks)
    slots, heads, _ = query_blocks[0].shape
    pool, width = keys.shape
    most = pool // block_rows + slots + unroll
    rows = (slots + slot_group) * heads
    return pl.pallas_call(
        functools.partial(
            attention_kernel,
            slots=slots,
            count=count,
            scale=1.0 / math.sqrt(lanes),
            unroll=unroll,
            masks_of=masks_in(jobs),
        ),
        in_specs=[smem] + [vmem] * (count + 2) + [hbm] * len(jobs),
        out_specs=[vmem] * (count + len(jobs)),
        out_shape=[jax.ShapeDtypeStruct((up_to(slots, 8), heads // count * lanes), BF16)] * count
        + job_shapes(jobs, parts),
        scratch_shapes=[
            pltpu.VMEM((count * slots, heads, lanes), BF16),
            pltpu.VMEM((rows, width), BF16),
            pltpu.VMEM((rows, lanes), I32),
            pltpu.VMEM((rows, lanes), I32),
            pltpu.VMEM((rows, lanes), F32),
            pltpu.VMEM((rows, lanes), F32),
            pltpu.VMEM((most, slot_group * heads, block_rows), F32),
            pltpu.VMEM((rows, width), F32),
            pltpu.VMEM((slots * heads, lanes), F32),
            pltpu.SMEM((2 * most,), I32),
            pltpu.SemaphoreType.DMA((job_count(jobs),)),
        ],
        compiler_params=params(6),
        cost_estimate=pl.CostEstimate(
            flops=4 * pool * heads * lanes, bytes_accessed=pool * width * 4, transcendentals=0
        ),
        name="attention",
    )(
        table,
        *query_blocks,
        in_vmem(keys),
        in_vmem(values),
        *[in_hbm(array) for array, _ in jobs],
    )


def selection_kernel(table, source, target, choose, sems, *, slots, count, masks_of):
    copies = job_copies(table[1], masks_of, [source], [target], sems)
    for copy in copies:
        copy.start()
    own = table[0]
    requests, padded = choose.shape[1:]
    row = lax.broadcasted_iota(I32, (requests, padded), 0)
    wanted = row
    for k in range(count):
        moved = row + ((own ^ k) - k) * slots
        wanted = jnp.where((row >= k * slots) & (row < (k + 1) * slots), moved, wanted)
    lane = lax.broadcasted_iota(I32, (1, padded), 1)
    for k in range(count):
        served = jnp.full((1, padded), -1, I32)
        for i in range(slots):
            request = table[2 + slots + (own ^ k) * slots + i]
            served = jnp.where(lane == i, request, served)
        choose[k] = (wanted == served).astype(F32).astype(BF16)
    for copy in copies:
        copy.wait()


def selection(table, jobs, parts, slots, padded, count):
    shapes = job_shapes(jobs, parts)
    moved = sum(2 * math.prod(shape.shape) for shape in shapes)
    return pl.pallas_call(
        functools.partial(
            selection_kernel, slots=slots, count=count, masks_of=masks_in(jobs)
        ),
        in_specs=[smem, hbm],
        out_specs=[vmem] * 2,
        out_shape=shapes + [jax.ShapeDtypeStruct((count, slots * count, padded), BF16)],
        scratch_shapes=[pltpu.SemaphoreType.DMA((job_count(jobs),))],
        compiler_params=params(1),
        cost_estimate=pl.CostEstimate(flops=0, bytes_accessed=2 * moved, transcendentals=0),
        name="selection",
    )(table, in_hbm(jobs[0][0]))


def ordered_kernel(choose, *refs):
    blocks, out = refs[:-1], refs[-1]
    total = None
    for k, block in enumerate(blocks):
        term = jnp.dot(choose[k], block[...], preferred_element_type=F32)
        total = term if total is None else total + term
    out[...] = total.astype(BF16)


def ordered(choose, blocks):
    return pl.pallas_call(
        ordered_kernel,
        in_specs=[vmem] * (1 + len(blocks)),
        out_specs=vmem,
        out_shape=jax.ShapeDtypeStruct((choose.shape[1], blocks[0].shape[1]), BF16),
        compiler_params=params(2),
        name="ordered",
    )(choose, *blocks)


def projection_kernel(*refs, slots, parts):
    pieces, weight, outs = refs[:parts], refs[parts], refs[parts + 1 :]
    total = None
    for p in range(parts):
        term = jnp.dot(pieces[p][...], weight[p], preferred_element_type=F32)
        total = term if total is None else total + term
    for k, out in enumerate(outs):
        out[...] = halves_stacked(total[k * slots : (k + 1) * slots]).astype(BF16)


def projection(pieces, weight, slots, count):
    parts, depth, width = weight.shape
    return pl.pallas_call(
        functools.partial(projection_kernel, slots=slots, parts=parts),
        in_specs=[vmem] * (1 + parts),
        out_specs=[vmem] * count,
        out_shape=[jax.ShapeDtypeStruct((2 * slots, width // 2), BF16)] * count,
        compiler_params=params(2),
        cost_estimate=pl.CostEstimate(
            flops=2 * slots * count * parts * depth * width,
            bytes_accessed=parts * depth * width,
            transcendentals=0,
        ),
        name="projection",
    )(*pieces, in_vmem(weight))


def residual_kernel(*refs, joined):
    base, blocks, out = refs[0], refs[1:-1], refs[-1]
    total = base[...].astype(F32)
    if not joined:
        total = halves_stacked(total)
    for block in blocks:
        total = total + block[...].astype(F32)
    out[...] = (halves_joined(total) if joined else total).astype(BF16)


def residual(base, blocks, joined):
    rows, half = blocks[0].shape
    shape = (rows // 2, 2 * half) if joined else (rows, half)
    return pl.pallas_call(
        functools.partial(residual_kernel, joined=joined),
        in_specs=[vmem] * (1 + len(blocks)),
        out_specs=vmem,
        out_shape=jax.ShapeDtypeStruct(shape, BF16),
        compiler_params=params(2),
        name="residual",
    )(base, *blocks)


def unit_product(scaled, weight, part):
    return lax.dot_general(scaled, weight[part], contract_minor, preferred_element_type=F32)


def product_cost(requests, units, width):
    return pl.CostEstimate(
        flops=2 * requests * units * width, bytes_accessed=units * width, transcendentals=0
    )


def hidden_first_kernel(*refs, count, part):
    blocks, (gain, weight, send, scaled, squares, joined) = refs[:count], refs[count:]
    rows = blocks[0].shape[0] // 2
    for k in range(count):
        joined[k * rows : (k + 1) * rows, :] = halves_joined(blocks[k][...])
    middle = joined[...]
    square = jnp.sum(middle * middle, axis=1, keepdims=True)
    scaled[...] = (middle * gain[...].astype(F32)).astype(BF16)
    units = weight.shape[1]
    send[:, :units] = unit_product(scaled[...], weight, part).astype(BF16)
    send[:, units:] = high_low(square).astype(BF16)
    squares[...] = jnp.broadcast_to(square, squares.shape)


def hidden_first(blocks, gain, weight, part):
    count = len(blocks)
    rows, half = blocks[0].shape
    requests, width = rows // 2 * count, 2 * half
    units = weight.shape[1]
    return pl.pallas_call(
        functools.partial(hidden_first_kernel, count=count, part=part),
        in_specs=[vmem] * (count + 2),
        out_specs=[vmem] * 3,
        out_shape=[
            jax.ShapeDtypeStruct((requests, units + lanes), BF16),
            jax.ShapeDtypeStruct((requests, width), BF16),
            jax.ShapeDtypeStruct((requests, lanes), F32),
        ],
        scratch_shapes=[pltpu.VMEM((requests, width), F32)],
        compiler_params=params(2),
        cost_estimate=product_cost(requests, units, width),
        name="hidden_first",
    )(*blocks, gain, in_vmem(weight))


def hidden_kernel(scaled, *refs, parts):
    weights, out = refs[:-1], refs[-1]
    for t, (weight, part) in enumerate(zip(weights, parts)):
        units = weight.shape[1]
        out[:, t * units : (t + 1) * units] = unit_product(scaled[...], weight, part).astype(
            out.dtype
        )


def hidden_next(scaled, chosen, kind):
    requests, width = scaled.shape
    units = chosen[0][0].shape[1]
    return pl.pallas_call(
        functools.partial(hidden_kernel, parts=tuple(part for _, part in chosen)),
        in_specs=[vmem] * (1 + len(chosen)),
        out_specs=vmem,
        out_shape=jax.ShapeDtypeStruct((requests, len(chosen) * units), kind),
        compiler_params=params(2),
        cost_estimate=product_cost(requests, len(chosen) * units, width),
        name="hidden_next",
    )(scaled, *[in_vmem(weight) for weight, _ in chosen])


def squares_sum_kernel(keep, own_squares, arrived, out, squares):
    width = keep.shape[1]
    out[:, :width] = (keep[...] + arrived[:, :width].astype(F32)).astype(BF16)
    tail = arrived[:, width:].astype(F32)
    chip = own_squares[...] + (tail[:, :1] + tail[:, lanes // 2 : lanes // 2 + 1])
    squares[...] = chip
    out[:, width:] = high_low(chip).astype(BF16)


def squares_sum(keep, own_squares, arrived):
    requests, width = arrived.shape
    return pl.pallas_call(
        squares_sum_kernel,
        in_specs=[vmem] * 3,
        out_specs=[vmem] * 2,
        out_shape=[
            jax.ShapeDtypeStruct((requests, width), BF16),
            jax.ShapeDtypeStruct((requests, lanes), F32),
        ],
        compiler_params=params(2),
        name="squares_sum",
    )(keep, own_squares, arrived)


def chip_sum_kernel(keep, arrived, out):
    out[...] = (keep[...] + arrived[...].astype(F32)).astype(BF16)


def chip_sum(keep, arrived):
    return pl.pallas_call(
        chip_sum_kernel,
        in_specs=[vmem] * 2,
        out_specs=vmem,
        out_shape=jax.ShapeDtypeStruct(arrived.shape, BF16),
        compiler_params=params(2),
        name="chip_sum",
    )(keep, arrived)


def active_kernel(near, beside, far_gate, far_up, squares, out, *, model_width):
    units = far_up.shape[1]
    tail = far_gate[:, units:].astype(F32)
    square = squares[:, :1] + (tail[:, :1] + tail[:, lanes // 2 : lanes // 2 + 1])
    scale = lax.rsqrt(square / model_width + epsilon)

    def total(at, far):
        both = near[:, at : at + units] + beside[:, at : at + units].astype(F32)
        return (both + far.astype(F32)) * scale

    gate = total(0, far_gate[:, :units])
    out[...] = (gate / (1.0 + jnp.exp(-gate)) * total(units, far_up[...])).astype(BF16)


def active_units(near, beside, far_gate, far_up, squares, model_width):
    requests, width = near.shape
    return pl.pallas_call(
        functools.partial(active_kernel, model_width=model_width),
        in_specs=[vmem] * 5,
        out_specs=vmem,
        out_shape=jax.ShapeDtypeStruct((requests, width // 2), BF16),
        compiler_params=params(2),
        name="active",
    )(near, beside, far_gate, far_up, squares)


def down_kernel(*refs, parts, count, first, last):
    terms = len(parts)
    pieces, weights, rest = refs[:terms], refs[terms : 2 * terms], refs[2 * terms :]
    total = None if first else rest[0][...]
    outs = rest if first else rest[1:]
    for piece, weight, part in zip(pieces, weights, parts):
        term = jnp.dot(piece[...], weight[part], preferred_element_type=F32)
        total = term if total is None else total + term
    if last:
        rows = total.shape[0] // count
        for k in range(count):
            outs[k][...] = halves_stacked(total[k * rows : (k + 1) * rows]).astype(BF16)
    else:
        outs[0][...] = total


def down_part(chosen, count, before, last):
    requests, units = chosen[0][0].shape
    width = chosen[0][1].shape[2]
    if last:
        outs = [jax.ShapeDtypeStruct((2 * requests // count, width // 2), BF16)] * count
    else:
        outs = [jax.ShapeDtypeStruct((requests, width), F32)]
    before = [] if before is None else [before]
    return pl.pallas_call(
        functools.partial(
            down_kernel,
            parts=tuple(part for _, _, part in chosen),
            count=count,
            first=not before,
            last=last,
        ),
        in_specs=[vmem] * (2 * len(chosen) + len(before)),
        out_specs=[vmem] * len(outs),
        out_shape=outs,
        compiler_params=params(2),
        cost_estimate=product_cost(requests, len(chosen) * units, width),
        name="down",
    )(*[piece for piece, _, _ in chosen], *[in_vmem(w) for _, w, _ in chosen], *before)


def swaps_of(blocks):
    count = len(blocks)
    arrived = {k: pair_swap(blocks[k], "att", k) for k in reversed(range(1, count))}
    return [blocks[0]] + [arrived[k] for k in range(1, count)]


def exchanging_device(*args):
    return exchanging_layer(*args)


def exchanging_layer(
    hidden_state,
    queries,
    key_cache,
    value_cache,
    lengths,
    assignment,
    out_weight,
    norm_gain,
    gate_weight,
    up_weight,
    down_weight,
):
    slots, columns = hidden_state.shape
    count = lax.axis_size("att")
    parts = lax.axis_size("ffn")
    model_width = columns * parts
    heads = queries.shape[1] // lanes
    own = jnp.stack([lax.axis_index("att"), lax.axis_index("ffn")]).astype(I32)
    table = jnp.concatenate([own, lengths, assignment])
    own_queries = queries.reshape(slots, heads, lanes)
    query_blocks = swaps_of([own_queries] * count)
    keys, values = fetch(table, [(key_cache, None), (value_cache, None)], parts)
    jobs = [
        (out_weight.reshape(-1, columns), (0, 1, 2, 3)),
        (up_weight, (3,)),
        (down_weight, (0, 1)),
    ]
    *blocks, project, up_corner, down_near = attention(table, query_blocks, keys, values, jobs, parts)

    blocks = swaps_of(blocks)
    padded = blocks[0].shape[0]
    jobs = [(down_weight, (2,))]
    down_across, choose = selection(table, jobs, parts, slots, padded, count)
    piece = ordered(choose, blocks)
    across = pair_swap(piece, "ffn", 2)
    beside = pair_swap(piece, "ffn", 1)
    corner = pair_swap(across, "ffn", 1)
    (down_corner,) = fetch(table, [(down_weight, (3,))], parts)
    gain = norm_gain.reshape(1, columns)
    partial = projection([piece, beside, across, corner], project, slots, count)
    (gate,) = fetch(table, [(gate_weight, (0, 1, 2, 3))], parts)
    middle = residual(hidden_state, swaps_of(partial), False)

    rows = swaps_of([middle] * count)
    (up,) = fetch(table, [(up_weight, (0, 1, 2))], parts)
    send, scaled, squares = hidden_first(rows, gain, gate, 3)
    arrived = pair_swap(send, "ffn", 1)
    keep = hidden_next(scaled, [(gate, 2)], F32)
    far_gate, squares = squares_sum(keep, squares, arrived)
    far_gate = pair_swap(far_gate, "ffn", 2)
    send = hidden_next(scaled, [(up_corner, 0)], BF16)
    arrived = pair_swap(send, "ffn", 1)
    keep = hidden_next(scaled, [(up, 2)], F32)
    far_up = pair_swap(chip_sum(keep, arrived), "ffn", 2)
    send = hidden_next(scaled, [(gate, 1), (up, 1)], BF16)
    arrived = pair_swap(send, "ffn", 1)
    keep = hidden_next(scaled, [(gate, 0), (up, 0)], F32)
    active = active_units(keep, arrived, far_gate, far_up, squares, model_width)

    across = pair_swap(active, "ffn", 2)
    beside = pair_swap(active, "ffn", 1)
    chosen = [(active, down_near, 0), (beside, down_near, 1)]
    (before,) = down_part(chosen, count, None, False)
    corner = pair_swap(across, "ffn", 1)
    (before,) = down_part([(across, down_across, 0)], count, before, False)
    partial = down_part([(corner, down_corner, 0)], count, before, True)
    return residual(middle, swaps_of(partial), True)


def solution(mesh):
    count, parts = mesh.shape["att"], mesh.shape["ffn"]
    paired = count == 4 and parts == 4
    in_specs = (
        P(("group", "att"), "ffn"),
        P(("group", "att"), "ffn"),
        P(("group", "att"), "ffn"),
        P(("group", "att"), "ffn"),
        P(("group", "att")),
        P("group"),
        P(None, "att", "ffn"),
        P("ffn"),
        P("att", "ffn"),
        P("att", "ffn"),
        P("att", "ffn"),
    )
    out_specs = P(("group", "att"), "ffn")
    return jax.shard_map(
        exchanging_device if paired else general_device,
        mesh=mesh,
        in_specs=in_specs,
        out_specs=out_specs,
        check_vma=False,
    )
```

```python
import functools
import math

import jax
import jax.numpy as jnp
from jax import lax
from jax.experimental import pallas as pl
from jax.experimental.pallas import tpu as pltpu
from jax.sharding import PartitionSpec as P

epsilon = 1e-05
masked_score = -1e30
lanes = 128
block_rows = 256
slot_group = 2
contract_minor = (((1,), (1,)), ((), ()))
F32 = jnp.float32
BF16 = jnp.bfloat16
I32 = jnp.int32
vmem = pl.BlockSpec(memory_space=pltpu.VMEM)
smem = pl.BlockSpec(memory_space=pltpu.SMEM)
hbm = pl.BlockSpec(memory_space=pltpu.HBM)


def softmax_rounded(scores):
    row_top = jnp.max(scores, axis=-1, keepdims=True)
    shifted = jnp.exp(scores - row_top)
    totals = jnp.sum(shifted, axis=-1, keepdims=True)
    return (shifted / totals).astype(jnp.bfloat16)


def general_device(
    hidden_state,
    queries,
    key_cache,
    value_cache,
    lengths,
    assignment,
    out_weight,
    norm_gain,
    gate_weight,
    up_weight,
    down_weight,
):
    rows_dev = hidden_state.shape[0]
    columns = hidden_state.shape[1]
    att_count = lax.axis_size("att")
    ffn_count = lax.axis_size("ffn")
    requests = rows_dev * att_count
    kv_total = out_weight.shape[0]
    kv_local = kv_total // ffn_count
    model_width = columns * ffn_count
    pool_rows = key_cache.shape[0]
    head_size = key_cache.shape[1] // kv_local
    per_group = queries.shape[1] // (kv_local * head_size)
    score_scale = 1.0 / math.sqrt(head_size)
    att_place = lax.axis_index("att")
    every_query = lax.all_gather(queries, "att", axis=0, tiled=True)
    own_slots = lax.dynamic_slice_in_dim(assignment, att_place * rows_dev, rows_dev)
    slot_queries = jnp.take(every_query, own_slots, axis=0).reshape(
        rows_dev, kv_local, per_group, head_size
    )
    keys_local = key_cache.reshape(pool_rows, kv_local, head_size)
    values_local = value_cache.reshape(pool_rows, kv_local, head_size)
    slot_starts = jnp.cumsum(lengths) - lengths
    slot_ends = slot_starts + lengths
    positions = jnp.arange(pool_rows, dtype=jnp.int32)
    owned_rows = (positions[None, :] >= slot_starts[:, None]) & (
        positions[None, :] < slot_ends[:, None]
    )
    owned_rows = owned_rows[:, None, None, :]
    raw_scores = (
        jnp.einsum("rkgc,pkc->rkgp", slot_queries, keys_local, preferred_element_type=jnp.float32)
        * score_scale
    )
    weights = softmax_rounded(jnp.where(owned_rows, raw_scores, masked_score))
    attended = jnp.einsum(
        "rkgp,pkc->rkgc", weights, values_local, preferred_element_type=jnp.float32
    )
    attended = attended.astype(jnp.bfloat16).reshape(rows_dev, kv_local, per_group * head_size)
    spread = lax.all_to_all(attended, "att", split_axis=2, concat_axis=0, tiled=True)
    pieces = lax.all_gather(spread, "ffn", axis=1, tiled=True)
    inverse = (
        jnp.zeros((requests,), jnp.int32).at[assignment].set(jnp.arange(requests, dtype=jnp.int32))
    )
    request_pieces = jnp.take(pieces, inverse, axis=0)
    block = request_pieces
    projected = lax.psum_scatter(
        jnp.einsum("rkc,kcd->rd", block, out_weight, preferred_element_type=jnp.float32).astype(
            jnp.bfloat16
        ),
        "att",
        scatter_dimension=0,
        tiled=True,
    ).astype(jnp.float32)
    middle_short = (hidden_state.astype(jnp.float32) + projected).astype(jnp.bfloat16)
    middle = lax.optimization_barrier(middle_short).astype(jnp.float32)
    squares = lax.psum(jnp.sum(middle * middle, axis=1), "ffn")
    normed = (
        middle * lax.rsqrt(squares[:, None] / model_width + epsilon) * norm_gain.astype(jnp.float32)
    ).astype(jnp.bfloat16)
    every_row = lax.all_gather(normed, "att", axis=0, tiled=True)
    contract = (((1,), (1,)), ((), ()))
    gate_part = lax.dot_general(
        gate_weight, every_row, contract, preferred_element_type=jnp.float32
    )
    up_part = lax.dot_general(up_weight, every_row, contract, preferred_element_type=jnp.float32)
    totals = lax.psum(
        jnp.concatenate([gate_part, up_part], axis=1).astype(jnp.bfloat16), "ffn"
    ).astype(jnp.float32)
    unit_active = (jax.nn.silu(totals[:, :requests]) * totals[:, requests:]).astype(jnp.bfloat16)
    block = unit_active
    returned = lax.psum_scatter(
        lax.dot_general(
            block, down_weight, (((0,), (0,)), ((), ())), preferred_element_type=jnp.float32
        ).astype(jnp.bfloat16),
        "att",
        scatter_dimension=0,
        tiled=True,
    ).astype(jnp.float32)
    return (middle + returned).astype(jnp.bfloat16)


def pair_swap(value, axis, bit):
    count = lax.axis_size(axis)
    return lax.ppermute(value, axis, [(i, i ^ bit) for i in range(count)])


def up_to(value, multiple):
    return -(-value // multiple) * multiple


def params(megabytes):
    return pltpu.CompilerParams(vmem_limit_bytes=megabytes << 20)


def halves_joined(block):
    block = block.astype(F32)
    rows = block.shape[0] // 2
    return jnp.concatenate([block[:rows], block[rows:]], axis=1)


def halves_stacked(block):
    half = block.shape[1] // 2
    return jnp.concatenate([block[:, :half], block[:, half:]], axis=0)


def high_low(value):
    high = value.astype(BF16).astype(F32)
    low = value - high
    lane = lax.broadcasted_iota(I32, (value.shape[0], lanes), 1)
    return jnp.where(lane < lanes // 2, high, low)


def in_hbm(value):
    return pltpu.with_memory_space_constraint(value, pltpu.HBM)


def in_vmem(value):
    return pltpu.with_memory_space_constraint(value, pltpu.VMEM)


def job_shapes(jobs, parts):
    shapes = []
    for array, masks in jobs:
        if masks is None:
            shapes.append(pltpu.VMEM(array.shape, array.dtype))
        else:
            rows, width = array.shape
            shapes.append(pltpu.VMEM((len(masks), rows // parts, width), array.dtype))
    return shapes


def job_count(jobs):
    return sum(1 if masks is None else len(masks) for _, masks in jobs)


def job_copies(own, masks_of, sources, targets, sems):
    copies = []
    for masks, source, target in zip(masks_of, sources, targets):
        if masks is None:
            copies.append(pltpu.make_async_copy(source, target, sems.at[len(copies)]))
            continue
        rows = target.shape[1]
        for m, mask in enumerate(masks):
            at = pl.ds(pl.multiple_of((own ^ mask) * rows, rows), rows)
            copies.append(
                pltpu.make_async_copy(source.at[at], target.at[m], sems.at[len(copies)])
            )
    return copies


def masks_in(jobs):
    return tuple(masks for _, masks in jobs)


def fetch_kernel(*refs, masks_of):
    count = len(masks_of)
    own = lax.axis_index("ffn")
    copies = job_copies(own, masks_of, refs[:count], refs[count:-1], refs[-1])
    for copy in copies:
        copy.start()
    for copy in copies:
        copy.wait()


def fetch(jobs, parts):
    shapes = job_shapes(jobs, parts)
    moved = sum(2 * math.prod(shape.shape) for shape in shapes)
    return pl.pallas_call(
        functools.partial(fetch_kernel, masks_of=masks_in(jobs)),
        in_specs=[hbm] * len(jobs),
        out_specs=[vmem] * len(jobs),
        out_shape=shapes,
        scratch_shapes=[pltpu.SemaphoreType.DMA((job_count(jobs),))],
        compiler_params=params(1),
        cost_estimate=pl.CostEstimate(flops=0, bytes_accessed=2 * moved, transcendentals=0),
        name="fetch",
    )(*[in_hbm(array) for array, _ in jobs])


def folded(combine, value):
    parts = [value[:, i : i + lanes] for i in range(0, value.shape[1], lanes)]
    return functools.reduce(combine, parts)


def attention_kernel(table, *refs, slots, count, scale, unroll, masks_of):
    jobs = len(masks_of)
    query_blocks, (keys, values), sources = (
        refs[:count],
        refs[count : count + 2],
        refs[count + 2 : count + 2 + jobs],
    )
    outs, targets = (
        refs[count + 2 + jobs : 2 * count + 2 + jobs],
        refs[2 * count + 2 + jobs : 2 * count + 2 + 2 * jobs],
    )
    queries, both, begins, ends, tops, sums, scores, total, attended, items, sems = refs[
        2 * count + 2 + 2 * jobs :
    ]
    copies = job_copies(table[1], masks_of, sources, targets, sems)
    for copy in copies:
        copy.start()
    pool, width = keys.shape
    heads = queries.shape[1]
    half = heads // 2
    own = table[0]
    group_rows = slot_group * heads
    top_half = lax.broadcasted_iota(I32, (heads, lanes), 0) < half
    for k in range(count):
        queries[k * slots : (k + 1) * slots] = query_blocks[k][...]

    tops[...] = jnp.full(tops.shape, masked_score, F32)
    sums[...] = jnp.zeros(sums.shape, F32)
    total[...] = jnp.zeros(total.shape, F32)
    spare = slots * heads
    both[spare:, :] = jnp.zeros((both.shape[0] - spare, width), BF16)
    begins[spare:, :] = jnp.full((begins.shape[0] - spare, lanes), pool, I32)
    ends[spare:, :] = jnp.zeros((ends.shape[0] - spare, lanes), I32)

    def slot(s, carry):
        start, made, last_block, last_slot = carry
        end = start + table[2 + s]
        request = table[2 + slots + own * slots + s]
        owner = sum((request >= k * slots).astype(I32) for k in range(1, count))
        query = queries[(owner ^ own) * slots + request - owner * slots]
        zero = jnp.zeros_like(query)
        at = pl.ds(pl.multiple_of(s * heads, heads), heads)
        both[at, :lanes] = jnp.where(top_half, query, zero)
        both[at, lanes:] = jnp.where(top_half, zero, query)
        begins[at, :] = jnp.full((heads, lanes), start, I32)
        ends[at, :] = jnp.full((heads, lanes), end, I32)
        first = start // block_rows
        covered = (first == last_block) & (s < last_slot + slot_group)
        first = jnp.where(covered, first + 1, first)
        last = (end - 1) // block_rows

        def item(block, made):
            items[2 * made] = block
            items[2 * made + 1] = s
            return made + 1

        made_now = lax.fori_loop(first, last + 1, item, made)
        new = made_now > made
        return (
            end,
            made_now,
            jnp.where(new, last, last_block),
            jnp.where(new, s, last_slot),
        )

    none = jnp.int32(-1)
    _, made, _, _ = lax.fori_loop(0, slots, slot, (jnp.int32(0), jnp.int32(0), none, none))
    for u in range(unroll):
        items[2 * (made + u)] = 0
        items[2 * (made + u) + 1] = slots
    steps = (made + unroll - 1) // unroll
    across = lax.broadcasted_iota(I32, (group_rows, block_rows), 1)

    def place_of(i):
        block = pl.multiple_of(items[2 * i] * block_rows, block_rows)
        rows = pl.multiple_of(items[2 * i + 1] * heads, heads)
        return block, pl.ds(block, block_rows), pl.ds(rows, group_rows)

    def score_step(step, carry):
        for u in range(unroll):
            i = step * unroll + u
            block, cache, rows = place_of(i)
            raw = lax.dot_general(
                both[rows, :], keys[cache, :], contract_minor, preferred_element_type=F32
            )
            position = block + across
            begin, end = (jnp.concatenate([b[rows, :]] * (block_rows // lanes), axis=1) for b in (begins, ends))
            inside = (position >= begin) & (position < end)
            masked = jnp.where(inside, raw * scale, masked_score)
            scores[i] = masked
            tops[rows, :] = jnp.maximum(tops[rows, :], folded(jnp.maximum, masked))
        return carry

    def value_step(step, carry):
        for u in range(unroll):
            i = step * unroll + u
            _, cache, rows = place_of(i)
            top = tops[rows, :]
            shifted = jnp.exp(scores[i] - jnp.concatenate([top] * (block_rows // lanes), axis=1))
            sums[rows, :] += folded(jnp.add, shifted)
            total[rows, :] += jnp.dot(
                shifted.astype(BF16), values[cache, :], preferred_element_type=F32
            )
        return carry

    lax.fori_loop(0, steps, score_step, 0)
    top = jnp.max(tops[...], axis=1, keepdims=True)
    tops[...] = jnp.broadcast_to(top, tops.shape)
    lax.fori_loop(0, steps, value_step, 0)

    real = slots * heads
    row = lax.broadcasted_iota(I32, (real, lanes), 0)
    upper = row % heads < half
    picked = jnp.where(upper, total[:real, :lanes], total[:real, lanes:])
    attended[...] = picked / jnp.sum(sums[:real, :], axis=1, keepdims=True)
    per_block = half // count
    for k in range(count):
        outs[k][...] = jnp.zeros(outs[k].shape, BF16)
        for kv in range(2):
            for j in range(per_block):
                head = kv * half + (own ^ k) * per_block + j
                at = (kv * per_block + j) * lanes
                outs[k][:slots, at : at + lanes] = attended[
                    pl.ds(head, slots, stride=heads), :
                ].astype(BF16)
    for copy in copies:
        copy.wait()


def attention(table, query_blocks, keys, values, jobs, parts, unroll=8):
    count = len(query_blocks)
    slots, heads, _ = query_blocks[0].shape
    pool, width = keys.shape
    most = pool // block_rows + slots + unroll
    rows = (slots + slot_group) * heads
    return pl.pallas_call(
        functools.partial(
            attention_kernel,
            slots=slots,
            count=count,
            scale=1.0 / math.sqrt(lanes),
            unroll=unroll,
            masks_of=masks_in(jobs),
        ),
        in_specs=[smem] + [vmem] * (count + 2) + [hbm] * len(jobs),
        out_specs=[vmem] * (count + len(jobs)),
        out_shape=[jax.ShapeDtypeStruct((up_to(slots, 8), heads // count * lanes), BF16)] * count
        + job_shapes(jobs, parts),
        scratch_shapes=[
            pltpu.VMEM((count * slots, heads, lanes), BF16),
            pltpu.VMEM((rows, width), BF16),
            pltpu.VMEM((rows, lanes), I32),
            pltpu.VMEM((rows, lanes), I32),
            pltpu.VMEM((rows, lanes), F32),
            pltpu.VMEM((rows, lanes), F32),
            pltpu.VMEM((most, slot_group * heads, block_rows), F32),
            pltpu.VMEM((rows, width), F32),
            pltpu.VMEM((slots * heads, lanes), F32),
            pltpu.SMEM((2 * most,), I32),
            pltpu.SemaphoreType.DMA((job_count(jobs),)),
        ],
        compiler_params=params(6),
        cost_estimate=pl.CostEstimate(
            flops=4 * pool * heads * lanes, bytes_accessed=pool * width * 4, transcendentals=0
        ),
        name="attention",
    )(
        table,
        *query_blocks,
        in_vmem(keys),
        in_vmem(values),
        *[in_hbm(array) for array, _ in jobs],
    )


def selection_kernel(served, source, target, choose, sems, *, slots, count, masks_of):
    copies = job_copies(lax.axis_index("ffn"), masks_of, [source], [target], sems)
    for copy in copies:
        copy.start()
    own = lax.axis_index("att")
    requests, padded = choose.shape[1:]
    row = lax.broadcasted_iota(I32, (requests, padded), 0)
    wanted = row
    for k in range(count):
        moved = row + ((own ^ k) - k) * slots
        wanted = jnp.where((row >= k * slots) & (row < (k + 1) * slots), moved, wanted)
    lane = lax.broadcasted_iota(I32, (1, padded), 1)
    for k in range(count):
        turn = (count - (own ^ k)) * slots
        first = pltpu.roll(served[...], lax.rem(turn + lanes - count * slots, lanes), 1)
        request = jnp.where(lane < slots, first[:1, :padded], -1)
        choose[k] = (wanted == request).astype(F32).astype(BF16)
    for copy in copies:
        copy.wait()


def selection(served, jobs, parts, slots, padded, count):
    shapes = job_shapes(jobs, parts)
    moved = sum(2 * math.prod(shape.shape) for shape in shapes)
    return pl.pallas_call(
        functools.partial(
            selection_kernel, slots=slots, count=count, masks_of=masks_in(jobs)
        ),
        in_specs=[vmem, hbm],
        out_specs=[vmem] * 2,
        out_shape=shapes + [jax.ShapeDtypeStruct((count, slots * count, padded), BF16)],
        scratch_shapes=[pltpu.SemaphoreType.DMA((job_count(jobs),))],
        compiler_params=params(1),
        cost_estimate=pl.CostEstimate(flops=0, bytes_accessed=2 * moved, transcendentals=0),
        name="selection",
    )(served, in_hbm(jobs[0][0]))


def ordered_kernel(choose, *refs):
    blocks, out = refs[:-1], refs[-1]
    total = None
    for k, block in enumerate(blocks):
        term = jnp.dot(choose[k], block[...], preferred_element_type=F32)
        total = term if total is None else total + term
    out[...] = total.astype(BF16)


def ordered(choose, blocks):
    return pl.pallas_call(
        ordered_kernel,
        in_specs=[vmem] * (1 + len(blocks)),
        out_specs=vmem,
        out_shape=jax.ShapeDtypeStruct((choose.shape[1], blocks[0].shape[1]), BF16),
        compiler_params=params(2),
        name="ordered",
    )(choose, *blocks)


def projection_kernel(*refs, slots, parts):
    pieces, weight, outs = refs[:parts], refs[parts], refs[parts + 1 :]
    total = None
    for p in range(parts):
        term = jnp.dot(pieces[p][...], weight[p], preferred_element_type=F32)
        total = term if total is None else total + term
    for k, out in enumerate(outs):
        out[...] = halves_stacked(total[k * slots : (k + 1) * slots]).astype(BF16)


def projection(pieces, weight, slots, count):
    parts, depth, width = weight.shape
    return pl.pallas_call(
        functools.partial(projection_kernel, slots=slots, parts=parts),
        in_specs=[vmem] * (1 + parts),
        out_specs=[vmem] * count,
        out_shape=[jax.ShapeDtypeStruct((2 * slots, width // 2), BF16)] * count,
        compiler_params=params(2),
        cost_estimate=pl.CostEstimate(
            flops=2 * slots * count * parts * depth * width,
            bytes_accessed=parts * depth * width,
            transcendentals=0,
        ),
        name="projection",
    )(*pieces, in_vmem(weight))


def residual_kernel(*refs, joined):
    base, blocks, out = refs[0], refs[1:-1], refs[-1]
    total = base[...].astype(F32)
    if not joined:
        total = halves_stacked(total)
    for block in blocks:
        total = total + block[...].astype(F32)
    out[...] = (halves_joined(total) if joined else total).astype(BF16)


def residual(base, blocks, joined):
    rows, half = blocks[0].shape
    shape = (rows // 2, 2 * half) if joined else (rows, half)
    return pl.pallas_call(
        functools.partial(residual_kernel, joined=joined),
        in_specs=[vmem] * (1 + len(blocks)),
        out_specs=vmem,
        out_shape=jax.ShapeDtypeStruct(shape, BF16),
        compiler_params=params(2),
        name="residual",
    )(base, *blocks)


def unit_product(scaled, weight, part):
    return lax.dot_general(scaled, weight[part], contract_minor, preferred_element_type=F32)


def product_cost(requests, units, width):
    return pl.CostEstimate(
        flops=2 * requests * units * width, bytes_accessed=units * width, transcendentals=0
    )


def hidden_first_kernel(*refs, count, part):
    blocks, (gain, weight, send, scaled, squares, joined) = refs[:count], refs[count:]
    rows = blocks[0].shape[0] // 2
    for k in range(count):
        joined[k * rows : (k + 1) * rows, :] = halves_joined(blocks[k][...])
    middle = joined[...]
    square = jnp.sum(middle * middle, axis=1, keepdims=True)
    scaled[...] = (middle * gain[...].astype(F32)).astype(BF16)
    units = weight.shape[1]
    send[:, :units] = unit_product(scaled[...], weight, part).astype(BF16)
    send[:, units:] = high_low(square).astype(BF16)
    squares[...] = jnp.broadcast_to(square, squares.shape)


def hidden_first(blocks, gain, weight, part):
    count = len(blocks)
    rows, half = blocks[0].shape
    requests, width = rows // 2 * count, 2 * half
    units = weight.shape[1]
    return pl.pallas_call(
        functools.partial(hidden_first_kernel, count=count, part=part),
        in_specs=[vmem] * (count + 2),
        out_specs=[vmem] * 3,
        out_shape=[
            jax.ShapeDtypeStruct((requests, units + lanes), BF16),
            jax.ShapeDtypeStruct((requests, width), BF16),
            jax.ShapeDtypeStruct((requests, lanes), F32),
        ],
        scratch_shapes=[pltpu.VMEM((requests, width), F32)],
        compiler_params=params(2),
        cost_estimate=product_cost(requests, units, width),
        name="hidden_first",
    )(*blocks, gain, in_vmem(weight))


def hidden_kernel(scaled, *refs, parts):
    weights, out = refs[:-1], refs[-1]
    for t, (weight, part) in enumerate(zip(weights, parts)):
        units = weight.shape[1]
        out[:, t * units : (t + 1) * units] = unit_product(scaled[...], weight, part).astype(
            out.dtype
        )


def hidden_next(scaled, chosen, kind):
    requests, width = scaled.shape
    units = chosen[0][0].shape[1]
    return pl.pallas_call(
        functools.partial(hidden_kernel, parts=tuple(part for _, part in chosen)),
        in_specs=[vmem] * (1 + len(chosen)),
        out_specs=vmem,
        out_shape=jax.ShapeDtypeStruct((requests, len(chosen) * units), kind),
        compiler_params=params(2),
        cost_estimate=product_cost(requests, len(chosen) * units, width),
        name="hidden_next",
    )(scaled, *[in_vmem(weight) for weight, _ in chosen])


def squares_sum_kernel(keep, own_squares, arrived, out, squares):
    width = keep.shape[1]
    out[:, :width] = (keep[...] + arrived[:, :width].astype(F32)).astype(BF16)
    tail = arrived[:, width:].astype(F32)
    chip = own_squares[...] + (tail[:, :1] + tail[:, lanes // 2 : lanes // 2 + 1])
    squares[...] = chip
    out[:, width:] = high_low(chip).astype(BF16)


def squares_sum(keep, own_squares, arrived):
    requests, width = arrived.shape
    return pl.pallas_call(
        squares_sum_kernel,
        in_specs=[vmem] * 3,
        out_specs=[vmem] * 2,
        out_shape=[
            jax.ShapeDtypeStruct((requests, width), BF16),
            jax.ShapeDtypeStruct((requests, lanes), F32),
        ],
        compiler_params=params(2),
        name="squares_sum",
    )(keep, own_squares, arrived)


def chip_sum_kernel(keep, arrived, out):
    out[...] = (keep[...] + arrived[...].astype(F32)).astype(BF16)


def chip_sum(keep, arrived):
    return pl.pallas_call(
        chip_sum_kernel,
        in_specs=[vmem] * 2,
        out_specs=vmem,
        out_shape=jax.ShapeDtypeStruct(arrived.shape, BF16),
        compiler_params=params(2),
        name="chip_sum",
    )(keep, arrived)


def active_kernel(near, beside, far_gate, far_up, squares, out, *, model_width):
    units = far_up.shape[1]
    tail = far_gate[:, units:].astype(F32)
    square = squares[:, :1] + (tail[:, :1] + tail[:, lanes // 2 : lanes // 2 + 1])
    scale = lax.rsqrt(square / model_width + epsilon)

    def total(at, far):
        both = near[:, at : at + units] + beside[:, at : at + units].astype(F32)
        return (both + far.astype(F32)) * scale

    gate = total(0, far_gate[:, :units])
    out[...] = (gate / (1.0 + jnp.exp(-gate)) * total(units, far_up[...])).astype(BF16)


def active_units(near, beside, far_gate, far_up, squares, model_width):
    requests, width = near.shape
    return pl.pallas_call(
        functools.partial(active_kernel, model_width=model_width),
        in_specs=[vmem] * 5,
        out_specs=vmem,
        out_shape=jax.ShapeDtypeStruct((requests, width // 2), BF16),
        compiler_params=params(2),
        name="active",
    )(near, beside, far_gate, far_up, squares)


def down_kernel(*refs, parts, count, first, last):
    terms = len(parts)
    pieces, weights, rest = refs[:terms], refs[terms : 2 * terms], refs[2 * terms :]
    total = None if first else rest[0][...]
    outs = rest if first else rest[1:]
    for piece, weight, part in zip(pieces, weights, parts):
        term = jnp.dot(piece[...], weight[part], preferred_element_type=F32)
        total = term if total is None else total + term
    if last:
        rows = total.shape[0] // count
        for k in range(count):
            outs[k][...] = halves_stacked(total[k * rows : (k + 1) * rows]).astype(BF16)
    else:
        outs[0][...] = total


def down_part(chosen, count, before, last):
    requests, units = chosen[0][0].shape
    width = chosen[0][1].shape[2]
    if last:
        outs = [jax.ShapeDtypeStruct((2 * requests // count, width // 2), BF16)] * count
    else:
        outs = [jax.ShapeDtypeStruct((requests, width), F32)]
    before = [] if before is None else [before]
    return pl.pallas_call(
        functools.partial(
            down_kernel,
            parts=tuple(part for _, _, part in chosen),
            count=count,
            first=not before,
            last=last,
        ),
        in_specs=[vmem] * (2 * len(chosen) + len(before)),
        out_specs=[vmem] * len(outs),
        out_shape=outs,
        compiler_params=params(2),
        cost_estimate=product_cost(requests, len(chosen) * units, width),
        name="down",
    )(*[piece for piece, _, _ in chosen], *[in_vmem(w) for _, w, _ in chosen], *before)


def swaps_of(blocks):
    count = len(blocks)
    arrived = {k: pair_swap(blocks[k], "att", k) for k in reversed(range(1, count))}
    return [blocks[0]] + [arrived[k] for k in range(1, count)]


def exchanging_device(*args):
    return exchanging_layer(*args)


def exchanging_layer(
    hidden_state,
    queries,
    key_cache,
    value_cache,
    lengths,
    assignment,
    out_weight,
    norm_gain,
    gate_weight,
    up_weight,
    down_weight,
):
    slots, columns = hidden_state.shape
    count = lax.axis_size("att")
    parts = lax.axis_size("ffn")
    model_width = columns * parts
    heads = queries.shape[1] // lanes
    own = jnp.stack([lax.axis_index("att"), lax.axis_index("ffn")]).astype(I32)
    table = jnp.concatenate([own, lengths, assignment])
    served = jnp.pad(assignment, (0, lanes - assignment.shape[0]))
    served = lax.broadcast_in_dim(served, (8, lanes), (1,))

    own_queries = queries.reshape(slots, heads, lanes)
    query_blocks = swaps_of([own_queries] * count)
    keys, values = fetch([(key_cache, None), (value_cache, None)], parts)
    jobs = [(out_weight.reshape(-1, columns), (0, 1, 2, 3)), (down_weight, (0, 1))]
    *blocks, project, down_near = attention(table, query_blocks, keys, values, jobs, parts)

    blocks = swaps_of(blocks)
    padded = blocks[0].shape[0]
    jobs = [(up_weight, (3,))]
    up_corner, choose = selection(served, jobs, parts, slots, padded, count)
    piece = ordered(choose, blocks)
    across = pair_swap(piece, "ffn", 2)
    beside = pair_swap(piece, "ffn", 1)
    corner = pair_swap(across, "ffn", 1)
    (down_far,) = fetch([(down_weight, (2, 3))], parts)
    gain = norm_gain.reshape(1, columns)
    partial = projection([piece, beside, across, corner], project, slots, count)
    (gate,) = fetch([(gate_weight, (0, 1, 2, 3))], parts)
    middle = residual(hidden_state, swaps_of(partial), False)

    rows = swaps_of([middle] * count)
    (up,) = fetch([(up_weight, (0, 1, 2))], parts)
    send, scaled, squares = hidden_first(rows, gain, gate, 3)
    arrived = pair_swap(send, "ffn", 1)
    keep = hidden_next(scaled, [(gate, 2)], F32)
    far_gate, squares = squares_sum(keep, squares, arrived)
    far_gate = pair_swap(far_gate, "ffn", 2)
    send = hidden_next(scaled, [(up_corner, 0)], BF16)
    arrived = pair_swap(send, "ffn", 1)
    keep = hidden_next(scaled, [(up, 2)], F32)
    far_up = pair_swap(chip_sum(keep, arrived), "ffn", 2)
    send = hidden_next(scaled, [(gate, 1), (up, 1)], BF16)
    arrived = pair_swap(send, "ffn", 1)
    keep = hidden_next(scaled, [(gate, 0), (up, 0)], F32)
    active = active_units(keep, arrived, far_gate, far_up, squares, model_width)

    across = pair_swap(active, "ffn", 2)
    beside = pair_swap(active, "ffn", 1)
    chosen = [(active, down_near, 0), (beside, down_near, 1)]
    (before,) = down_part(chosen, count, None, False)
    corner = pair_swap(across, "ffn", 1)
    (before,) = down_part([(across, down_far, 0)], count, before, False)
    partial = down_part([(corner, down_far, 1)], count, before, True)
    return residual(middle, swaps_of(partial), True)


def solution(mesh):
    count, parts = mesh.shape["att"], mesh.shape["ffn"]
    paired = count == 4 and parts == 4
    in_specs = (
        P(("group", "att"), "ffn"),
        P(("group", "att"), "ffn"),
        P(("group", "att"), "ffn"),
        P(("group", "att"), "ffn"),
        P(("group", "att")),
        P("group"),
        P(None, "att", "ffn"),
        P("ffn"),
        P("att", "ffn"),
        P("att", "ffn"),
        P("att", "ffn"),
    )
    out_specs = P(("group", "att"), "ffn")
    return jax.shard_map(
        exchanging_device if paired else general_device,
        mesh=mesh,
        in_specs=in_specs,
        out_specs=out_specs,
        check_vma=False,
    )
```

```python
import functools
import math

import jax
import jax.numpy as jnp
from jax import lax
from jax.experimental import pallas as pl
from jax.experimental.pallas import tpu as pltpu
from jax.sharding import PartitionSpec as P

epsilon = 1e-05
masked_score = -1e30
lanes = 128
block_rows = 256
max_context = 1279
most_blocks = (max_context + block_rows - 2) // block_rows + 1
slot_group = 2
contract_minor = (((1,), (1,)), ((), ()))
F32 = jnp.float32
BF16 = jnp.bfloat16
I32 = jnp.int32
vmem = pl.BlockSpec(memory_space=pltpu.VMEM)
smem = pl.BlockSpec(memory_space=pltpu.SMEM)
hbm = pl.BlockSpec(memory_space=pltpu.HBM)


def softmax_rounded(scores):
    row_top = jnp.max(scores, axis=-1, keepdims=True)
    shifted = jnp.exp(scores - row_top)
    totals = jnp.sum(shifted, axis=-1, keepdims=True)
    return (shifted / totals).astype(jnp.bfloat16)


def general_device(
    hidden_state,
    queries,
    key_cache,
    value_cache,
    lengths,
    assignment,
    out_weight,
    norm_gain,
    gate_weight,
    up_weight,
    down_weight,
):
    rows_dev = hidden_state.shape[0]
    columns = hidden_state.shape[1]
    att_count = lax.axis_size("att")
    ffn_count = lax.axis_size("ffn")
    requests = rows_dev * att_count
    kv_total = out_weight.shape[0]
    kv_local = kv_total // ffn_count
    model_width = columns * ffn_count
    pool_rows = key_cache.shape[0]
    head_size = key_cache.shape[1] // kv_local
    per_group = queries.shape[1] // (kv_local * head_size)
    score_scale = 1.0 / math.sqrt(head_size)
    att_place = lax.axis_index("att")
    every_query = lax.all_gather(queries, "att", axis=0, tiled=True)
    own_slots = lax.dynamic_slice_in_dim(assignment, att_place * rows_dev, rows_dev)
    slot_queries = jnp.take(every_query, own_slots, axis=0).reshape(
        rows_dev, kv_local, per_group, head_size
    )
    keys_local = key_cache.reshape(pool_rows, kv_local, head_size)
    values_local = value_cache.reshape(pool_rows, kv_local, head_size)
    slot_starts = jnp.cumsum(lengths) - lengths
    slot_ends = slot_starts + lengths
    positions = jnp.arange(pool_rows, dtype=jnp.int32)
    owned_rows = (positions[None, :] >= slot_starts[:, None]) & (
        positions[None, :] < slot_ends[:, None]
    )
    owned_rows = owned_rows[:, None, None, :]
    raw_scores = (
        jnp.einsum("rkgc,pkc->rkgp", slot_queries, keys_local, preferred_element_type=jnp.float32)
        * score_scale
    )
    weights = softmax_rounded(jnp.where(owned_rows, raw_scores, masked_score))
    attended = jnp.einsum(
        "rkgp,pkc->rkgc", weights, values_local, preferred_element_type=jnp.float32
    )
    attended = attended.astype(jnp.bfloat16).reshape(rows_dev, kv_local, per_group * head_size)
    spread = lax.all_to_all(attended, "att", split_axis=2, concat_axis=0, tiled=True)
    pieces = lax.all_gather(spread, "ffn", axis=1, tiled=True)
    inverse = (
        jnp.zeros((requests,), jnp.int32).at[assignment].set(jnp.arange(requests, dtype=jnp.int32))
    )
    request_pieces = jnp.take(pieces, inverse, axis=0)
    block = request_pieces
    projected = lax.psum_scatter(
        jnp.einsum("rkc,kcd->rd", block, out_weight, preferred_element_type=jnp.float32).astype(
            jnp.bfloat16
        ),
        "att",
        scatter_dimension=0,
        tiled=True,
    ).astype(jnp.float32)
    middle_short = (hidden_state.astype(jnp.float32) + projected).astype(jnp.bfloat16)
    middle = lax.optimization_barrier(middle_short).astype(jnp.float32)
    squares = lax.psum(jnp.sum(middle * middle, axis=1), "ffn")
    normed = (
        middle * lax.rsqrt(squares[:, None] / model_width + epsilon) * norm_gain.astype(jnp.float32)
    ).astype(jnp.bfloat16)
    every_row = lax.all_gather(normed, "att", axis=0, tiled=True)
    contract = (((1,), (1,)), ((), ()))
    gate_part = lax.dot_general(
        gate_weight, every_row, contract, preferred_element_type=jnp.float32
    )
    up_part = lax.dot_general(up_weight, every_row, contract, preferred_element_type=jnp.float32)
    totals = lax.psum(
        jnp.concatenate([gate_part, up_part], axis=1).astype(jnp.bfloat16), "ffn"
    ).astype(jnp.float32)
    unit_active = (jax.nn.silu(totals[:, :requests]) * totals[:, requests:]).astype(jnp.bfloat16)
    block = unit_active
    returned = lax.psum_scatter(
        lax.dot_general(
            block, down_weight, (((0,), (0,)), ((), ())), preferred_element_type=jnp.float32
        ).astype(jnp.bfloat16),
        "att",
        scatter_dimension=0,
        tiled=True,
    ).astype(jnp.float32)
    return (middle + returned).astype(jnp.bfloat16)


def pair_swap(value, axis, bit):
    count = lax.axis_size(axis)
    return lax.ppermute(value, axis, [(i, i ^ bit) for i in range(count)])


def up_to(value, multiple):
    return -(-value // multiple) * multiple


def params(megabytes):
    return pltpu.CompilerParams(vmem_limit_bytes=megabytes << 20)


def halves_joined(block):
    block = block.astype(F32)
    rows = block.shape[0] // 2
    return jnp.concatenate([block[:rows], block[rows:]], axis=1)


def halves_stacked(block):
    half = block.shape[1] // 2
    return jnp.concatenate([block[:, :half], block[:, half:]], axis=0)


def high_low(value):
    high = value.astype(BF16).astype(F32)
    low = value - high
    lane = lax.broadcasted_iota(I32, (value.shape[0], lanes), 1)
    return jnp.where(lane < lanes // 2, high, low)


def in_hbm(value):
    return pltpu.with_memory_space_constraint(value, pltpu.HBM)


def in_vmem(value):
    return pltpu.with_memory_space_constraint(value, pltpu.VMEM)


def job_shapes(jobs, parts):
    shapes = []
    for array, masks in jobs:
        if masks is None:
            shapes.append(pltpu.VMEM(array.shape, array.dtype))
        else:
            rows, width = array.shape
            shapes.append(pltpu.VMEM((len(masks), rows // parts, width), array.dtype))
    return shapes


def job_count(jobs):
    return sum(1 if masks is None else len(masks) for _, masks in jobs)


def job_copies(own, masks_of, sources, targets, sems):
    copies = []
    for masks, source, target in zip(masks_of, sources, targets):
        if masks is None:
            copies.append(pltpu.make_async_copy(source, target, sems.at[len(copies)]))
            continue
        rows = target.shape[1]
        for m, mask in enumerate(masks):
            at = pl.ds(pl.multiple_of((own ^ mask) * rows, rows), rows)
            copies.append(
                pltpu.make_async_copy(source.at[at], target.at[m], sems.at[len(copies)])
            )
    return copies


def masks_in(jobs):
    return tuple(masks for _, masks in jobs)


def fetch_kernel(*refs, masks_of):
    count = len(masks_of)
    own = lax.axis_index("ffn")
    copies = job_copies(own, masks_of, refs[:count], refs[count:-1], refs[-1])
    for copy in copies:
        copy.start()
    for copy in copies:
        copy.wait()


def fetch(jobs, parts):
    shapes = job_shapes(jobs, parts)
    moved = sum(2 * math.prod(shape.shape) for shape in shapes)
    return pl.pallas_call(
        functools.partial(fetch_kernel, masks_of=masks_in(jobs)),
        in_specs=[hbm] * len(jobs),
        out_specs=[vmem] * len(jobs),
        out_shape=shapes,
        scratch_shapes=[pltpu.SemaphoreType.DMA((job_count(jobs),))],
        compiler_params=params(1),
        cost_estimate=pl.CostEstimate(flops=0, bytes_accessed=2 * moved, transcendentals=0),
        name="fetch",
    )(*[in_hbm(array) for array, _ in jobs])


def folded(combine, value):
    parts = [value[:, i : i + lanes] for i in range(0, value.shape[1], lanes)]
    return functools.reduce(combine, parts)


def attention_kernel(table, *refs, slots, count, scale, unroll, masks_of):
    jobs = len(masks_of)
    query_blocks, (keys, values), sources = (
        refs[:count],
        refs[count : count + 2],
        refs[count + 2 : count + 2 + jobs],
    )
    outs, targets = (
        refs[count + 2 + jobs : 2 * count + 2 + jobs],
        refs[2 * count + 2 + jobs : 2 * count + 2 + 2 * jobs],
    )
    queries, both, begins, ends, tops, sums, scores, total, attended, items, sems = refs[
        2 * count + 2 + 2 * jobs :
    ]
    copies = job_copies(table[1], masks_of, sources, targets, sems)
    for copy in copies:
        copy.start()
    pool, width = keys.shape
    heads = queries.shape[1]
    half = heads // 2
    own = table[0]
    group_rows = slot_group * heads
    top_half = lax.broadcasted_iota(I32, (heads, lanes), 0) < half
    for k in range(count):
        queries[k * slots : (k + 1) * slots] = query_blocks[k][...]

    tops[...] = jnp.full(tops.shape, masked_score, F32)
    sums[...] = jnp.zeros(sums.shape, F32)
    total[...] = jnp.zeros(total.shape, F32)
    spare = slots * heads
    both[spare:, :] = jnp.zeros((both.shape[0] - spare, width), BF16)
    begins[spare:, :] = jnp.full((begins.shape[0] - spare, lanes), pool, I32)
    ends[spare:, :] = jnp.zeros((ends.shape[0] - spare, lanes), I32)

    def slot(s, carry):
        start, made, last_block, last_slot = carry
        end = start + table[2 + s]
        request = table[2 + slots + own * slots + s]
        owner = sum((request >= k * slots).astype(I32) for k in range(1, count))
        query = queries[(owner ^ own) * slots + request - owner * slots]
        zero = jnp.zeros_like(query)
        at = pl.ds(pl.multiple_of(s * heads, heads), heads)
        both[at, :lanes] = jnp.where(top_half, query, zero)
        both[at, lanes:] = jnp.where(top_half, zero, query)
        begins[at, :] = jnp.full((heads, lanes), start, I32)
        ends[at, :] = jnp.full((heads, lanes), end, I32)
        first = start // block_rows
        covered = (first == last_block) & (s < last_slot + slot_group)
        first = jnp.where(covered, first + 1, first)
        last = (end - 1) // block_rows

        for j in range(most_blocks):
            items[2 * (made + j)] = first + j
            items[2 * (made + j) + 1] = s
        made_now = made + jnp.maximum(last + 1 - first, 0)
        new = made_now > made
        return (
            end,
            made_now,
            jnp.where(new, last, last_block),
            jnp.where(new, s, last_slot),
        )

    none = jnp.int32(-1)
    start = (jnp.int32(0), jnp.int32(0), none, none)
    _, made, _, _ = lax.fori_loop(0, slots, slot, start, unroll=True)
    for u in range(unroll):
        items[2 * (made + u)] = 0
        items[2 * (made + u) + 1] = slots
    steps = (made + unroll - 1) // unroll
    across = lax.broadcasted_iota(I32, (group_rows, block_rows), 1)

    def place_of(i):
        block = pl.multiple_of(items[2 * i] * block_rows, block_rows)
        rows = pl.multiple_of(items[2 * i + 1] * heads, heads)
        return block, pl.ds(block, block_rows), pl.ds(rows, group_rows)

    def score_step(step, carry):
        for u in range(unroll):
            i = step * unroll + u
            block, cache, rows = place_of(i)
            raw = lax.dot_general(
                both[rows, :], keys[cache, :], contract_minor, preferred_element_type=F32
            )
            position = block + across
            begin, end = (jnp.concatenate([b[rows, :]] * (block_rows // lanes), axis=1) for b in (begins, ends))
            inside = (position >= begin) & (position < end)
            masked = jnp.where(inside, raw * scale, masked_score)
            scores[i] = masked
            tops[rows, :] = jnp.maximum(tops[rows, :], folded(jnp.maximum, masked))
        return carry

    def value_step(step, carry):
        for u in range(unroll):
            i = step * unroll + u
            _, cache, rows = place_of(i)
            top = tops[rows, :]
            shifted = jnp.exp(scores[i] - jnp.concatenate([top] * (block_rows // lanes), axis=1))
            sums[rows, :] += folded(jnp.add, shifted)
            total[rows, :] += jnp.dot(
                shifted.astype(BF16), values[cache, :], preferred_element_type=F32
            )
        return carry

    lax.fori_loop(0, steps, score_step, 0)
    top = jnp.max(tops[...], axis=1, keepdims=True)
    tops[...] = jnp.broadcast_to(top, tops.shape)
    lax.fori_loop(0, steps, value_step, 0)

    real = slots * heads
    row = lax.broadcasted_iota(I32, (real, lanes), 0)
    upper = row % heads < half
    picked = jnp.where(upper, total[:real, :lanes], total[:real, lanes:])
    attended[...] = picked / jnp.sum(sums[:real, :], axis=1, keepdims=True)
    per_block = half // count
    for k in range(count):
        outs[k][...] = jnp.zeros(outs[k].shape, BF16)
        for kv in range(2):
            for j in range(per_block):
                head = kv * half + (own ^ k) * per_block + j
                at = (kv * per_block + j) * lanes
                outs[k][:slots, at : at + lanes] = attended[
                    pl.ds(head, slots, stride=heads), :
                ].astype(BF16)
    for copy in copies:
        copy.wait()


def attention(table, query_blocks, keys, values, jobs, parts, unroll=14):
    count = len(query_blocks)
    slots, heads, _ = query_blocks[0].shape
    pool, width = keys.shape
    most = pool // block_rows + slots + max(unroll, most_blocks)
    rows = (slots + slot_group) * heads
    return pl.pallas_call(
        functools.partial(
            attention_kernel,
            slots=slots,
            count=count,
            scale=1.0 / math.sqrt(lanes),
            unroll=unroll,
            masks_of=masks_in(jobs),
        ),
        in_specs=[smem] + [vmem] * (count + 2) + [hbm] * len(jobs),
        out_specs=[vmem] * (count + len(jobs)),
        out_shape=[jax.ShapeDtypeStruct((up_to(slots, 8), heads // count * lanes), BF16)] * count
        + job_shapes(jobs, parts),
        scratch_shapes=[
            pltpu.VMEM((count * slots, heads, lanes), BF16),
            pltpu.VMEM((rows, width), BF16),
            pltpu.VMEM((rows, lanes), I32),
            pltpu.VMEM((rows, lanes), I32),
            pltpu.VMEM((rows, lanes), F32),
            pltpu.VMEM((rows, lanes), F32),
            pltpu.VMEM((most, slot_group * heads, block_rows), F32),
            pltpu.VMEM((rows, width), F32),
            pltpu.VMEM((slots * heads, lanes), F32),
            pltpu.SMEM((2 * most,), I32),
            pltpu.SemaphoreType.DMA((job_count(jobs),)),
        ],
        compiler_params=params(6),
        cost_estimate=pl.CostEstimate(
            flops=4 * pool * heads * lanes, bytes_accessed=pool * width * 4, transcendentals=0
        ),
        name="attention",
    )(
        table,
        *query_blocks,
        in_vmem(keys),
        in_vmem(values),
        *[in_hbm(array) for array, _ in jobs],
    )


def selection_kernel(served, source, target, choose, sems, *, slots, count, masks_of):
    copies = job_copies(lax.axis_index("ffn"), masks_of, [source], [target], sems)
    for copy in copies:
        copy.start()
    own = lax.axis_index("att")
    requests, padded = choose.shape[1:]
    row = lax.broadcasted_iota(I32, (requests, padded), 0)
    wanted = row
    for k in range(count):
        moved = row + ((own ^ k) - k) * slots
        wanted = jnp.where((row >= k * slots) & (row < (k + 1) * slots), moved, wanted)
    lane = lax.broadcasted_iota(I32, (1, padded), 1)
    for k in range(count):
        turn = (count - (own ^ k)) * slots
        first = pltpu.roll(served[...], lax.rem(turn + lanes - count * slots, lanes), 1)
        request = jnp.where(lane < slots, first[:1, :padded], -1)
        choose[k] = (wanted == request).astype(F32).astype(BF16)
    for copy in copies:
        copy.wait()


def selection(served, jobs, parts, slots, padded, count):
    shapes = job_shapes(jobs, parts)
    moved = sum(2 * math.prod(shape.shape) for shape in shapes)
    return pl.pallas_call(
        functools.partial(
            selection_kernel, slots=slots, count=count, masks_of=masks_in(jobs)
        ),
        in_specs=[vmem, hbm],
        out_specs=[vmem] * 2,
        out_shape=shapes + [jax.ShapeDtypeStruct((count, slots * count, padded), BF16)],
        scratch_shapes=[pltpu.SemaphoreType.DMA((job_count(jobs),))],
        compiler_params=params(1),
        cost_estimate=pl.CostEstimate(flops=0, bytes_accessed=2 * moved, transcendentals=0),
        name="selection",
    )(served, in_hbm(jobs[0][0]))


def ordered_kernel(choose, *refs):
    blocks, out = refs[:-1], refs[-1]
    total = None
    for k, block in enumerate(blocks):
        term = jnp.dot(choose[k], block[...], preferred_element_type=F32)
        total = term if total is None else total + term
    out[...] = total.astype(BF16)


def ordered(choose, blocks):
    return pl.pallas_call(
        ordered_kernel,
        in_specs=[vmem] * (1 + len(blocks)),
        out_specs=vmem,
        out_shape=jax.ShapeDtypeStruct((choose.shape[1], blocks[0].shape[1]), BF16),
        compiler_params=params(2),
        name="ordered",
    )(choose, *blocks)


def projection_kernel(*refs, slots, parts):
    pieces, weight, outs = refs[:parts], refs[parts], refs[parts + 1 :]
    total = None
    for p in range(parts):
        term = jnp.dot(pieces[p][...], weight[p], preferred_element_type=F32)
        total = term if total is None else total + term
    for k, out in enumerate(outs):
        out[...] = halves_stacked(total[k * slots : (k + 1) * slots]).astype(BF16)


def projection(pieces, weight, slots, count):
    parts, depth, width = weight.shape
    return pl.pallas_call(
        functools.partial(projection_kernel, slots=slots, parts=parts),
        in_specs=[vmem] * (1 + parts),
        out_specs=[vmem] * count,
        out_shape=[jax.ShapeDtypeStruct((2 * slots, width // 2), BF16)] * count,
        compiler_params=params(2),
        cost_estimate=pl.CostEstimate(
            flops=2 * slots * count * parts * depth * width,
            bytes_accessed=parts * depth * width,
            transcendentals=0,
        ),
        name="projection",
    )(*pieces, in_vmem(weight))


def residual_kernel(*refs, joined):
    base, blocks, out = refs[0], refs[1:-1], refs[-1]
    total = base[...].astype(F32)
    if not joined:
        total = halves_stacked(total)
    for block in blocks:
        total = total + block[...].astype(F32)
    out[...] = (halves_joined(total) if joined else total).astype(BF16)


def residual(base, blocks, joined):
    rows, half = blocks[0].shape
    shape = (rows // 2, 2 * half) if joined else (rows, half)
    return pl.pallas_call(
        functools.partial(residual_kernel, joined=joined),
        in_specs=[vmem] * (1 + len(blocks)),
        out_specs=vmem,
        out_shape=jax.ShapeDtypeStruct(shape, BF16),
        compiler_params=params(2),
        name="residual",
    )(base, *blocks)


def unit_product(scaled, weight, part):
    return lax.dot_general(scaled, weight[part], contract_minor, preferred_element_type=F32)


def product_cost(requests, units, width):
    return pl.CostEstimate(
        flops=2 * requests * units * width, bytes_accessed=units * width, transcendentals=0
    )


def hidden_first_kernel(*refs, count, part):
    blocks, (gain, weight, send, scaled, squares, joined) = refs[:count], refs[count:]
    rows = blocks[0].shape[0] // 2
    for k in range(count):
        joined[k * rows : (k + 1) * rows, :] = halves_joined(blocks[k][...])
    middle = joined[...]
    square = jnp.sum(middle * middle, axis=1, keepdims=True)
    scaled[...] = (middle * gain[...].astype(F32)).astype(BF16)
    units = weight.shape[1]
    send[:, :units] = unit_product(scaled[...], weight, part).astype(BF16)
    send[:, units:] = high_low(square).astype(BF16)
    squares[...] = jnp.broadcast_to(square, squares.shape)


def hidden_first(blocks, gain, weight, part):
    count = len(blocks)
    rows, half = blocks[0].shape
    requests, width = rows // 2 * count, 2 * half
    units = weight.shape[1]
    return pl.pallas_call(
        functools.partial(hidden_first_kernel, count=count, part=part),
        in_specs=[vmem] * (count + 2),
        out_specs=[vmem] * 3,
        out_shape=[
            jax.ShapeDtypeStruct((requests, units + lanes), BF16),
            jax.ShapeDtypeStruct((requests, width), BF16),
            jax.ShapeDtypeStruct((requests, lanes), F32),
        ],
        scratch_shapes=[pltpu.VMEM((requests, width), F32)],
        compiler_params=params(2),
        cost_estimate=product_cost(requests, units, width),
        name="hidden_first",
    )(*blocks, gain, in_vmem(weight))


def hidden_kernel(scaled, *refs, parts):
    weights, out = refs[:-1], refs[-1]
    for t, (weight, part) in enumerate(zip(weights, parts)):
        units = weight.shape[1]
        out[:, t * units : (t + 1) * units] = unit_product(scaled[...], weight, part).astype(
            out.dtype
        )


def hidden_next(scaled, chosen, kind):
    requests, width = scaled.shape
    units = chosen[0][0].shape[1]
    return pl.pallas_call(
        functools.partial(hidden_kernel, parts=tuple(part for _, part in chosen)),
        in_specs=[vmem] * (1 + len(chosen)),
        out_specs=vmem,
        out_shape=jax.ShapeDtypeStruct((requests, len(chosen) * units), kind),
        compiler_params=params(2),
        cost_estimate=product_cost(requests, len(chosen) * units, width),
        name="hidden_next",
    )(scaled, *[in_vmem(weight) for weight, _ in chosen])


def squares_sum_kernel(keep, own_squares, arrived, out, squares):
    width = keep.shape[1]
    out[:, :width] = (keep[...] + arrived[:, :width].astype(F32)).astype(BF16)
    tail = arrived[:, width:].astype(F32)
    chip = own_squares[...] + (tail[:, :1] + tail[:, lanes // 2 : lanes // 2 + 1])
    squares[...] = chip
    out[:, width:] = high_low(chip).astype(BF16)


def squares_sum(keep, own_squares, arrived):
    requests, width = arrived.shape
    return pl.pallas_call(
        squares_sum_kernel,
        in_specs=[vmem] * 3,
        out_specs=[vmem] * 2,
        out_shape=[
            jax.ShapeDtypeStruct((requests, width), BF16),
            jax.ShapeDtypeStruct((requests, lanes), F32),
        ],
        compiler_params=params(2),
        name="squares_sum",
    )(keep, own_squares, arrived)


def chip_sum_kernel(keep, arrived, out):
    out[...] = (keep[...] + arrived[...].astype(F32)).astype(BF16)


def chip_sum(keep, arrived):
    return pl.pallas_call(
        chip_sum_kernel,
        in_specs=[vmem] * 2,
        out_specs=vmem,
        out_shape=jax.ShapeDtypeStruct(arrived.shape, BF16),
        compiler_params=params(2),
        name="chip_sum",
    )(keep, arrived)


def active_kernel(near, beside, far_gate, far_up, squares, out, *, model_width):
    units = far_up.shape[1]
    tail = far_gate[:, units:].astype(F32)
    square = squares[:, :1] + (tail[:, :1] + tail[:, lanes // 2 : lanes // 2 + 1])
    scale = lax.rsqrt(square / model_width + epsilon)

    def total(at, far):
        both = near[:, at : at + units] + beside[:, at : at + units].astype(F32)
        return (both + far.astype(F32)) * scale

    gate = total(0, far_gate[:, :units])
    out[...] = (gate / (1.0 + jnp.exp(-gate)) * total(units, far_up[...])).astype(BF16)


def active_units(near, beside, far_gate, far_up, squares, model_width):
    requests, width = near.shape
    return pl.pallas_call(
        functools.partial(active_kernel, model_width=model_width),
        in_specs=[vmem] * 5,
        out_specs=vmem,
        out_shape=jax.ShapeDtypeStruct((requests, width // 2), BF16),
        compiler_params=params(2),
        name="active",
    )(near, beside, far_gate, far_up, squares)


def down_kernel(*refs, parts, count, first, last):
    terms = len(parts)
    pieces, weights, rest = refs[:terms], refs[terms : 2 * terms], refs[2 * terms :]
    total = None if first else rest[0][...]
    outs = rest if first else rest[1:]
    for piece, weight, part in zip(pieces, weights, parts):
        term = jnp.dot(piece[...], weight[part], preferred_element_type=F32)
        total = term if total is None else total + term
    if last:
        rows = total.shape[0] // count
        for k in range(count):
            outs[k][...] = halves_stacked(total[k * rows : (k + 1) * rows]).astype(BF16)
    else:
        outs[0][...] = total


def down_part(chosen, count, before, last):
    requests, units = chosen[0][0].shape
    width = chosen[0][1].shape[2]
    if last:
        outs = [jax.ShapeDtypeStruct((2 * requests // count, width // 2), BF16)] * count
    else:
        outs = [jax.ShapeDtypeStruct((requests, width), F32)]
    before = [] if before is None else [before]
    return pl.pallas_call(
        functools.partial(
            down_kernel,
            parts=tuple(part for _, _, part in chosen),
            count=count,
            first=not before,
            last=last,
        ),
        in_specs=[vmem] * (2 * len(chosen) + len(before)),
        out_specs=[vmem] * len(outs),
        out_shape=outs,
        compiler_params=params(2),
        cost_estimate=product_cost(requests, len(chosen) * units, width),
        name="down",
    )(*[piece for piece, _, _ in chosen], *[in_vmem(w) for _, w, _ in chosen], *before)


def swaps_of(blocks):
    count = len(blocks)
    arrived = {k: pair_swap(blocks[k], "att", k) for k in reversed(range(1, count))}
    return [blocks[0]] + [arrived[k] for k in range(1, count)]


def exchanging_device(*args):
    return exchanging_layer(*args)


def exchanging_layer(
    hidden_state,
    queries,
    key_cache,
    value_cache,
    lengths,
    assignment,
    out_weight,
    norm_gain,
    gate_weight,
    up_weight,
    down_weight,
):
    slots, columns = hidden_state.shape
    count = lax.axis_size("att")
    parts = lax.axis_size("ffn")
    model_width = columns * parts
    heads = queries.shape[1] // lanes
    own = jnp.stack([lax.axis_index("att"), lax.axis_index("ffn")]).astype(I32)
    table = jnp.concatenate([own, lengths, assignment])
    served = jnp.pad(assignment, (0, lanes - assignment.shape[0]))
    served = lax.broadcast_in_dim(served, (8, lanes), (1,))

    own_queries = queries.reshape(slots, heads, lanes)
    query_blocks = swaps_of([own_queries] * count)
    keys, values = fetch([(key_cache, None), (value_cache, None)], parts)
    jobs = [(out_weight.reshape(-1, columns), (0, 1, 2, 3)), (down_weight, (0, 1))]
    *blocks, project, down_near = attention(table, query_blocks, keys, values, jobs, parts)

    blocks = swaps_of(blocks)
    padded = blocks[0].shape[0]
    jobs = [(up_weight, (3,))]
    up_corner, choose = selection(served, jobs, parts, slots, padded, count)
    piece = ordered(choose, blocks)
    across = pair_swap(piece, "ffn", 2)
    beside = pair_swap(piece, "ffn", 1)
    corner = pair_swap(across, "ffn", 1)
    (down_far,) = fetch([(down_weight, (2, 3))], parts)
    gain = norm_gain.reshape(1, columns)
    partial = projection([piece, beside, across, corner], project, slots, count)
    (gate,) = fetch([(gate_weight, (0, 1, 2, 3))], parts)
    middle = residual(hidden_state, swaps_of(partial), False)

    rows = swaps_of([middle] * count)
    (up,) = fetch([(up_weight, (0, 1, 2))], parts)
    send, scaled, squares = hidden_first(rows, gain, gate, 3)
    arrived = pair_swap(send, "ffn", 1)
    keep = hidden_next(scaled, [(gate, 2)], F32)
    far_gate, squares = squares_sum(keep, squares, arrived)
    far_gate = pair_swap(far_gate, "ffn", 2)
    send = hidden_next(scaled, [(up_corner, 0)], BF16)
    arrived = pair_swap(send, "ffn", 1)
    keep = hidden_next(scaled, [(up, 2)], F32)
    far_up = pair_swap(chip_sum(keep, arrived), "ffn", 2)
    send = hidden_next(scaled, [(gate, 1), (up, 1)], BF16)
    arrived = pair_swap(send, "ffn", 1)
    keep = hidden_next(scaled, [(gate, 0), (up, 0)], F32)
    active = active_units(keep, arrived, far_gate, far_up, squares, model_width)

    across = pair_swap(active, "ffn", 2)
    beside = pair_swap(active, "ffn", 1)
    chosen = [(active, down_near, 0), (beside, down_near, 1)]
    (before,) = down_part(chosen, count, None, False)
    corner = pair_swap(across, "ffn", 1)
    (before,) = down_part([(across, down_far, 0)], count, before, False)
    partial = down_part([(corner, down_far, 1)], count, before, True)
    return residual(middle, swaps_of(partial), True)


def solution(mesh):
    count, parts = mesh.shape["att"], mesh.shape["ffn"]
    paired = count == 4 and parts == 4
    in_specs = (
        P(("group", "att"), "ffn"),
        P(("group", "att"), "ffn"),
        P(("group", "att"), "ffn"),
        P(("group", "att"), "ffn"),
        P(("group", "att")),
        P("group"),
        P(None, "att", "ffn"),
        P("ffn"),
        P("att", "ffn"),
        P("att", "ffn"),
        P("att", "ffn"),
    )
    out_specs = P(("group", "att"), "ffn")
    return jax.shard_map(
        exchanging_device if paired else general_device,
        mesh=mesh,
        in_specs=in_specs,
        out_specs=out_specs,
        check_vma=False,
    )
```

```python
import functools
import math

import jax
import jax.numpy as jnp
from jax import lax
from jax.experimental import pallas as pl
from jax.experimental.pallas import tpu as pltpu
from jax.sharding import PartitionSpec as P

epsilon = 1e-05
masked_score = -1e30
lanes = 128
block_rows = 256
max_context = 1279
most_blocks = (max_context + block_rows - 2) // block_rows + 1
slot_group = 2
contract_minor = (((1,), (1,)), ((), ()))
F32 = jnp.float32
BF16 = jnp.bfloat16
I32 = jnp.int32
vmem = pl.BlockSpec(memory_space=pltpu.VMEM)
smem = pl.BlockSpec(memory_space=pltpu.SMEM)
hbm = pl.BlockSpec(memory_space=pltpu.HBM)


def softmax_rounded(scores):
    row_top = jnp.max(scores, axis=-1, keepdims=True)
    shifted = jnp.exp(scores - row_top)
    totals = jnp.sum(shifted, axis=-1, keepdims=True)
    return (shifted / totals).astype(jnp.bfloat16)


def general_device(
    hidden_state,
    queries,
    key_cache,
    value_cache,
    lengths,
    assignment,
    out_weight,
    norm_gain,
    gate_weight,
    up_weight,
    down_weight,
):
    rows_dev = hidden_state.shape[0]
    columns = hidden_state.shape[1]
    att_count = lax.axis_size("att")
    ffn_count = lax.axis_size("ffn")
    requests = rows_dev * att_count
    kv_total = out_weight.shape[0]
    kv_local = kv_total // ffn_count
    model_width = columns * ffn_count
    pool_rows = key_cache.shape[0]
    head_size = key_cache.shape[1] // kv_local
    per_group = queries.shape[1] // (kv_local * head_size)
    score_scale = 1.0 / math.sqrt(head_size)
    att_place = lax.axis_index("att")
    every_query = lax.all_gather(queries, "att", axis=0, tiled=True)
    own_slots = lax.dynamic_slice_in_dim(assignment, att_place * rows_dev, rows_dev)
    slot_queries = jnp.take(every_query, own_slots, axis=0).reshape(
        rows_dev, kv_local, per_group, head_size
    )
    keys_local = key_cache.reshape(pool_rows, kv_local, head_size)
    values_local = value_cache.reshape(pool_rows, kv_local, head_size)
    slot_starts = jnp.cumsum(lengths) - lengths
    slot_ends = slot_starts + lengths
    positions = jnp.arange(pool_rows, dtype=jnp.int32)
    owned_rows = (positions[None, :] >= slot_starts[:, None]) & (
        positions[None, :] < slot_ends[:, None]
    )
    owned_rows = owned_rows[:, None, None, :]
    raw_scores = (
        jnp.einsum("rkgc,pkc->rkgp", slot_queries, keys_local, preferred_element_type=jnp.float32)
        * score_scale
    )
    weights = softmax_rounded(jnp.where(owned_rows, raw_scores, masked_score))
    attended = jnp.einsum(
        "rkgp,pkc->rkgc", weights, values_local, preferred_element_type=jnp.float32
    )
    attended = attended.astype(jnp.bfloat16).reshape(rows_dev, kv_local, per_group * head_size)
    spread = lax.all_to_all(attended, "att", split_axis=2, concat_axis=0, tiled=True)
    pieces = lax.all_gather(spread, "ffn", axis=1, tiled=True)
    inverse = (
        jnp.zeros((requests,), jnp.int32).at[assignment].set(jnp.arange(requests, dtype=jnp.int32))
    )
    request_pieces = jnp.take(pieces, inverse, axis=0)
    block = request_pieces
    projected = lax.psum_scatter(
        jnp.einsum("rkc,kcd->rd", block, out_weight, preferred_element_type=jnp.float32).astype(
            jnp.bfloat16
        ),
        "att",
        scatter_dimension=0,
        tiled=True,
    ).astype(jnp.float32)
    middle_short = (hidden_state.astype(jnp.float32) + projected).astype(jnp.bfloat16)
    middle = lax.optimization_barrier(middle_short).astype(jnp.float32)
    squares = lax.psum(jnp.sum(middle * middle, axis=1), "ffn")
    normed = (
        middle * lax.rsqrt(squares[:, None] / model_width + epsilon) * norm_gain.astype(jnp.float32)
    ).astype(jnp.bfloat16)
    every_row = lax.all_gather(normed, "att", axis=0, tiled=True)
    contract = (((1,), (1,)), ((), ()))
    gate_part = lax.dot_general(
        gate_weight, every_row, contract, preferred_element_type=jnp.float32
    )
    up_part = lax.dot_general(up_weight, every_row, contract, preferred_element_type=jnp.float32)
    totals = lax.psum(
        jnp.concatenate([gate_part, up_part], axis=1).astype(jnp.bfloat16), "ffn"
    ).astype(jnp.float32)
    unit_active = (jax.nn.silu(totals[:, :requests]) * totals[:, requests:]).astype(jnp.bfloat16)
    block = unit_active
    returned = lax.psum_scatter(
        lax.dot_general(
            block, down_weight, (((0,), (0,)), ((), ())), preferred_element_type=jnp.float32
        ).astype(jnp.bfloat16),
        "att",
        scatter_dimension=0,
        tiled=True,
    ).astype(jnp.float32)
    return (middle + returned).astype(jnp.bfloat16)


def pair_swap(value, axis, bit):
    count = lax.axis_size(axis)
    return lax.ppermute(value, axis, [(i, i ^ bit) for i in range(count)])


def up_to(value, multiple):
    return -(-value // multiple) * multiple


def params(megabytes):
    return pltpu.CompilerParams(vmem_limit_bytes=megabytes << 20)


def halves_joined(block):
    block = block.astype(F32)
    rows = block.shape[0] // 2
    return jnp.concatenate([block[:rows], block[rows:]], axis=1)


def halves_stacked(block):
    half = block.shape[1] // 2
    return jnp.concatenate([block[:, :half], block[:, half:]], axis=0)


def high_low(value):
    high = value.astype(BF16).astype(F32)
    low = value - high
    lane = lax.broadcasted_iota(I32, (value.shape[0], lanes), 1)
    return jnp.where(lane < lanes // 2, high, low)


def in_hbm(value):
    return pltpu.with_memory_space_constraint(value, pltpu.HBM)


def in_vmem(value):
    return pltpu.with_memory_space_constraint(value, pltpu.VMEM)


def job_shapes(jobs, parts):
    shapes = []
    for array, masks in jobs:
        if masks is None:
            shapes.append(pltpu.VMEM(array.shape, array.dtype))
        else:
            rows, width = array.shape
            shapes.append(pltpu.VMEM((len(masks), rows // parts, width), array.dtype))
    return shapes


def job_count(jobs):
    return sum(1 if masks is None else len(masks) for _, masks in jobs)


def job_copies(own, masks_of, sources, targets, sems):
    copies = []
    for masks, source, target in zip(masks_of, sources, targets):
        if masks is None:
            copies.append(pltpu.make_async_copy(source, target, sems.at[len(copies)]))
            continue
        rows = target.shape[1]
        for m, mask in enumerate(masks):
            at = pl.ds(pl.multiple_of((own ^ mask) * rows, rows), rows)
            copies.append(
                pltpu.make_async_copy(source.at[at], target.at[m], sems.at[len(copies)])
            )
    return copies


def masks_in(jobs):
    return tuple(masks for _, masks in jobs)


def fetch_kernel(*refs, masks_of):
    count = len(masks_of)
    own = lax.axis_index("ffn")
    copies = job_copies(own, masks_of, refs[:count], refs[count:-1], refs[-1])
    for copy in copies:
        copy.start()
    for copy in copies:
        copy.wait()


def fetch(jobs, parts):
    shapes = job_shapes(jobs, parts)
    moved = sum(2 * math.prod(shape.shape) for shape in shapes)
    return pl.pallas_call(
        functools.partial(fetch_kernel, masks_of=masks_in(jobs)),
        in_specs=[hbm] * len(jobs),
        out_specs=[vmem] * len(jobs),
        out_shape=shapes,
        scratch_shapes=[pltpu.SemaphoreType.DMA((job_count(jobs),))],
        compiler_params=params(1),
        cost_estimate=pl.CostEstimate(flops=0, bytes_accessed=2 * moved, transcendentals=0),
        name="fetch",
    )(*[in_hbm(array) for array, _ in jobs])


def folded(combine, value):
    parts = [value[:, i : i + lanes] for i in range(0, value.shape[1], lanes)]
    return functools.reduce(combine, parts)


def attention_kernel(table, *refs, slots, count, scale, unroll, masks_of):
    jobs = len(masks_of)
    query_blocks, (keys, values), sources = (
        refs[:count],
        refs[count : count + 2],
        refs[count + 2 : count + 2 + jobs],
    )
    outs, targets = (
        refs[count + 2 + jobs : 2 * count + 2 + jobs],
        refs[2 * count + 2 + jobs : 2 * count + 2 + 2 * jobs],
    )
    queries, both, begins, ends, tops, sums, scores, total, attended, items, sems = refs[
        2 * count + 2 + 2 * jobs :
    ]
    copies = job_copies(table[1], masks_of, sources, targets, sems)
    for copy in copies:
        copy.start()
    pool, width = keys.shape
    heads = queries.shape[1]
    half = heads // 2
    own = table[0]
    group_rows = slot_group * heads
    top_half = lax.broadcasted_iota(I32, (heads, lanes), 0) < half
    for k in range(count):
        queries[k * slots : (k + 1) * slots] = query_blocks[k][...]

    tops[...] = jnp.full(tops.shape, masked_score, F32)
    sums[...] = jnp.zeros(sums.shape, F32)
    total[...] = jnp.zeros(total.shape, F32)
    spare = slots * heads
    both[spare:, :] = jnp.zeros((both.shape[0] - spare, width), BF16)
    begins[spare:, :] = jnp.full((begins.shape[0] - spare, lanes), pool, I32)
    ends[spare:, :] = jnp.zeros((ends.shape[0] - spare, lanes), I32)

    def slot(s, carry):
        start, made, last_block, last_slot = carry
        end = start + table[2 + s]
        request = table[2 + slots + own * slots + s]
        owner = sum((request >= k * slots).astype(I32) for k in range(1, count))
        query = queries[(owner ^ own) * slots + request - owner * slots]
        zero = jnp.zeros_like(query)
        at = pl.ds(pl.multiple_of(s * heads, heads), heads)
        both[at, :lanes] = jnp.where(top_half, query, zero)
        both[at, lanes:] = jnp.where(top_half, zero, query)
        begins[at, :] = jnp.full((heads, lanes), start, I32)
        ends[at, :] = jnp.full((heads, lanes), end, I32)
        first = start // block_rows
        covered = (first == last_block) & (s < last_slot + slot_group)
        first = jnp.where(covered, first + 1, first)
        last = (end - 1) // block_rows

        for j in range(most_blocks):
            items[2 * (made + j)] = first + j
            items[2 * (made + j) + 1] = s
        made_now = made + jnp.maximum(last + 1 - first, 0)
        new = made_now > made
        return (
            end,
            made_now,
            jnp.where(new, last, last_block),
            jnp.where(new, s, last_slot),
        )

    none = jnp.int32(-1)
    start = (jnp.int32(0), jnp.int32(0), none, none)
    _, made, _, _ = lax.fori_loop(0, slots, slot, start, unroll=True)
    for u in range(unroll):
        items[2 * (made + u)] = 0
        items[2 * (made + u) + 1] = slots
    steps = (made + unroll - 1) // unroll
    across = lax.broadcasted_iota(I32, (group_rows, block_rows), 1)

    def place_of(i):
        block = pl.multiple_of(items[2 * i] * block_rows, block_rows)
        rows = pl.multiple_of(items[2 * i + 1] * heads, heads)
        return block, pl.ds(block, block_rows), pl.ds(rows, group_rows)

    def score_step(step, carry):
        for u in range(unroll):
            i = step * unroll + u
            block, cache, rows = place_of(i)
            raw = lax.dot_general(
                both[rows, :], keys[cache, :], contract_minor, preferred_element_type=F32
            )
            position = block + across
            begin, end = (jnp.concatenate([b[rows, :]] * (block_rows // lanes), axis=1) for b in (begins, ends))
            inside = (position >= begin) & (position < end)
            masked = jnp.where(inside, raw * scale, masked_score)
            scores[i] = masked
            tops[rows, :] = jnp.maximum(tops[rows, :], folded(jnp.maximum, masked))
        return carry

    def value_step(step, carry):
        for u in range(unroll):
            i = step * unroll + u
            _, cache, rows = place_of(i)
            top = tops[rows, :]
            shifted = jnp.exp(scores[i] - jnp.concatenate([top] * (block_rows // lanes), axis=1))
            sums[rows, :] += folded(jnp.add, shifted)
            total[rows, :] += jnp.dot(
                shifted.astype(BF16), values[cache, :], preferred_element_type=F32
            )
        return carry

    lax.fori_loop(0, steps, score_step, 0)
    top = jnp.max(tops[...], axis=1, keepdims=True)
    tops[...] = jnp.broadcast_to(top, tops.shape)
    lax.fori_loop(0, steps, value_step, 0)

    real = slots * heads
    row = lax.broadcasted_iota(I32, (real, lanes), 0)
    upper = row % heads < half
    picked = jnp.where(upper, total[:real, :lanes], total[:real, lanes:])
    attended[...] = picked / jnp.sum(sums[:real, :], axis=1, keepdims=True)
    per_block = half // count
    for k in range(count):
        outs[k][...] = jnp.zeros(outs[k].shape, BF16)
        for kv in range(2):
            for j in range(per_block):
                head = kv * half + (own ^ k) * per_block + j
                at = (kv * per_block + j) * lanes
                outs[k][:slots, at : at + lanes] = attended[
                    pl.ds(head, slots, stride=heads), :
                ].astype(BF16)
    for copy in copies:
        copy.wait()


def attention(table, query_blocks, keys, values, jobs, parts, unroll=14):
    count = len(query_blocks)
    slots, heads, _ = query_blocks[0].shape
    pool, width = keys.shape
    most = pool // block_rows + slots + max(unroll, most_blocks)
    rows = (slots + slot_group) * heads
    return pl.pallas_call(
        functools.partial(
            attention_kernel,
            slots=slots,
            count=count,
            scale=1.0 / math.sqrt(lanes),
            unroll=unroll,
            masks_of=masks_in(jobs),
        ),
        in_specs=[smem] + [vmem] * (count + 2) + [hbm] * len(jobs),
        out_specs=[vmem] * (count + len(jobs)),
        out_shape=[jax.ShapeDtypeStruct((up_to(slots, 8), heads // count * lanes), BF16)] * count
        + job_shapes(jobs, parts),
        scratch_shapes=[
            pltpu.VMEM((count * slots, heads, lanes), BF16),
            pltpu.VMEM((rows, width), BF16),
            pltpu.VMEM((rows, lanes), I32),
            pltpu.VMEM((rows, lanes), I32),
            pltpu.VMEM((rows, lanes), F32),
            pltpu.VMEM((rows, lanes), F32),
            pltpu.VMEM((most, slot_group * heads, block_rows), F32),
            pltpu.VMEM((rows, width), F32),
            pltpu.VMEM((slots * heads, lanes), F32),
            pltpu.SMEM((2 * most,), I32),
            pltpu.SemaphoreType.DMA((job_count(jobs),)),
        ],
        compiler_params=params(6),
        cost_estimate=pl.CostEstimate(
            flops=4 * pool * heads * lanes, bytes_accessed=pool * width * 4, transcendentals=0
        ),
        name="attention",
    )(
        table,
        *query_blocks,
        in_vmem(keys),
        in_vmem(values),
        *[in_hbm(array) for array, _ in jobs],
    )


def selection_kernel(served, source, target, choose, sems, *, slots, count, masks_of):
    copies = job_copies(lax.axis_index("ffn"), masks_of, [source], [target], sems)
    for copy in copies:
        copy.start()
    own = lax.axis_index("att")
    requests, padded = choose.shape[1:]
    row = lax.broadcasted_iota(I32, (requests, padded), 0)
    wanted = row
    for k in range(count):
        moved = row + ((own ^ k) - k) * slots
        wanted = jnp.where((row >= k * slots) & (row < (k + 1) * slots), moved, wanted)
    lane = lax.broadcasted_iota(I32, (1, padded), 1)
    for k in range(count):
        turn = (count - (own ^ k)) * slots
        first = pltpu.roll(served[...], lax.rem(turn + lanes - count * slots, lanes), 1)
        request = jnp.where(lane < slots, first[:1, :padded], -1)
        choose[k] = (wanted == request).astype(F32).astype(BF16)
    for copy in copies:
        copy.wait()


def selection(served, jobs, parts, slots, padded, count):
    shapes = job_shapes(jobs, parts)
    moved = sum(2 * math.prod(shape.shape) for shape in shapes)
    return pl.pallas_call(
        functools.partial(
            selection_kernel, slots=slots, count=count, masks_of=masks_in(jobs)
        ),
        in_specs=[vmem, hbm],
        out_specs=[vmem] * 2,
        out_shape=shapes + [jax.ShapeDtypeStruct((count, slots * count, padded), BF16)],
        scratch_shapes=[pltpu.SemaphoreType.DMA((job_count(jobs),))],
        compiler_params=params(1),
        cost_estimate=pl.CostEstimate(flops=0, bytes_accessed=2 * moved, transcendentals=0),
        name="selection",
    )(served, in_hbm(jobs[0][0]))


def ordered_kernel(choose, *refs):
    blocks, out = refs[:-1], refs[-1]
    total = None
    for k, block in enumerate(blocks):
        term = jnp.dot(choose[k], block[...], preferred_element_type=F32)
        total = term if total is None else total + term
    out[...] = total.astype(BF16)


def ordered(choose, blocks):
    return pl.pallas_call(
        ordered_kernel,
        in_specs=[vmem] * (1 + len(blocks)),
        out_specs=vmem,
        out_shape=jax.ShapeDtypeStruct((choose.shape[1], blocks[0].shape[1]), BF16),
        compiler_params=params(2),
        name="ordered",
    )(choose, *blocks)


def projection_kernel(*refs, slots, parts):
    pieces, weight, outs = refs[:parts], refs[parts], refs[parts + 1 :]
    total = None
    for p in range(parts):
        term = jnp.dot(pieces[p][...], weight[p], preferred_element_type=F32)
        total = term if total is None else total + term
    for k, out in enumerate(outs):
        out[...] = halves_stacked(total[k * slots : (k + 1) * slots]).astype(BF16)


def projection(pieces, weight, slots, count):
    parts, depth, width = weight.shape
    return pl.pallas_call(
        functools.partial(projection_kernel, slots=slots, parts=parts),
        in_specs=[vmem] * (1 + parts),
        out_specs=[vmem] * count,
        out_shape=[jax.ShapeDtypeStruct((2 * slots, width // 2), BF16)] * count,
        compiler_params=params(2),
        cost_estimate=pl.CostEstimate(
            flops=2 * slots * count * parts * depth * width,
            bytes_accessed=parts * depth * width,
            transcendentals=0,
        ),
        name="projection",
    )(*pieces, in_vmem(weight))


def residual_kernel(*refs, joined):
    base, blocks, out = refs[0], refs[1:-1], refs[-1]
    total = base[...].astype(F32)
    if not joined:
        total = halves_stacked(total)
    for block in blocks:
        total = total + block[...].astype(F32)
    out[...] = (halves_joined(total) if joined else total).astype(BF16)


def residual(base, blocks, joined):
    rows, half = blocks[0].shape
    shape = (rows // 2, 2 * half) if joined else (rows, half)
    return pl.pallas_call(
        functools.partial(residual_kernel, joined=joined),
        in_specs=[vmem] * (1 + len(blocks)),
        out_specs=vmem,
        out_shape=jax.ShapeDtypeStruct(shape, BF16),
        compiler_params=params(2),
        name="residual",
    )(base, *blocks)


def unit_product(scaled, weight, part):
    return lax.dot_general(scaled, weight[part], contract_minor, preferred_element_type=F32)


def product_cost(requests, units, width):
    return pl.CostEstimate(
        flops=2 * requests * units * width, bytes_accessed=units * width, transcendentals=0
    )


def hidden_first_kernel(*refs, count, part):
    blocks, (gain, weight, send, scaled, squares, joined) = refs[:count], refs[count:]
    rows = blocks[0].shape[0] // 2
    for k in range(count):
        joined[k * rows : (k + 1) * rows, :] = halves_joined(blocks[k][...])
    middle = joined[...]
    square = jnp.sum(middle * middle, axis=1, keepdims=True)
    scaled[...] = (middle * gain[...].astype(F32)).astype(BF16)
    units = weight.shape[1]
    send[:, :units] = unit_product(scaled[...], weight, part).astype(BF16)
    send[:, units:] = high_low(square).astype(BF16)
    squares[...] = jnp.broadcast_to(square, squares.shape)


def hidden_first(blocks, gain, weight, part):
    count = len(blocks)
    rows, half = blocks[0].shape
    requests, width = rows // 2 * count, 2 * half
    units = weight.shape[1]
    return pl.pallas_call(
        functools.partial(hidden_first_kernel, count=count, part=part),
        in_specs=[vmem] * (count + 2),
        out_specs=[vmem] * 3,
        out_shape=[
            jax.ShapeDtypeStruct((requests, units + lanes), BF16),
            jax.ShapeDtypeStruct((requests, width), BF16),
            jax.ShapeDtypeStruct((requests, lanes), F32),
        ],
        scratch_shapes=[pltpu.VMEM((requests, width), F32)],
        compiler_params=params(2),
        cost_estimate=product_cost(requests, units, width),
        name="hidden_first",
    )(*blocks, gain, in_vmem(weight))


def hidden_kernel(scaled, *refs, parts):
    weights, out = refs[:-1], refs[-1]
    for t, (weight, part) in enumerate(zip(weights, parts)):
        units = weight.shape[1]
        out[:, t * units : (t + 1) * units] = unit_product(scaled[...], weight, part).astype(
            out.dtype
        )


def hidden_next(scaled, chosen, kind):
    requests, width = scaled.shape
    units = chosen[0][0].shape[1]
    return pl.pallas_call(
        functools.partial(hidden_kernel, parts=tuple(part for _, part in chosen)),
        in_specs=[vmem] * (1 + len(chosen)),
        out_specs=vmem,
        out_shape=jax.ShapeDtypeStruct((requests, len(chosen) * units), kind),
        compiler_params=params(2),
        cost_estimate=product_cost(requests, len(chosen) * units, width),
        name="hidden_next",
    )(scaled, *[in_vmem(weight) for weight, _ in chosen])


def squares_sum_kernel(keep, own_squares, arrived, out, squares):
    width = keep.shape[1]
    out[:, :width] = (keep[...] + arrived[:, :width].astype(F32)).astype(BF16)
    tail = arrived[:, width:].astype(F32)
    chip = own_squares[...] + (tail[:, :1] + tail[:, lanes // 2 : lanes // 2 + 1])
    squares[...] = chip
    out[:, width:] = high_low(chip).astype(BF16)


def squares_sum(keep, own_squares, arrived):
    requests, width = arrived.shape
    return pl.pallas_call(
        squares_sum_kernel,
        in_specs=[vmem] * 3,
        out_specs=[vmem] * 2,
        out_shape=[
            jax.ShapeDtypeStruct((requests, width), BF16),
            jax.ShapeDtypeStruct((requests, lanes), F32),
        ],
        compiler_params=params(2),
        name="squares_sum",
    )(keep, own_squares, arrived)


def chip_sum_kernel(keep, arrived, out):
    out[...] = (keep[...] + arrived[...].astype(F32)).astype(BF16)


def chip_sum(keep, arrived):
    return pl.pallas_call(
        chip_sum_kernel,
        in_specs=[vmem] * 2,
        out_specs=vmem,
        out_shape=jax.ShapeDtypeStruct(arrived.shape, BF16),
        compiler_params=params(2),
        name="chip_sum",
    )(keep, arrived)


def active_kernel(near, beside, far_gate, far_up, squares, out, *, model_width):
    units = far_up.shape[1]
    tail = far_gate[:, units:].astype(F32)
    square = squares[:, :1] + (tail[:, :1] + tail[:, lanes // 2 : lanes // 2 + 1])
    scale = lax.rsqrt(square / model_width + epsilon)

    def total(at, far):
        both = near[:, at : at + units] + beside[:, at : at + units].astype(F32)
        return (both + far.astype(F32)) * scale

    gate = total(0, far_gate[:, :units])
    out[...] = (gate / (1.0 + jnp.exp(-gate)) * total(units, far_up[...])).astype(BF16)


def active_units(near, beside, far_gate, far_up, squares, model_width):
    requests, width = near.shape
    return pl.pallas_call(
        functools.partial(active_kernel, model_width=model_width),
        in_specs=[vmem] * 5,
        out_specs=vmem,
        out_shape=jax.ShapeDtypeStruct((requests, width // 2), BF16),
        compiler_params=params(2),
        name="active",
    )(near, beside, far_gate, far_up, squares)


def down_kernel(*refs, parts, count, first, last):
    terms = len(parts)
    pieces, weights, rest = refs[:terms], refs[terms : 2 * terms], refs[2 * terms :]
    total = None if first else rest[0][...]
    outs = rest if first else rest[1:]
    for piece, weight, part in zip(pieces, weights, parts):
        term = jnp.dot(piece[...], weight[part], preferred_element_type=F32)
        total = term if total is None else total + term
    if last:
        rows = total.shape[0] // count
        for k in range(count):
            outs[k][...] = halves_stacked(total[k * rows : (k + 1) * rows]).astype(BF16)
    else:
        outs[0][...] = total


def down_part(chosen, count, before, last):
    requests, units = chosen[0][0].shape
    width = chosen[0][1].shape[2]
    if last:
        outs = [jax.ShapeDtypeStruct((2 * requests // count, width // 2), BF16)] * count
    else:
        outs = [jax.ShapeDtypeStruct((requests, width), F32)]
    before = [] if before is None else [before]
    return pl.pallas_call(
        functools.partial(
            down_kernel,
            parts=tuple(part for _, _, part in chosen),
            count=count,
            first=not before,
            last=last,
        ),
        in_specs=[vmem] * (2 * len(chosen) + len(before)),
        out_specs=[vmem] * len(outs),
        out_shape=outs,
        compiler_params=params(2),
        cost_estimate=product_cost(requests, len(chosen) * units, width),
        name="down",
    )(*[piece for piece, _, _ in chosen], *[in_vmem(w) for _, w, _ in chosen], *before)


def swaps_of(blocks):
    count = len(blocks)
    arrived = {k: pair_swap(blocks[k], "att", k) for k in reversed(range(1, count))}
    return [blocks[0]] + [arrived[k] for k in range(1, count)]


def exchanging_device(*args):
    return exchanging_layer(*args)


def exchanging_layer(
    hidden_state,
    queries,
    key_cache,
    value_cache,
    lengths,
    assignment,
    out_weight,
    norm_gain,
    gate_weight,
    up_weight,
    down_weight,
):
    slots, columns = hidden_state.shape
    count = lax.axis_size("att")
    parts = lax.axis_size("ffn")
    model_width = columns * parts
    heads = queries.shape[1] // lanes
    own = jnp.stack([lax.axis_index("att"), lax.axis_index("ffn")]).astype(I32)
    table = jnp.concatenate([own, lengths, assignment])
    served = jnp.pad(assignment, (0, lanes - assignment.shape[0]))
    served = lax.broadcast_in_dim(served, (8, lanes), (1,))

    own_queries = queries.reshape(slots, heads, lanes)
    query_blocks = swaps_of([own_queries] * count)
    keys, values = fetch([(key_cache, None), (value_cache, None)], parts)
    jobs = [(out_weight.reshape(-1, columns), (0, 1, 2, 3)), (down_weight, (0,))]
    *blocks, project, down_near = attention(table, query_blocks, keys, values, jobs, parts)

    blocks = swaps_of(blocks)
    padded = blocks[0].shape[0]
    jobs = [(up_weight, (3,))]
    up_corner, choose = selection(served, jobs, parts, slots, padded, count)
    piece = ordered(choose, blocks)
    across = pair_swap(piece, "ffn", 2)
    beside = pair_swap(piece, "ffn", 1)
    corner = pair_swap(across, "ffn", 1)
    (down_far,) = fetch([(down_weight, (2, 3))], parts)
    gain = norm_gain.reshape(1, columns)
    partial = projection([piece, beside, across, corner], project, slots, count)
    jobs = [(gate_weight, (0, 1, 2, 3)), (down_weight, (1,))]
    gate, down_beside = fetch(jobs, parts)
    middle = residual(hidden_state, swaps_of(partial), False)

    rows = swaps_of([middle] * count)
    (up,) = fetch([(up_weight, (0, 1, 2))], parts)
    send, scaled, squares = hidden_first(rows, gain, gate, 3)
    arrived = pair_swap(send, "ffn", 1)
    keep = hidden_next(scaled, [(gate, 2)], F32)
    far_gate, squares = squares_sum(keep, squares, arrived)
    far_gate = pair_swap(far_gate, "ffn", 2)
    send = hidden_next(scaled, [(up_corner, 0)], BF16)
    arrived = pair_swap(send, "ffn", 1)
    keep = hidden_next(scaled, [(up, 2)], F32)
    far_up = pair_swap(chip_sum(keep, arrived), "ffn", 2)
    send = hidden_next(scaled, [(gate, 1), (up, 1)], BF16)
    arrived = pair_swap(send, "ffn", 1)
    keep = hidden_next(scaled, [(gate, 0), (up, 0)], F32)
    active = active_units(keep, arrived, far_gate, far_up, squares, model_width)

    across = pair_swap(active, "ffn", 2)
    beside = pair_swap(active, "ffn", 1)
    chosen = [(active, down_near, 0), (beside, down_beside, 0)]
    (before,) = down_part(chosen, count, None, False)
    corner = pair_swap(across, "ffn", 1)
    (before,) = down_part([(across, down_far, 0)], count, before, False)
    partial = down_part([(corner, down_far, 1)], count, before, True)
    return residual(middle, swaps_of(partial), True)


def solution(mesh):
    count, parts = mesh.shape["att"], mesh.shape["ffn"]
    paired = count == 4 and parts == 4
    in_specs = (
        P(("group", "att"), "ffn"),
        P(("group", "att"), "ffn"),
        P(("group", "att"), "ffn"),
        P(("group", "att"), "ffn"),
        P(("group", "att")),
        P("group"),
        P(None, "att", "ffn"),
        P("ffn"),
        P("att", "ffn"),
        P("att", "ffn"),
        P("att", "ffn"),
    )
    out_specs = P(("group", "att"), "ffn")
    return jax.shard_map(
        exchanging_device if paired else general_device,
        mesh=mesh,
        in_specs=in_specs,
        out_specs=out_specs,
        check_vma=False,
    )
```

```python
import functools
import math

import jax
import jax.numpy as jnp
from jax import lax
from jax.experimental import pallas as pl
from jax.experimental.pallas import tpu as pltpu
from jax.sharding import PartitionSpec as P

epsilon = 1e-05
masked_score = -1e30
lanes = 128
block_rows = 256
max_context = 1279
most_blocks = (max_context + block_rows - 2) // block_rows + 1
slot_group = 2
contract_minor = (((1,), (1,)), ((), ()))
F32 = jnp.float32
BF16 = jnp.bfloat16
I32 = jnp.int32
vmem = pl.BlockSpec(memory_space=pltpu.VMEM)
smem = pl.BlockSpec(memory_space=pltpu.SMEM)
hbm = pl.BlockSpec(memory_space=pltpu.HBM)


def softmax_rounded(scores):
    row_top = jnp.max(scores, axis=-1, keepdims=True)
    shifted = jnp.exp(scores - row_top)
    totals = jnp.sum(shifted, axis=-1, keepdims=True)
    return (shifted / totals).astype(jnp.bfloat16)


def general_device(
    hidden_state,
    queries,
    key_cache,
    value_cache,
    lengths,
    assignment,
    out_weight,
    norm_gain,
    gate_weight,
    up_weight,
    down_weight,
):
    rows_dev = hidden_state.shape[0]
    columns = hidden_state.shape[1]
    att_count = lax.axis_size("att")
    ffn_count = lax.axis_size("ffn")
    requests = rows_dev * att_count
    kv_total = out_weight.shape[0]
    kv_local = kv_total // ffn_count
    model_width = columns * ffn_count
    pool_rows = key_cache.shape[0]
    head_size = key_cache.shape[1] // kv_local
    per_group = queries.shape[1] // (kv_local * head_size)
    score_scale = 1.0 / math.sqrt(head_size)
    att_place = lax.axis_index("att")
    every_query = lax.all_gather(queries, "att", axis=0, tiled=True)
    own_slots = lax.dynamic_slice_in_dim(assignment, att_place * rows_dev, rows_dev)
    slot_queries = jnp.take(every_query, own_slots, axis=0).reshape(
        rows_dev, kv_local, per_group, head_size
    )
    keys_local = key_cache.reshape(pool_rows, kv_local, head_size)
    values_local = value_cache.reshape(pool_rows, kv_local, head_size)
    slot_starts = jnp.cumsum(lengths) - lengths
    slot_ends = slot_starts + lengths
    positions = jnp.arange(pool_rows, dtype=jnp.int32)
    owned_rows = (positions[None, :] >= slot_starts[:, None]) & (
        positions[None, :] < slot_ends[:, None]
    )
    owned_rows = owned_rows[:, None, None, :]
    raw_scores = (
        jnp.einsum("rkgc,pkc->rkgp", slot_queries, keys_local, preferred_element_type=jnp.float32)
        * score_scale
    )
    weights = softmax_rounded(jnp.where(owned_rows, raw_scores, masked_score))
    attended = jnp.einsum(
        "rkgp,pkc->rkgc", weights, values_local, preferred_element_type=jnp.float32
    )
    attended = attended.astype(jnp.bfloat16).reshape(rows_dev, kv_local, per_group * head_size)
    spread = lax.all_to_all(attended, "att", split_axis=2, concat_axis=0, tiled=True)
    pieces = lax.all_gather(spread, "ffn", axis=1, tiled=True)
    inverse = (
        jnp.zeros((requests,), jnp.int32).at[assignment].set(jnp.arange(requests, dtype=jnp.int32))
    )
    request_pieces = jnp.take(pieces, inverse, axis=0)
    block = request_pieces
    projected = lax.psum_scatter(
        jnp.einsum("rkc,kcd->rd", block, out_weight, preferred_element_type=jnp.float32).astype(
            jnp.bfloat16
        ),
        "att",
        scatter_dimension=0,
        tiled=True,
    ).astype(jnp.float32)
    middle_short = (hidden_state.astype(jnp.float32) + projected).astype(jnp.bfloat16)
    middle = lax.optimization_barrier(middle_short).astype(jnp.float32)
    squares = lax.psum(jnp.sum(middle * middle, axis=1), "ffn")
    normed = (
        middle * lax.rsqrt(squares[:, None] / model_width + epsilon) * norm_gain.astype(jnp.float32)
    ).astype(jnp.bfloat16)
    every_row = lax.all_gather(normed, "att", axis=0, tiled=True)
    contract = (((1,), (1,)), ((), ()))
    gate_part = lax.dot_general(
        gate_weight, every_row, contract, preferred_element_type=jnp.float32
    )
    up_part = lax.dot_general(up_weight, every_row, contract, preferred_element_type=jnp.float32)
    totals = lax.psum(
        jnp.concatenate([gate_part, up_part], axis=1).astype(jnp.bfloat16), "ffn"
    ).astype(jnp.float32)
    unit_active = (jax.nn.silu(totals[:, :requests]) * totals[:, requests:]).astype(jnp.bfloat16)
    block = unit_active
    returned = lax.psum_scatter(
        lax.dot_general(
            block, down_weight, (((0,), (0,)), ((), ())), preferred_element_type=jnp.float32
        ).astype(jnp.bfloat16),
        "att",
        scatter_dimension=0,
        tiled=True,
    ).astype(jnp.float32)
    return (middle + returned).astype(jnp.bfloat16)


def pair_swap(value, axis, bit):
    count = lax.axis_size(axis)
    return lax.ppermute(value, axis, [(i, i ^ bit) for i in range(count)])


def up_to(value, multiple):
    return -(-value // multiple) * multiple


def params(megabytes):
    return pltpu.CompilerParams(vmem_limit_bytes=megabytes << 20)


def halves_joined(block):
    block = block.astype(F32)
    rows = block.shape[0] // 2
    return jnp.concatenate([block[:rows], block[rows:]], axis=1)


def halves_stacked(block):
    half = block.shape[1] // 2
    return jnp.concatenate([block[:, :half], block[:, half:]], axis=0)


def high_low(value):
    high = value.astype(BF16).astype(F32)
    low = value - high
    lane = lax.broadcasted_iota(I32, (value.shape[0], lanes), 1)
    return jnp.where(lane < lanes // 2, high, low)


def in_hbm(value):
    return pltpu.with_memory_space_constraint(value, pltpu.HBM)


def in_vmem(value):
    return pltpu.with_memory_space_constraint(value, pltpu.VMEM)


def job_shapes(jobs, parts):
    shapes = []
    for array, masks in jobs:
        if masks is None:
            shapes.append(pltpu.VMEM(array.shape, array.dtype))
        else:
            rows, width = array.shape
            shapes.append(pltpu.VMEM((len(masks), rows // parts, width), array.dtype))
    return shapes


def job_count(jobs):
    return sum(1 if masks is None else len(masks) for _, masks in jobs)


def job_copies(own, masks_of, sources, targets, sems):
    copies = []
    for masks, source, target in zip(masks_of, sources, targets):
        if masks is None:
            copies.append(pltpu.make_async_copy(source, target, sems.at[len(copies)]))
            continue
        rows = target.shape[1]
        for m, mask in enumerate(masks):
            at = pl.ds(pl.multiple_of((own ^ mask) * rows, rows), rows)
            copies.append(
                pltpu.make_async_copy(source.at[at], target.at[m], sems.at[len(copies)])
            )
    return copies


def masks_in(jobs):
    return tuple(masks for _, masks in jobs)


def fetch_kernel(*refs, masks_of):
    count = len(masks_of)
    own = lax.axis_index("ffn")
    copies = job_copies(own, masks_of, refs[:count], refs[count:-1], refs[-1])
    for copy in copies:
        copy.start()
    for copy in copies:
        copy.wait()


def fetch(jobs, parts):
    shapes = job_shapes(jobs, parts)
    moved = sum(2 * math.prod(shape.shape) for shape in shapes)
    return pl.pallas_call(
        functools.partial(fetch_kernel, masks_of=masks_in(jobs)),
        in_specs=[hbm] * len(jobs),
        out_specs=[vmem] * len(jobs),
        out_shape=shapes,
        scratch_shapes=[pltpu.SemaphoreType.DMA((job_count(jobs),))],
        compiler_params=params(1),
        cost_estimate=pl.CostEstimate(flops=0, bytes_accessed=2 * moved, transcendentals=0),
        name="fetch",
    )(*[in_hbm(array) for array, _ in jobs])


def folded(combine, value):
    parts = [value[:, i : i + lanes] for i in range(0, value.shape[1], lanes)]
    return functools.reduce(combine, parts)


def attention_kernel(table, *refs, slots, count, scale, unroll, masks_of):
    jobs = len(masks_of)
    query_blocks, (keys, values), sources = (
        refs[:count],
        refs[count : count + 2],
        refs[count + 2 : count + 2 + jobs],
    )
    outs, targets = (
        refs[count + 2 + jobs : 2 * count + 2 + jobs],
        refs[2 * count + 2 + jobs : 2 * count + 2 + 2 * jobs],
    )
    queries, both, begins, ends, tops, sums, scores, total, attended, items, sems = refs[
        2 * count + 2 + 2 * jobs :
    ]
    copies = job_copies(table[1], masks_of, sources, targets, sems)
    for copy in copies:
        copy.start()
    pool, width = keys.shape
    heads = queries.shape[1]
    half = heads // 2
    own = table[0]
    group_rows = slot_group * heads
    top_half = lax.broadcasted_iota(I32, (heads, lanes), 0) < half
    for k in range(count):
        queries[k * slots : (k + 1) * slots] = query_blocks[k][...]

    tops[...] = jnp.full(tops.shape, masked_score, F32)
    sums[...] = jnp.zeros(sums.shape, F32)
    total[...] = jnp.zeros(total.shape, F32)
    spare = slots * heads
    both[spare:, :] = jnp.zeros((both.shape[0] - spare, width), BF16)
    begins[spare:, :] = jnp.full((begins.shape[0] - spare, lanes), pool, I32)
    ends[spare:, :] = jnp.zeros((ends.shape[0] - spare, lanes), I32)

    def slot(s, carry):
        start, made, last_block, last_slot = carry
        end = start + table[2 + s]
        request = table[2 + slots + own * slots + s]
        owner = sum((request >= k * slots).astype(I32) for k in range(1, count))
        query = queries[(owner ^ own) * slots + request - owner * slots]
        zero = jnp.zeros_like(query)
        at = pl.ds(pl.multiple_of(s * heads, heads), heads)
        both[at, :lanes] = jnp.where(top_half, query, zero)
        both[at, lanes:] = jnp.where(top_half, zero, query)
        begins[at, :] = jnp.full((heads, lanes), start, I32)
        ends[at, :] = jnp.full((heads, lanes), end, I32)
        first = start // block_rows
        covered = (first == last_block) & (s < last_slot + slot_group)
        first = jnp.where(covered, first + 1, first)
        last = (end - 1) // block_rows

        for j in range(most_blocks):
            items[2 * (made + j)] = first + j
            items[2 * (made + j) + 1] = s
        made_now = made + jnp.maximum(last + 1 - first, 0)
        new = made_now > made
        return (
            end,
            made_now,
            jnp.where(new, last, last_block),
            jnp.where(new, s, last_slot),
        )

    none = jnp.int32(-1)
    start = (jnp.int32(0), jnp.int32(0), none, none)
    _, made, _, _ = lax.fori_loop(0, slots, slot, start, unroll=True)
    for u in range(unroll):
        items[2 * (made + u)] = 0
        items[2 * (made + u) + 1] = slots
    steps = (made + unroll - 1) // unroll
    across = lax.broadcasted_iota(I32, (group_rows, block_rows), 1)

    def place_of(i):
        block = pl.multiple_of(items[2 * i] * block_rows, block_rows)
        rows = pl.multiple_of(items[2 * i + 1] * heads, heads)
        return block, pl.ds(block, block_rows), pl.ds(rows, group_rows)

    def score_step(step, carry):
        for u in range(unroll):
            i = step * unroll + u
            block, cache, rows = place_of(i)
            raw = lax.dot_general(
                both[rows, :], keys[cache, :], contract_minor, preferred_element_type=F32
            )
            position = block + across
            begin, end = (jnp.concatenate([b[rows, :]] * (block_rows // lanes), axis=1) for b in (begins, ends))
            inside = (position >= begin) & (position < end)
            masked = jnp.where(inside, raw * scale, masked_score)
            scores[i] = masked
            tops[rows, :] = jnp.maximum(tops[rows, :], folded(jnp.maximum, masked))
        return carry

    def value_step(step, carry):
        for u in range(unroll):
            i = step * unroll + u
            _, cache, rows = place_of(i)
            top = tops[rows, :]
            shifted = jnp.exp(scores[i] - jnp.concatenate([top] * (block_rows // lanes), axis=1))
            sums[rows, :] += folded(jnp.add, shifted)
            total[rows, :] += jnp.dot(
                shifted.astype(BF16), values[cache, :], preferred_element_type=F32
            )
        return carry

    lax.fori_loop(0, steps, score_step, 0)
    top = jnp.max(tops[...], axis=1, keepdims=True)
    tops[...] = jnp.broadcast_to(top, tops.shape)
    lax.fori_loop(0, steps, value_step, 0)

    real = slots * heads
    row = lax.broadcasted_iota(I32, (real, lanes), 0)
    upper = row % heads < half
    picked = jnp.where(upper, total[:real, :lanes], total[:real, lanes:])
    attended[...] = picked / jnp.sum(sums[:real, :], axis=1, keepdims=True)
    per_block = half // count
    for k in range(count):
        outs[k][...] = jnp.zeros(outs[k].shape, BF16)
        for kv in range(2):
            for j in range(per_block):
                head = kv * half + (own ^ k) * per_block + j
                at = (kv * per_block + j) * lanes
                outs[k][:slots, at : at + lanes] = attended[
                    pl.ds(head, slots, stride=heads), :
                ].astype(BF16)
    for copy in copies:
        copy.wait()


def attention(table, query_blocks, keys, values, jobs, parts, unroll=14):
    count = len(query_blocks)
    slots, heads, _ = query_blocks[0].shape
    pool, width = keys.shape
    most = pool // block_rows + slots + max(unroll, most_blocks)
    rows = (slots + slot_group) * heads
    return pl.pallas_call(
        functools.partial(
            attention_kernel,
            slots=slots,
            count=count,
            scale=1.0 / math.sqrt(lanes),
            unroll=unroll,
            masks_of=masks_in(jobs),
        ),
        in_specs=[smem] + [vmem] * (count + 2) + [hbm] * len(jobs),
        out_specs=[vmem] * (count + len(jobs)),
        out_shape=[jax.ShapeDtypeStruct((up_to(slots, 8), heads // count * lanes), BF16)] * count
        + job_shapes(jobs, parts),
        scratch_shapes=[
            pltpu.VMEM((count * slots, heads, lanes), BF16),
            pltpu.VMEM((rows, width), BF16),
            pltpu.VMEM((rows, lanes), I32),
            pltpu.VMEM((rows, lanes), I32),
            pltpu.VMEM((rows, lanes), F32),
            pltpu.VMEM((rows, lanes), F32),
            pltpu.VMEM((most, slot_group * heads, block_rows), F32),
            pltpu.VMEM((rows, width), F32),
            pltpu.VMEM((slots * heads, lanes), F32),
            pltpu.SMEM((2 * most,), I32),
            pltpu.SemaphoreType.DMA((job_count(jobs),)),
        ],
        compiler_params=params(6),
        cost_estimate=pl.CostEstimate(
            flops=4 * pool * heads * lanes, bytes_accessed=pool * width * 4, transcendentals=0
        ),
        name="attention",
    )(
        table,
        *query_blocks,
        in_vmem(keys),
        in_vmem(values),
        *[in_hbm(array) for array, _ in jobs],
    )


def selection_kernel(served, source, target, choose, sems, *, slots, count, masks_of):
    copies = job_copies(lax.axis_index("ffn"), masks_of, [source], [target], sems)
    for copy in copies:
        copy.start()
    own = lax.axis_index("att")
    requests, padded = choose.shape[1:]
    row = lax.broadcasted_iota(I32, (requests, padded), 0)
    wanted = row
    for k in range(count):
        moved = row + ((own ^ k) - k) * slots
        wanted = jnp.where((row >= k * slots) & (row < (k + 1) * slots), moved, wanted)
    lane = lax.broadcasted_iota(I32, (1, padded), 1)
    for k in range(count):
        turn = (count - (own ^ k)) * slots
        first = pltpu.roll(served[...], lax.rem(turn + lanes - count * slots, lanes), 1)
        request = jnp.where(lane < slots, first[:1, :padded], -1)
        choose[k] = (wanted == request).astype(F32).astype(BF16)
    for copy in copies:
        copy.wait()


def selection(served, jobs, parts, slots, padded, count):
    shapes = job_shapes(jobs, parts)
    moved = sum(2 * math.prod(shape.shape) for shape in shapes)
    return pl.pallas_call(
        functools.partial(
            selection_kernel, slots=slots, count=count, masks_of=masks_in(jobs)
        ),
        in_specs=[vmem, hbm],
        out_specs=[vmem] * 2,
        out_shape=shapes + [jax.ShapeDtypeStruct((count, slots * count, padded), BF16)],
        scratch_shapes=[pltpu.SemaphoreType.DMA((job_count(jobs),))],
        compiler_params=params(1),
        cost_estimate=pl.CostEstimate(flops=0, bytes_accessed=2 * moved, transcendentals=0),
        name="selection",
    )(served, in_hbm(jobs[0][0]))


def ordered_kernel(choose, *refs):
    blocks, out = refs[:-1], refs[-1]
    total = None
    for k, block in enumerate(blocks):
        term = jnp.dot(choose[k], block[...], preferred_element_type=F32)
        total = term if total is None else total + term
    out[...] = total.astype(BF16)


def ordered(choose, blocks):
    return pl.pallas_call(
        ordered_kernel,
        in_specs=[vmem] * (1 + len(blocks)),
        out_specs=vmem,
        out_shape=jax.ShapeDtypeStruct((choose.shape[1], blocks[0].shape[1]), BF16),
        compiler_params=params(2),
        name="ordered",
    )(choose, *blocks)


def projection_kernel(*refs, slots, parts):
    pieces, weight, outs = refs[:parts], refs[parts], refs[parts + 1 :]
    total = None
    for p in range(parts):
        term = jnp.dot(pieces[p][...], weight[p], preferred_element_type=F32)
        total = term if total is None else total + term
    for k, out in enumerate(outs):
        out[...] = halves_stacked(total[k * slots : (k + 1) * slots]).astype(BF16)


def projection(pieces, weight, slots, count):
    parts, depth, width = weight.shape
    return pl.pallas_call(
        functools.partial(projection_kernel, slots=slots, parts=parts),
        in_specs=[vmem] * (1 + parts),
        out_specs=[vmem] * count,
        out_shape=[jax.ShapeDtypeStruct((2 * slots, width // 2), BF16)] * count,
        compiler_params=params(2),
        cost_estimate=pl.CostEstimate(
            flops=2 * slots * count * parts * depth * width,
            bytes_accessed=parts * depth * width,
            transcendentals=0,
        ),
        name="projection",
    )(*pieces, in_vmem(weight))


def residual_kernel(*refs, joined):
    base, blocks, out = refs[0], refs[1:-1], refs[-1]
    total = base[...].astype(F32)
    if not joined:
        total = halves_stacked(total)
    for block in blocks:
        total = total + block[...].astype(F32)
    out[...] = (halves_joined(total) if joined else total).astype(BF16)


def residual(base, blocks, joined):
    rows, half = blocks[0].shape
    shape = (rows // 2, 2 * half) if joined else (rows, half)
    return pl.pallas_call(
        functools.partial(residual_kernel, joined=joined),
        in_specs=[vmem] * (1 + len(blocks)),
        out_specs=vmem,
        out_shape=jax.ShapeDtypeStruct(shape, BF16),
        compiler_params=params(2),
        name="residual",
    )(base, *blocks)


def unit_product(scaled, weight, part):
    return lax.dot_general(scaled, weight[part], contract_minor, preferred_element_type=F32)


def product_cost(requests, units, width):
    return pl.CostEstimate(
        flops=2 * requests * units * width, bytes_accessed=units * width, transcendentals=0
    )


def hidden_first_kernel(*refs, count, part):
    blocks, (gain, weight, send, scaled, squares, joined) = refs[:count], refs[count:]
    rows = blocks[0].shape[0] // 2
    for k in range(count):
        joined[k * rows : (k + 1) * rows, :] = halves_joined(blocks[k][...])
    middle = joined[...]
    square = jnp.sum(middle * middle, axis=1, keepdims=True)
    scaled[...] = (middle * gain[...].astype(F32)).astype(BF16)
    units = weight.shape[1]
    send[:, :units] = unit_product(scaled[...], weight, part).astype(BF16)
    send[:, units:] = high_low(square).astype(BF16)
    squares[...] = jnp.broadcast_to(square, squares.shape)


def hidden_first(blocks, gain, weight, part):
    count = len(blocks)
    rows, half = blocks[0].shape
    requests, width = rows // 2 * count, 2 * half
    units = weight.shape[1]
    return pl.pallas_call(
        functools.partial(hidden_first_kernel, count=count, part=part),
        in_specs=[vmem] * (count + 2),
        out_specs=[vmem] * 3,
        out_shape=[
            jax.ShapeDtypeStruct((requests, units + lanes), BF16),
            jax.ShapeDtypeStruct((requests, width), BF16),
            jax.ShapeDtypeStruct((requests, lanes), F32),
        ],
        scratch_shapes=[pltpu.VMEM((requests, width), F32)],
        compiler_params=params(2),
        cost_estimate=product_cost(requests, units, width),
        name="hidden_first",
    )(*blocks, gain, in_vmem(weight))


def hidden_kernel(scaled, *refs, parts):
    weights, out = refs[:-1], refs[-1]
    for t, (weight, part) in enumerate(zip(weights, parts)):
        units = weight.shape[1]
        out[:, t * units : (t + 1) * units] = unit_product(scaled[...], weight, part).astype(
            out.dtype
        )


def hidden_next(scaled, chosen, kind):
    requests, width = scaled.shape
    units = chosen[0][0].shape[1]
    return pl.pallas_call(
        functools.partial(hidden_kernel, parts=tuple(part for _, part in chosen)),
        in_specs=[vmem] * (1 + len(chosen)),
        out_specs=vmem,
        out_shape=jax.ShapeDtypeStruct((requests, len(chosen) * units), kind),
        compiler_params=params(2),
        cost_estimate=product_cost(requests, len(chosen) * units, width),
        name="hidden_next",
    )(scaled, *[in_vmem(weight) for weight, _ in chosen])


def squares_sum_kernel(keep, own_squares, arrived, out, squares):
    width = keep.shape[1]
    out[:, :width] = (keep[...] + arrived[:, :width].astype(F32)).astype(BF16)
    tail = arrived[:, width:].astype(F32)
    chip = own_squares[...] + (tail[:, :1] + tail[:, lanes // 2 : lanes // 2 + 1])
    squares[...] = chip
    out[:, width:] = high_low(chip).astype(BF16)


def squares_sum(keep, own_squares, arrived):
    requests, width = arrived.shape
    return pl.pallas_call(
        squares_sum_kernel,
        in_specs=[vmem] * 3,
        out_specs=[vmem] * 2,
        out_shape=[
            jax.ShapeDtypeStruct((requests, width), BF16),
            jax.ShapeDtypeStruct((requests, lanes), F32),
        ],
        compiler_params=params(2),
        name="squares_sum",
    )(keep, own_squares, arrived)


def chip_sum_kernel(keep, arrived, out):
    out[...] = (keep[...] + arrived[...].astype(F32)).astype(BF16)


def chip_sum(keep, arrived):
    return pl.pallas_call(
        chip_sum_kernel,
        in_specs=[vmem] * 2,
        out_specs=vmem,
        out_shape=jax.ShapeDtypeStruct(arrived.shape, BF16),
        compiler_params=params(2),
        name="chip_sum",
    )(keep, arrived)


def active_kernel(near, beside, far_gate, far_up, squares, out, *, model_width):
    units = far_up.shape[1]
    tail = far_gate[:, units:].astype(F32)
    square = squares[:, :1] + (tail[:, :1] + tail[:, lanes // 2 : lanes // 2 + 1])
    scale = lax.rsqrt(square / model_width + epsilon)

    def total(at, far):
        both = near[:, at : at + units] + beside[:, at : at + units].astype(F32)
        return (both + far.astype(F32)) * scale

    gate = total(0, far_gate[:, :units])
    out[...] = (gate / (1.0 + jnp.exp(-gate)) * total(units, far_up[...])).astype(BF16)


def active_units(near, beside, far_gate, far_up, squares, model_width):
    requests, width = near.shape
    return pl.pallas_call(
        functools.partial(active_kernel, model_width=model_width),
        in_specs=[vmem] * 5,
        out_specs=vmem,
        out_shape=jax.ShapeDtypeStruct((requests, width // 2), BF16),
        compiler_params=params(2),
        name="active",
    )(near, beside, far_gate, far_up, squares)


def down_kernel(*refs, parts, count, first, last):
    terms = len(parts)
    pieces, weights, rest = refs[:terms], refs[terms : 2 * terms], refs[2 * terms :]
    total = None if first else rest[0][...]
    outs = rest if first else rest[1:]
    for piece, weight, part in zip(pieces, weights, parts):
        term = jnp.dot(piece[...], weight[part], preferred_element_type=F32)
        total = term if total is None else total + term
    if last:
        rows = total.shape[0] // count
        for k in range(count):
            outs[k][...] = halves_stacked(total[k * rows : (k + 1) * rows]).astype(BF16)
    else:
        outs[0][...] = total


def down_part(chosen, count, before, last):
    requests, units = chosen[0][0].shape
    width = chosen[0][1].shape[2]
    if last:
        outs = [jax.ShapeDtypeStruct((2 * requests // count, width // 2), BF16)] * count
    else:
        outs = [jax.ShapeDtypeStruct((requests, width), F32)]
    before = [] if before is None else [before]
    return pl.pallas_call(
        functools.partial(
            down_kernel,
            parts=tuple(part for _, _, part in chosen),
            count=count,
            first=not before,
            last=last,
        ),
        in_specs=[vmem] * (2 * len(chosen) + len(before)),
        out_specs=[vmem] * len(outs),
        out_shape=outs,
        compiler_params=params(2),
        cost_estimate=product_cost(requests, len(chosen) * units, width),
        name="down",
    )(*[piece for piece, _, _ in chosen], *[in_vmem(w) for _, w, _ in chosen], *before)


def swaps_of(blocks):
    count = len(blocks)
    arrived = {k: pair_swap(blocks[k], "att", k) for k in reversed(range(1, count))}
    return [blocks[0]] + [arrived[k] for k in range(1, count)]


def exchanging_device(*args):
    return exchanging_layer(*args)


def exchanging_layer(
    hidden_state,
    queries,
    key_cache,
    value_cache,
    lengths,
    assignment,
    out_weight,
    norm_gain,
    gate_weight,
    up_weight,
    down_weight,
):
    slots, columns = hidden_state.shape
    count = lax.axis_size("att")
    parts = lax.axis_size("ffn")
    model_width = columns * parts
    heads = queries.shape[1] // lanes
    own = jnp.stack([lax.axis_index("att"), lax.axis_index("ffn")]).astype(I32)
    table = jnp.concatenate([own, lengths, assignment])
    served = jnp.pad(assignment, (0, lanes - assignment.shape[0]))
    served = lax.broadcast_in_dim(served, (8, lanes), (1,))

    own_queries = queries.reshape(slots, heads, lanes)
    query_blocks = swaps_of([own_queries] * count)
    keys, values = fetch([(key_cache, None), (value_cache, None)], parts)
    jobs = [(out_weight.reshape(-1, columns), (0, 1, 2, 3)), (down_weight, (0,))]
    *blocks, project, down_near = attention(table, query_blocks, keys, values, jobs, parts)

    blocks = swaps_of(blocks)
    padded = blocks[0].shape[0]
    jobs = [(up_weight, (3,))]
    up_corner, choose = selection(served, jobs, parts, slots, padded, count)
    piece = ordered(choose, blocks)
    across = pair_swap(piece, "ffn", 2)
    beside = pair_swap(piece, "ffn", 1)
    corner = pair_swap(across, "ffn", 1)
    (down_across,) = fetch([(down_weight, (2,))], parts)
    gain = norm_gain.reshape(1, columns)
    partial = projection([piece, beside, across, corner], project, slots, count)
    jobs = [(gate_weight, (0, 1, 2, 3)), (down_weight, (1,))]
    gate, down_beside = fetch(jobs, parts)
    middle = residual(hidden_state, swaps_of(partial), False)

    rows = swaps_of([middle] * count)
    jobs = [(up_weight, (0, 1, 2)), (down_weight, (3,))]
    up, down_corner = fetch(jobs, parts)
    send, scaled, squares = hidden_first(rows, gain, gate, 3)
    arrived = pair_swap(send, "ffn", 1)
    keep = hidden_next(scaled, [(gate, 2)], F32)
    far_gate, squares = squares_sum(keep, squares, arrived)
    far_gate = pair_swap(far_gate, "ffn", 2)
    send = hidden_next(scaled, [(up_corner, 0)], BF16)
    arrived = pair_swap(send, "ffn", 1)
    keep = hidden_next(scaled, [(up, 2)], F32)
    far_up = pair_swap(chip_sum(keep, arrived), "ffn", 2)
    send = hidden_next(scaled, [(gate, 1), (up, 1)], BF16)
    arrived = pair_swap(send, "ffn", 1)
    keep = hidden_next(scaled, [(gate, 0), (up, 0)], F32)
    active = active_units(keep, arrived, far_gate, far_up, squares, model_width)

    across = pair_swap(active, "ffn", 2)
    beside = pair_swap(active, "ffn", 1)
    chosen = [(active, down_near, 0), (beside, down_beside, 0)]
    (before,) = down_part(chosen, count, None, False)
    corner = pair_swap(across, "ffn", 1)
    (before,) = down_part([(across, down_across, 0)], count, before, False)
    partial = down_part([(corner, down_corner, 0)], count, before, True)
    return residual(middle, swaps_of(partial), True)


def solution(mesh):
    count, parts = mesh.shape["att"], mesh.shape["ffn"]
    paired = count == 4 and parts == 4
    in_specs = (
        P(("group", "att"), "ffn"),
        P(("group", "att"), "ffn"),
        P(("group", "att"), "ffn"),
        P(("group", "att"), "ffn"),
        P(("group", "att")),
        P("group"),
        P(None, "att", "ffn"),
        P("ffn"),
        P("att", "ffn"),
        P("att", "ffn"),
        P("att", "ffn"),
    )
    out_specs = P(("group", "att"), "ffn")
    return jax.shard_map(
        exchanging_device if paired else general_device,
        mesh=mesh,
        in_specs=in_specs,
        out_specs=out_specs,
        check_vma=False,
    )
```
